512 devices in a mesh: seq: 32 (over x, y), exp: 16 (over z, core).
Axes of the slice: x: 4, y: 8, z: 8, core: 2. Of those that a mesh axis runs over, the one named last changes fastest.
Arguments:
- tokens: bfloat16 [16384, 1024], P(('seq', 'exp')), may hold values from -22 to 22
- array_type: int32 [16384], P(('seq', 'exp')), may hold values from 0 to 15, as said below
- block_pattern: int32 [32, 32], replicated, may hold values from 0 to 1, as said below
- gain_attn: float32 [1024], replicated, may hold values from 0.25 to 1.75
- w_query: bfloat16 [1024, 1024], P(None, 'exp'), may hold values from -0.1875 to 0.1875
- w_key: bfloat16 [1024, 1024], P(None, 'exp'), may hold values from -0.1875 to 0.1875
- w_value: bfloat16 [1024, 1024], P(None, 'exp'), may hold values from -0.1875 to 0.1875
- logit_scale: float32 [16], P('exp'), may hold values from 0.06 to 30
- w_out: bfloat16 [1024, 1024], P('exp'), may hold values from -0.1875 to 0.1875
- gain_ffn: float32 [1024], replicated, may hold values from 0.25 to 1.75
- w_gate: bfloat16 [16, 1024, 4096], P('exp', None, 'seq'), may hold values from -0.1875 to 0.1875
- w_up: bfloat16 [16, 1024, 4096], P('exp', None, 'seq'), may hold values from -0.1875 to 0.1875
- w_down: bfloat16 [16, 1024, 4096], P('exp', None, 'seq'), may hold values from -0.09375 to 0.09375
Outputs:
- encoded: bfloat16 [16384, 1024], P(('seq', 'exp'))
The draws below stay inside these ranges and needn't reach their ends.
Inputs may be any that keep to these rules, and one draw needn't show every extreme that they name: `array_type`: in each aligned block of 32 rows no type occurs more than 4 times and some type occurs exactly 4 times; in some aligned block of 512 rows one type occurs exactly 4 times in each of its blocks of 32 rows. block_pattern[q][q] is 1, and block_pattern[q][k] is 0 where blocks q and k lie more than 3 apart around the loop of 32 blocks.
All inputs are finite; a program needn't handle non-finite values.
Results may differ from the reference program's by a relative error of at most 0.011.
The reference program's roundings to bfloat16 on the way count: a program that leaves them out, or rounds other values in their place, can miss the bound.
Values may be sent and summed in bfloat16 or wider, within the bound.
A program may use at most 64 MiB of HBM per device.

```python
import jax
import jax.numpy as jnp
from jax import lax

D = 1024
H = 16
HS = 64
E = 16
FF = 4096
REACH = 3
TOK_DEV = 512
TOKENS = 16384
NBLK = 32
ROWS = 32
CAP = 4
SLICES = 32
DEVICES = 512


def draw_tokens(key, part):
    key_base, key_row, key_col = jax.random.split(key, 3)
    row_scale = jnp.exp(jax.random.uniform(key_row, (TOKENS, 1), jnp.float32, jnp.log(0.3), jnp.log(3.0)))
    col_scale = jnp.exp(jax.random.uniform(key_col, (1, D), jnp.float32, jnp.log(0.6), jnp.log(1.8)))
    base = jax.random.normal(key_base, (TOKENS, D), jnp.float32)
    base = jnp.clip(base, -4.0, 4.0)
    return (base * row_scale * col_scale).astype(jnp.bfloat16)


def draw_array_type(key, part):
    blocks = TOKENS // ROWS
    group = TOK_DEV // ROWS
    key_hot, key_seq, key_type, key_rows = jax.random.split(key, 4)
    hot_type = jax.random.randint(key_hot, (blocks,), 0, E).astype(jnp.int32)
    seq_star = jax.random.randint(key_seq, (), 0, blocks // group).astype(jnp.int32)
    type_star = jax.random.randint(key_type, (), 0, E).astype(jnp.int32)
    block_seq = (jnp.arange(blocks, dtype=jnp.int32) // group).astype(jnp.int32)
    hot_type = jnp.where(block_seq == seq_star, type_star, hot_type).astype(jnp.int32)
    pool = (jnp.arange((E - 1) * CAP, dtype=jnp.int32) // CAP).astype(jnp.int32)

    def one_block(block_key, hot):
        key_pick, key_order = jax.random.split(block_key)
        picks = jax.random.permutation(key_pick, pool)[:ROWS - CAP]
        others = picks + (picks >= hot).astype(jnp.int32)
        filled = jnp.concatenate([jnp.full((CAP,), hot, jnp.int32), others.astype(jnp.int32)])
        return jax.random.permutation(key_order, filled)
    block_keys = jax.random.split(key_rows, blocks)
    return jax.vmap(one_block)(block_keys, hot_type).reshape(TOKENS).astype(jnp.int32)


def draw_block_pattern(key, part):
    row_ids = jnp.arange(NBLK, dtype=jnp.int32)[:, None]
    col_ids = jnp.arange(NBLK, dtype=jnp.int32)[None, :]
    ahead = (col_ids - row_ids) % NBLK
    behind = (row_ids - col_ids) % NBLK
    distance = jnp.minimum(ahead, behind)
    coin = jax.random.randint(key, (NBLK, NBLK), 0, 5)
    inside = ((distance <= REACH) & (coin >= 2)).astype(jnp.int32)
    return jnp.where(distance == 0, 1, inside).astype(jnp.int32)


def draw_logit_scale(key, part):
    fraction = jax.random.uniform(key, (H,), jnp.float32, 0.0, 1.0)
    upper = 0.3
    return jnp.exp(jnp.log(0.06) + fraction * (jnp.log(upper) - jnp.log(0.06))).astype(jnp.float32)


def block_scale(own_key, extent, pieces, least, top_value):
    level = 1.0
    for axis_at, blocks in pieces:
        steps = jax.random.uniform(jax.random.fold_in(jax.random.fold_in(own_key, 6), axis_at), (blocks,), jnp.float32, least / len(pieces), top_value / len(pieces))
        level = level * jnp.repeat(jnp.exp(steps), extent[axis_at] // blocks).reshape((-1,) + (1,) * (len(extent) - 1 - axis_at))
    return level


def normal_values(rng, dims, width, limit, cuts=(), kind=jnp.bfloat16):
    values = width * jax.random.normal(rng, dims, jnp.float32)
    if cuts:
        values = values * block_scale(rng, dims, cuts, -0.22, 0.18)
    return jnp.clip(values, -limit, limit).astype(kind)


def setup_inputs(seed: int = 0) -> dict:
    arg_keys = jax.random.split(jax.random.key(seed), 14)
    tokens = draw_tokens(jax.random.fold_in(arg_keys[13], 71), 0)
    array_type = draw_array_type(jax.random.fold_in(arg_keys[13], 71), 0)
    block_pattern = draw_block_pattern(jax.random.fold_in(arg_keys[13], 71), 0)
    gain_attn = jnp.clip(1.0 + 0.15 * jax.random.normal(arg_keys[3], (D,), jnp.float32), 0.25, 1.75)
    w_query = normal_values(arg_keys[4], (D, H * HS), D ** -0.5, 0.1875, ((1, 16),))
    w_key = normal_values(arg_keys[5], (D, H * HS), D ** -0.5, 0.1875, ((1, 16),))
    w_value = normal_values(arg_keys[6], (D, H * HS), D ** -0.5, 0.1875, ((1, 16),))
    logit_scale = draw_logit_scale(jax.random.fold_in(arg_keys[13], 71), 0)
    w_out = normal_values(arg_keys[8], (H * HS, D), (H * HS) ** -0.5, 0.1875, ((0, 16),))
    gain_ffn = jnp.clip(1.0 + 0.15 * jax.random.normal(arg_keys[9], (D,), jnp.float32), 0.25, 1.75)
    w_gate = normal_values(arg_keys[10], (E, D, FF), D ** -0.5, 0.1875, ((0, 16), (2, 32)))
    w_up = normal_values(arg_keys[11], (E, D, FF), D ** -0.5, 0.1875, ((0, 16), (2, 32)))
    w_down = normal_values(arg_keys[12], (E, D, FF), FF ** -0.5, 0.09375, ((0, 16), (2, 32)))
    return {"tokens": tokens, "array_type": array_type, "block_pattern": block_pattern, "gain_attn": gain_attn, "w_query": w_query, "w_key": w_key, "w_value": w_value, "logit_scale": logit_scale, "w_out": w_out, "gain_ffn": gain_ffn, "w_gate": w_gate, "w_up": w_up, "w_down": w_down}


EPSILON = 1e-05

def rms_scale(matrix, gain):
    mean_square = lax.optimization_barrier(jnp.mean(matrix * matrix, axis=-1, keepdims=True))
    return matrix * lax.rsqrt(mean_square + EPSILON) * gain

def reference(tokens, array_type, block_pattern, gain_attn, w_query, w_key, w_value, logit_scale, w_out, gain_ffn, w_gate, w_up, w_down):
    inputs = tokens.astype(jnp.float32)
    normed_attn = rms_scale(inputs, gain_attn.astype(jnp.float32)).astype(jnp.bfloat16)
    query = jnp.dot(normed_attn, w_query, preferred_element_type=jnp.float32).astype(jnp.bfloat16)
    keys = jnp.dot(normed_attn, w_key, preferred_element_type=jnp.float32).astype(jnp.bfloat16)
    values_all = jnp.dot(normed_attn, w_value, preferred_element_type=jnp.float32).astype(jnp.bfloat16)
    blocks = TOKENS // TOK_DEV
    query_blocks = query.reshape(blocks, TOK_DEV, H, HS)
    key_blocks = keys.reshape(blocks, TOK_DEV, H, HS)
    value_blocks = values_all.reshape(blocks, TOK_DEV, H, HS)
    offsets = jnp.arange(-REACH, REACH + 1, dtype=jnp.int32)
    head_scale = logit_scale.astype(jnp.float32)[:, None, None]
    band_len = (2 * REACH + 1) * TOK_DEV

    def one_block(block_id):
        neighbor_ids = ((block_id + offsets) % blocks).astype(jnp.int32)
        query_rows = query_blocks[block_id].astype(jnp.float32)
        key_band = key_blocks[neighbor_ids].astype(jnp.float32).reshape(band_len, H, HS)
        value_band = value_blocks[neighbor_ids].astype(jnp.float32).reshape(band_len, H, HS)
        allowed = jnp.repeat(block_pattern[block_id, neighbor_ids] > 0, TOK_DEV, total_repeat_length=band_len)
        scores = jnp.einsum('qhd,khd->hqk', query_rows, key_band) * head_scale
        scores = jnp.where(allowed[None, None, :], scores, -jnp.inf)
        row_top = lax.optimization_barrier(jnp.max(scores, axis=2, keepdims=True))
        weights = jnp.exp(scores - row_top)
        weight_sum = lax.optimization_barrier(jnp.sum(weights, axis=2))
        weights_low = lax.optimization_barrier(weights.astype(jnp.bfloat16))
        weighted = jnp.einsum('hqk,khd->qhd', weights_low.astype(jnp.float32), value_band)
        return (weighted / jnp.transpose(weight_sum)[:, :, None]).astype(jnp.bfloat16)
    heads_out = lax.map(one_block, jnp.arange(blocks, dtype=jnp.int32)).reshape(TOKENS, H * HS)
    attn_out = jnp.dot(heads_out, w_out, preferred_element_type=jnp.float32)
    hidden_state = inputs + attn_out
    normed_ffn = rms_scale(hidden_state, gain_ffn.astype(jnp.float32)).astype(jnp.bfloat16)
    one_hot = (array_type[:, None] == jnp.arange(E, dtype=jnp.int32)[None, :]).astype(jnp.int32)
    slot_rank = (lax.optimization_barrier(jnp.sum(jnp.cumsum(one_hot, axis=0) * one_hot, axis=1)) - 1).astype(jnp.int32)
    most_rows = DEVICES * CAP
    table = jnp.zeros((E, most_rows), jnp.int32).at[array_type, slot_rank].set(jnp.arange(TOKENS, dtype=jnp.int32))
    group_width = FF // SLICES

    def one_expert(expert):
        chosen = normed_ffn[table[expert]]
        gate = jnp.dot(chosen, w_gate[expert], preferred_element_type=jnp.float32)
        upward = jnp.dot(chosen, w_up[expert], preferred_element_type=jnp.float32)
        act = (jax.nn.silu(gate) * upward).astype(jnp.bfloat16)
        down_rows = w_down[expert]

        def add_group(carry, group_id):
            start = (group_id * group_width).astype(jnp.int32)
            act_group = lax.dynamic_slice_in_dim(act, start, group_width, 1)
            down_group = lax.dynamic_slice_in_dim(down_rows, start, group_width, 1)
            partial_sum = jnp.dot(act_group, jnp.transpose(down_group), preferred_element_type=jnp.float32).astype(jnp.bfloat16)
            partial_sum = lax.optimization_barrier(partial_sum)
            return (carry + partial_sum.astype(jnp.float32), None)
        summed, _ = lax.scan(add_group, jnp.zeros((most_rows, D), jnp.float32), jnp.arange(SLICES, dtype=jnp.int32))
        return summed.astype(jnp.bfloat16)
    expert_table = lax.map(one_expert, jnp.arange(E, dtype=jnp.int32))
    expert_out = expert_table[array_type, slot_rank].astype(jnp.float32)
    return (hidden_state + expert_out).astype(jnp.bfloat16)
```

```python
import jax
import jax.numpy as jnp
from jax import lax
from jax.sharding import PartitionSpec as P

REACH = 3


EPSILON = 1e-05


def passed_along(block, axis, distance):
    devices = range(lax.axis_size(axis))
    route = [((i - distance) % len(devices), i) for i in devices]
    return lax.ppermute(block, axis, route)


def rms_scale(matrix, gain):
    mean_square = jnp.mean(matrix * matrix, axis=-1, keepdims=True)
    return matrix * lax.rsqrt(mean_square + EPSILON) * gain


def expert_terms(block, gate_slice, up_slice, down_slice):
    gate = jnp.einsum("nek,ekf->nef", block, gate_slice, preferred_element_type=jnp.float32)
    upward = jnp.einsum("nek,ekf->nef", block, up_slice, preferred_element_type=jnp.float32)
    act = (jax.nn.silu(gate) * upward).astype(jnp.bfloat16)
    return jnp.einsum("nef,ekf->nek", act, down_slice, preferred_element_type=jnp.float32)


def local(
    tokens,
    array_type,
    block_pattern,
    gain_attn,
    w_query,
    w_key,
    w_value,
    logit_scale,
    w_out,
    gain_ffn,
    w_gate,
    w_up,
    w_down,
):
    n_exp = lax.axis_size("exp")
    row_count = tokens.shape[0]
    width = tokens.shape[1]
    head_cols = w_query.shape[1]
    heads_dev = logit_scale.shape[0]
    head_size = head_cols // heads_dev
    n_blocks = block_pattern.shape[0]
    inputs = tokens.astype(jnp.float32)
    normed_attn = rms_scale(inputs, gain_attn).astype(jnp.bfloat16)
    projector = jnp.concatenate([w_query, w_key, w_value], axis=1)
    joined_qkv = jnp.dot(
        lax.all_gather(normed_attn, "exp", axis=0, tiled=True),
        projector,
        preferred_element_type=jnp.float32,
    ).astype(jnp.bfloat16)
    block_len = joined_qkv.shape[0]
    query_heads = joined_qkv[:, :head_cols].reshape(block_len, heads_dev, head_size)
    key_value = joined_qkv[:, head_cols:]
    position = lax.axis_index("seq")
    head_scale = logit_scale[:, None, None]

    def attend(state, kv_block, source):
        row_top, weight_sum, numerator = state
        key_rows = kv_block[:, :head_cols].reshape(block_len, heads_dev, head_size)
        value_rows = kv_block[:, head_cols:].reshape(block_len, heads_dev, head_size)
        allowed = block_pattern[position, source] > 0
        scores = (
            jnp.einsum("qhd,khd->hqk", query_heads, key_rows, preferred_element_type=jnp.float32)
            * head_scale
        )
        block_top = jnp.max(scores, axis=2)
        new_top = jnp.where(allowed, jnp.maximum(row_top, block_top), row_top)
        shifted = jnp.minimum(scores - new_top[:, :, None], 0.0)
        weights = jnp.where(allowed, jnp.exp(shifted), 0.0)
        rescale = jnp.exp(row_top - new_top)
        weight_sum = weight_sum * rescale + jnp.sum(weights, axis=2)
        contrib = jnp.einsum(
            "hqk,khd->qhd",
            weights.astype(jnp.bfloat16),
            value_rows,
            preferred_element_type=jnp.float32,
        )
        numerator = numerator * jnp.transpose(rescale)[:, :, None] + contrib
        return (new_top, weight_sum, numerator)

    start_state = (
        jnp.full((heads_dev, block_len), -jnp.inf, jnp.float32),
        jnp.zeros((heads_dev, block_len), jnp.float32),
        jnp.zeros((block_len, heads_dev, head_size), jnp.float32),
    )
    state = attend(start_state, key_value, position)
    lower = key_value
    upper = key_value
    for distance in range(1, REACH + 1):
        lower = passed_along(lower, "seq", 1)
        upper = passed_along(upper, "seq", -1)
        state = attend(state, lower, (position - distance) % n_blocks)
        state = attend(state, upper, (position + distance) % n_blocks)
    heads_out = (
        (state[2] / jnp.transpose(state[1])[:, :, None])
        .astype(jnp.bfloat16)
        .reshape(block_len, head_cols)
    )
    all_heads = lax.all_to_all(heads_out, "exp", split_axis=0, concat_axis=1, tiled=True)
    attn_out = jnp.dot(
        all_heads,
        lax.all_gather(w_out, "exp", axis=0, tiled=True),
        preferred_element_type=jnp.float32,
    )
    hidden_state = inputs + attn_out
    normed_ffn = rms_scale(hidden_state, gain_ffn).astype(jnp.bfloat16)
    experts_dev = w_gate.shape[0]
    n_total = experts_dev * n_exp
    capacity = 2 * row_count // n_total
    one_hot = (array_type[:, None] == jnp.arange(n_total, dtype=jnp.int32)[None, :]).astype(
        jnp.int32
    )
    slot_rank = jnp.sum(jnp.cumsum(one_hot, axis=0) * one_hot, axis=1) - 1
    owner = array_type // experts_dev
    local_expert = array_type % experts_dev
    slot_id = (owner * capacity + slot_rank) * experts_dev + local_expert
    n_slots = n_exp * capacity * experts_dev
    selector = (slot_id[None, :] == jnp.arange(n_slots, dtype=jnp.int32)[:, None]).astype(
        jnp.bfloat16
    )
    outgoing = jnp.dot(selector, normed_ffn, preferred_element_type=jnp.float32).astype(
        jnp.bfloat16
    )
    outgoing = outgoing.reshape(n_exp * capacity, experts_dev, width)
    arrived = lax.all_to_all(outgoing, "exp", split_axis=0, concat_axis=0, tiled=True)
    gathered = lax.all_gather(arrived, "seq", axis=0, tiled=True)
    n_seq = lax.axis_size("seq")
    partial = expert_terms(gathered, w_gate, w_up, w_down).astype(jnp.bfloat16)
    scattered = lax.all_to_all(partial, "seq", split_axis=0, concat_axis=0, tiled=True)
    summed = (
        jnp.sum(
            scattered.reshape((n_seq, -1) + scattered.shape[1:]).astype(jnp.float32),
            axis=0,
        )
        .astype(jnp.bfloat16)
    )
    returned = lax.all_to_all(summed, "exp", split_axis=0, concat_axis=0, tiled=True)
    expert_out = jnp.dot(
        jnp.transpose(selector),
        returned.reshape(n_slots, width),
        preferred_element_type=jnp.float32,
    )
    return (hidden_state + expert_out).astype(jnp.bfloat16)


def solution(mesh):
    return jax.shard_map(
        local,
        mesh=mesh,
        in_specs=(
            P(("seq", "exp"), None),
            P(("seq", "exp")),
            P(),
            P(),
            P(None, "exp"),
            P(None, "exp"),
            P(None, "exp"),
            P("exp"),
            P("exp", None),
            P(),
            P("exp", None, "seq"),
            P("exp", None, "seq"),
            P("exp", None, "seq"),
        ),
        out_specs=P(("seq", "exp"), None),
        check_vma=False,
    )
```

```python
import jax
import jax.numpy as jnp
from jax import lax
from jax.sharding import PartitionSpec as P
from jax.experimental import pallas as pl
from jax.experimental.pallas import tpu as pltpu
import functools

REACH = 3
Y_RING = 8


EPSILON = 1e-05


def passed_along(block, axis, distance):
    devices = range(lax.axis_size(axis))
    route = [((i - distance) % len(devices), i) for i in devices]
    return lax.ppermute(block, axis, route)


def ring_reduce_kernel(nx, ny, part_ref, out_ref, recv1, send1, acc, recv2, send2,
                       s1_send, s1_recv, s2_send, s2_recv):
    me = lax.axis_index("seq")
    col = lax.axis_index("exp")
    x = me // ny
    y = me % ny
    y_up = x * ny + (y + 1) % ny
    y_down = x * ny + (y + ny - 1) % ny
    x_up = ((x + 1) % nx) * ny + y
    x_down = ((x + nx - 1) % nx) * ny + y
    half_x = nx // 2
    rows = part_ref.shape[2]
    half_r = rows // 2

    barrier = pltpu.get_barrier_semaphore()
    for peer in (y_up, y_down, x_up, x_down):
        pl.semaphore_signal(barrier, inc=1, device_id=(peer, col),
                            device_id_type=pl.DeviceIdType.MESH)
    pl.semaphore_wait(barrier, 4)

    lanes = ((y_up, 0, half_x, 1), (y_down, half_x, nx, -1))
    copies1 = []
    for k in range(ny - 1):
        step_copies = []
        for d, (peer, lo, hi, sign) in enumerate(lanes):
            c = (y - sign * (k + 1) + 2 * ny) % ny
            if k == 0:
                src = part_ref.at[lo:hi, c]
            else:
                copies1[k - 1][d].wait_recv()
                send1[d, k] = (recv1[d, k - 1].astype(jnp.float32)
                               + part_ref[lo:hi, c].astype(jnp.float32)).astype(send1.dtype)
                src = send1.at[d, k]
            cp = pltpu.make_async_remote_copy(
                src_ref=src, dst_ref=recv1.at[d, k],
                send_sem=s1_send.at[d, k], recv_sem=s1_recv.at[d, k],
                device_id=(peer, col), device_id_type=pl.DeviceIdType.MESH)
            cp.start()
            step_copies.append(cp)
        copies1.append(step_copies)
    for d, (peer, lo, hi, sign) in enumerate(lanes):
        copies1[ny - 2][d].wait_recv()
        acc[lo:hi] = recv1[d, ny - 2].astype(jnp.float32) + part_ref[lo:hi, y].astype(jnp.float32)

    lanes2 = ((x_up, 0, half_r, 1), (x_down, half_r, rows, -1))
    copies2 = []
    for k in range(nx - 1):
        step_copies = []
        for d, (peer, lo, hi, sign) in enumerate(lanes2):
            c = (x - sign * (k + 1) + 2 * nx) % nx
            if k == 0:
                src = acc.at[c, lo:hi]
            else:
                copies2[k - 1][d].wait_recv()
                send2[d, k] = recv2[d, k - 1] + acc[c, lo:hi]
                src = send2.at[d, k]
            cp = pltpu.make_async_remote_copy(
                src_ref=src, dst_ref=recv2.at[d, k],
                send_sem=s2_send.at[d, k], recv_sem=s2_recv.at[d, k],
                device_id=(peer, col), device_id_type=pl.DeviceIdType.MESH)
            cp.start()
            step_copies.append(cp)
        copies2.append(step_copies)
    for d, (peer, lo, hi, sign) in enumerate(lanes2):
        copies2[nx - 2][d].wait_recv()
        out_ref[lo:hi] = (recv2[d, nx - 2] + acc[x, lo:hi]).astype(out_ref.dtype)
    for step_copies in copies1 + copies2:
        for cp in step_copies:
            cp.wait_send()


def ring_reduce(part, nx, ny):
    width = part.shape[-1]
    rows = part.shape[0] // (nx * ny)
    part = part.reshape(nx, ny, rows, width)
    half_x = nx // 2
    half_r = rows // 2
    vmem = pltpu.MemorySpace.VMEM
    return pl.pallas_call(
        functools.partial(ring_reduce_kernel, nx, ny),
        out_shape=jax.ShapeDtypeStruct((rows, width), jnp.bfloat16),
        in_specs=[pl.BlockSpec(memory_space=vmem)],
        out_specs=pl.BlockSpec(memory_space=vmem),
        scratch_shapes=[
            pltpu.VMEM((2, ny - 1, half_x, rows, width), jnp.bfloat16),
            pltpu.VMEM((2, ny - 1, half_x, rows, width), jnp.bfloat16),
            pltpu.VMEM((nx, rows, width), jnp.float32),
            pltpu.VMEM((2, nx - 1, half_r, width), jnp.float32),
            pltpu.VMEM((2, nx - 1, half_r, width), jnp.float32),
            pltpu.SemaphoreType.DMA((2, ny - 1)),
            pltpu.SemaphoreType.DMA((2, ny - 1)),
            pltpu.SemaphoreType.DMA((2, nx - 1)),
            pltpu.SemaphoreType.DMA((2, nx - 1)),
        ],
        compiler_params=pltpu.CompilerParams(
            collective_id=1, has_side_effects=True, vmem_limit_bytes=48 * 1024 * 1024
        ),
    )(part)


def rms_scale(matrix, gain):
    mean_square = jnp.mean(matrix * matrix, axis=-1, keepdims=True)
    return matrix * lax.rsqrt(mean_square + EPSILON) * gain


def expert_terms(block, gate_slice, up_slice, down_slice):
    gate = jnp.einsum("nek,ekf->nef", block, gate_slice, preferred_element_type=jnp.float32)
    upward = jnp.einsum("nek,ekf->nef", block, up_slice, preferred_element_type=jnp.float32)
    act = (jax.nn.silu(gate) * upward).astype(jnp.bfloat16)
    return jnp.einsum("nef,ekf->nek", act, down_slice, preferred_element_type=jnp.float32)


def local(
    tokens,
    array_type,
    block_pattern,
    gain_attn,
    w_query,
    w_key,
    w_value,
    logit_scale,
    w_out,
    gain_ffn,
    w_gate,
    w_up,
    w_down,
):
    n_exp = lax.axis_size("exp")
    row_count = tokens.shape[0]
    width = tokens.shape[1]
    head_cols = w_query.shape[1]
    heads_dev = logit_scale.shape[0]
    head_size = head_cols // heads_dev
    n_blocks = block_pattern.shape[0]
    inputs = tokens.astype(jnp.float32)
    normed_attn = rms_scale(inputs, gain_attn).astype(jnp.bfloat16)
    projector = jnp.concatenate([w_query, w_key, w_value], axis=1)
    joined_qkv = jnp.dot(
        lax.all_gather(normed_attn, "exp", axis=0, tiled=True),
        projector,
        preferred_element_type=jnp.float32,
    ).astype(jnp.bfloat16)
    block_len = joined_qkv.shape[0]
    query_heads = joined_qkv[:, :head_cols].reshape(block_len, heads_dev, head_size)
    key_value = joined_qkv[:, head_cols:]
    position = lax.axis_index("seq")
    head_scale = logit_scale[:, None, None]

    def attend(state, kv_block, source):
        row_top, weight_sum, numerator = state
        key_rows = kv_block[:, :head_cols].reshape(block_len, heads_dev, head_size)
        value_rows = kv_block[:, head_cols:].reshape(block_len, heads_dev, head_size)
        allowed = block_pattern[position, source] > 0
        scores = (
            jnp.einsum("qhd,khd->hqk", query_heads, key_rows, preferred_element_type=jnp.float32)
            * head_scale
        )
        block_top = jnp.max(scores, axis=2)
        new_top = jnp.where(allowed, jnp.maximum(row_top, block_top), row_top)
        shifted = jnp.minimum(scores - new_top[:, :, None], 0.0)
        weights = jnp.where(allowed, jnp.exp(shifted), 0.0)
        rescale = jnp.exp(row_top - new_top)
        weight_sum = weight_sum * rescale + jnp.sum(weights, axis=2)
        contrib = jnp.einsum(
            "hqk,khd->qhd",
            weights.astype(jnp.bfloat16),
            value_rows,
            preferred_element_type=jnp.float32,
        )
        numerator = numerator * jnp.transpose(rescale)[:, :, None] + contrib
        return (new_top, weight_sum, numerator)

    start_state = (
        jnp.full((heads_dev, block_len), -jnp.inf, jnp.float32),
        jnp.zeros((heads_dev, block_len), jnp.float32),
        jnp.zeros((block_len, heads_dev, head_size), jnp.float32),
    )
    state = attend(start_state, key_value, position)
    lower = key_value
    upper = key_value
    for distance in range(1, REACH + 1):
        lower = passed_along(lower, "seq", 1)
        upper = passed_along(upper, "seq", -1)
        state = attend(state, lower, (position - distance) % n_blocks)
        state = attend(state, upper, (position + distance) % n_blocks)
    heads_out = (
        (state[2] / jnp.transpose(state[1])[:, :, None])
        .astype(jnp.bfloat16)
        .reshape(block_len, head_cols)
    )
    all_heads = lax.all_to_all(heads_out, "exp", split_axis=0, concat_axis=1, tiled=True)
    attn_out = jnp.dot(
        all_heads,
        lax.all_gather(w_out, "exp", axis=0, tiled=True),
        preferred_element_type=jnp.float32,
    )
    hidden_state = inputs + attn_out
    normed_ffn = rms_scale(hidden_state, gain_ffn).astype(jnp.bfloat16)
    experts_dev = w_gate.shape[0]
    n_total = experts_dev * n_exp
    capacity = 2 * row_count // n_total
    one_hot = (array_type[:, None] == jnp.arange(n_total, dtype=jnp.int32)[None, :]).astype(
        jnp.int32
    )
    slot_rank = jnp.sum(jnp.cumsum(one_hot, axis=0) * one_hot, axis=1) - 1
    owner = array_type // experts_dev
    local_expert = array_type % experts_dev
    slot_id = (owner * capacity + slot_rank) * experts_dev + local_expert
    n_slots = n_exp * capacity * experts_dev
    selector = (slot_id[None, :] == jnp.arange(n_slots, dtype=jnp.int32)[:, None]).astype(
        jnp.bfloat16
    )
    outgoing = jnp.dot(selector, normed_ffn, preferred_element_type=jnp.float32).astype(
        jnp.bfloat16
    )
    outgoing = outgoing.reshape(n_exp * capacity, experts_dev, width)
    arrived = lax.all_to_all(outgoing, "exp", split_axis=0, concat_axis=0, tiled=True)
    gathered = lax.all_gather(arrived, "seq", axis=0, tiled=True)
    n_seq = lax.axis_size("seq")
    y_size = Y_RING if n_seq % Y_RING == 0 else n_seq
    partial = expert_terms(gathered, w_gate, w_up, w_down).astype(jnp.bfloat16)
    summed = ring_reduce(
        partial.reshape(partial.shape[0], width), n_seq // y_size, y_size
    ).reshape((-1,) + partial.shape[1:])
    returned = lax.all_to_all(summed, "exp", split_axis=0, concat_axis=0, tiled=True)
    expert_out = jnp.dot(
        jnp.transpose(selector),
        returned.reshape(n_slots, width),
        preferred_element_type=jnp.float32,
    )
    return (hidden_state + expert_out).astype(jnp.bfloat16)


def solution(mesh):
    return jax.shard_map(
        local,
        mesh=mesh,
        in_specs=(
            P(("seq", "exp"), None),
            P(("seq", "exp")),
            P(),
            P(),
            P(None, "exp"),
            P(None, "exp"),
            P(None, "exp"),
            P("exp"),
            P("exp", None),
            P(),
            P("exp", None, "seq"),
            P("exp", None, "seq"),
            P("exp", None, "seq"),
        ),
        out_specs=P(("seq", "exp"), None),
        check_vma=False,
    )
```

```python
import jax
import jax.numpy as jnp
from jax import lax
from jax.sharding import PartitionSpec as P
from jax.experimental import pallas as pl
from jax.experimental.pallas import tpu as pltpu
import functools

REACH = 3
Y_RING = 8


EPSILON = 1e-05


def passed_along(block, axis, distance):
    devices = range(lax.axis_size(axis))
    route = [((i - distance) % len(devices), i) for i in devices]
    return lax.ppermute(block, axis, route)


def ring_reduce_kernel(nx, ny, part_ref, out_ref, recv1, send1, acc, recv2, send2,
                       s1_send, s1_recv, s2_send, s2_recv):
    me = lax.axis_index("seq")
    col = lax.axis_index("exp")
    x = me // ny
    y = me % ny
    y_up = x * ny + (y + 1) % ny
    y_down = x * ny + (y + ny - 1) % ny
    x_up = ((x + 1) % nx) * ny + y
    x_down = ((x + nx - 1) % nx) * ny + y
    half_x = nx // 2
    rows = part_ref.shape[2]
    half_r = rows // 2

    barrier = pltpu.get_barrier_semaphore()
    for peer in (y_up, y_down, x_up, x_down):
        pl.semaphore_signal(barrier, inc=1, device_id=(peer, col),
                            device_id_type=pl.DeviceIdType.MESH)
    pl.semaphore_wait(barrier, 4)

    lanes = ((y_up, 0, half_x, 1), (y_down, half_x, nx, -1))
    copies1 = []
    for k in range(ny - 1):
        step_copies = []
        for d, (peer, lo, hi, sign) in enumerate(lanes):
            c = (y - sign * (k + 1) + 2 * ny) % ny
            if k == 0:
                src = part_ref.at[lo:hi, c]
            else:
                copies1[k - 1][d].wait_recv()
                send1[d, k] = (recv1[d, k - 1].astype(jnp.float32)
                               + part_ref[lo:hi, c].astype(jnp.float32)).astype(send1.dtype)
                src = send1.at[d, k]
            cp = pltpu.make_async_remote_copy(
                src_ref=src, dst_ref=recv1.at[d, k],
                send_sem=s1_send.at[d, k], recv_sem=s1_recv.at[d, k],
                device_id=(peer, col), device_id_type=pl.DeviceIdType.MESH)
            cp.start()
            step_copies.append(cp)
        copies1.append(step_copies)
    for d, (peer, lo, hi, sign) in enumerate(lanes):
        copies1[ny - 2][d].wait_recv()
        acc[lo:hi] = recv1[d, ny - 2].astype(jnp.float32) + part_ref[lo:hi, y].astype(jnp.float32)

    lanes2 = ((x_up, 0, half_r, 1), (x_down, half_r, rows, -1))
    copies2 = []
    for k in range(nx - 1):
        step_copies = []
        for d, (peer, lo, hi, sign) in enumerate(lanes2):
            c = (x - sign * (k + 1) + 2 * nx) % nx
            if k == 0:
                src = acc.at[c, lo:hi]
            else:
                copies2[k - 1][d].wait_recv()
                send2[d, k] = recv2[d, k - 1] + acc[c, lo:hi]
                src = send2.at[d, k]
            cp = pltpu.make_async_remote_copy(
                src_ref=src, dst_ref=recv2.at[d, k],
                send_sem=s2_send.at[d, k], recv_sem=s2_recv.at[d, k],
                device_id=(peer, col), device_id_type=pl.DeviceIdType.MESH)
            cp.start()
            step_copies.append(cp)
        copies2.append(step_copies)
    for d, (peer, lo, hi, sign) in enumerate(lanes2):
        copies2[nx - 2][d].wait_recv()
        out_ref[lo:hi] = (recv2[d, nx - 2] + acc[x, lo:hi]).astype(out_ref.dtype)
    for step_copies in copies1 + copies2:
        for cp in step_copies:
            cp.wait_send()


def ring_reduce(part, nx, ny):
    width = part.shape[-1]
    rows = part.shape[0] // (nx * ny)
    part = part.reshape(nx, ny, rows, width)
    half_x = nx // 2
    half_r = rows // 2
    vmem = pltpu.MemorySpace.VMEM
    return pl.pallas_call(
        functools.partial(ring_reduce_kernel, nx, ny),
        out_shape=jax.ShapeDtypeStruct((rows, width), jnp.bfloat16),
        in_specs=[pl.BlockSpec(memory_space=vmem)],
        out_specs=pl.BlockSpec(memory_space=vmem),
        scratch_shapes=[
            pltpu.VMEM((2, ny - 1, half_x, rows, width), jnp.bfloat16),
            pltpu.VMEM((2, ny - 1, half_x, rows, width), jnp.bfloat16),
            pltpu.VMEM((nx, rows, width), jnp.float32),
            pltpu.VMEM((2, nx - 1, half_r, width), jnp.float32),
            pltpu.VMEM((2, nx - 1, half_r, width), jnp.float32),
            pltpu.SemaphoreType.DMA((2, ny - 1)),
            pltpu.SemaphoreType.DMA((2, ny - 1)),
            pltpu.SemaphoreType.DMA((2, nx - 1)),
            pltpu.SemaphoreType.DMA((2, nx - 1)),
        ],
        compiler_params=pltpu.CompilerParams(
            collective_id=1, has_side_effects=True, vmem_limit_bytes=48 * 1024 * 1024
        ),
    )(part)


def rms_scale(matrix, gain):
    mean_square = jnp.mean(matrix * matrix, axis=-1, keepdims=True)
    return matrix * lax.rsqrt(mean_square + EPSILON) * gain


def expert_terms(block, gate_slice, up_slice, down_slice):
    gate = jnp.einsum("nek,ekf->nef", block, gate_slice, preferred_element_type=jnp.float32)
    upward = jnp.einsum("nek,ekf->nef", block, up_slice, preferred_element_type=jnp.float32)
    act = (jax.nn.silu(gate) * upward).astype(jnp.bfloat16)
    return jnp.einsum("nef,ekf->nek", act, down_slice, preferred_element_type=jnp.float32)


def local(
    tokens,
    array_type,
    block_pattern,
    gain_attn,
    w_query,
    w_key,
    w_value,
    logit_scale,
    w_out,
    gain_ffn,
    w_gate,
    w_up,
    w_down,
):
    n_exp = lax.axis_size("exp")
    row_count = tokens.shape[0]
    width = tokens.shape[1]
    head_cols = w_query.shape[1]
    heads_dev = logit_scale.shape[0]
    head_size = head_cols // heads_dev
    n_blocks = block_pattern.shape[0]
    inputs = tokens.astype(jnp.float32)
    normed_attn = rms_scale(inputs, gain_attn).astype(jnp.bfloat16)
    projector = jnp.concatenate([w_query, w_key, w_value], axis=1)
    joined_qkv = jnp.dot(
        lax.all_gather(normed_attn, "exp", axis=0, tiled=True),
        projector,
        preferred_element_type=jnp.float32,
    ).astype(jnp.bfloat16)
    block_len = joined_qkv.shape[0]
    query_heads = joined_qkv[:, :head_cols].reshape(block_len, heads_dev, head_size)
    key_value = joined_qkv[:, head_cols:]
    position = lax.axis_index("seq")
    head_scale = logit_scale[:, None, None]

    def attend(state, kv_block, source):
        row_top, weight_sum, numerator = state
        key_rows = kv_block[:, :head_cols].reshape(block_len, heads_dev, head_size)
        value_rows = kv_block[:, head_cols:].reshape(block_len, heads_dev, head_size)
        allowed = block_pattern[position, source] > 0
        scores = (
            jnp.einsum("qhd,khd->hqk", query_heads, key_rows, preferred_element_type=jnp.float32)
            * head_scale
        )
        block_top = jnp.max(scores, axis=2)
        new_top = jnp.where(allowed, jnp.maximum(row_top, block_top), row_top)
        shifted = jnp.minimum(scores - new_top[:, :, None], 0.0)
        weights = jnp.where(allowed, jnp.exp(shifted), 0.0)
        rescale = jnp.exp(row_top - new_top)
        weight_sum = weight_sum * rescale + jnp.sum(weights, axis=2)
        contrib = jnp.einsum(
            "hqk,khd->qhd",
            weights.astype(jnp.bfloat16),
            value_rows,
            preferred_element_type=jnp.float32,
        )
        numerator = numerator * jnp.transpose(rescale)[:, :, None] + contrib
        return (new_top, weight_sum, numerator)

    start_state = (
        jnp.full((heads_dev, block_len), -jnp.inf, jnp.float32),
        jnp.zeros((heads_dev, block_len), jnp.float32),
        jnp.zeros((block_len, heads_dev, head_size), jnp.float32),
    )
    state = attend(start_state, key_value, position)
    lowers = [passed_along(key_value, "seq", d) for d in range(1, REACH + 1)]
    uppers = [passed_along(key_value, "seq", -d) for d in range(1, REACH + 1)]
    for distance in range(1, REACH + 1):
        state = attend(state, lowers[distance - 1], (position - distance) % n_blocks)
        state = attend(state, uppers[distance - 1], (position + distance) % n_blocks)
    heads_out = (
        (state[2] / jnp.transpose(state[1])[:, :, None])
        .astype(jnp.bfloat16)
        .reshape(block_len, head_cols)
    )
    all_heads = lax.all_to_all(heads_out, "exp", split_axis=0, concat_axis=1, tiled=True)
    attn_out = jnp.dot(
        all_heads,
        lax.all_gather(w_out, "exp", axis=0, tiled=True),
        preferred_element_type=jnp.float32,
    )
    hidden_state = inputs + attn_out
    normed_ffn = rms_scale(hidden_state, gain_ffn).astype(jnp.bfloat16)
    experts_dev = w_gate.shape[0]
    n_total = experts_dev * n_exp
    capacity = 2 * row_count // n_total
    one_hot = (array_type[:, None] == jnp.arange(n_total, dtype=jnp.int32)[None, :]).astype(
        jnp.int32
    )
    slot_rank = jnp.sum(jnp.cumsum(one_hot, axis=0) * one_hot, axis=1) - 1
    owner = array_type // experts_dev
    local_expert = array_type % experts_dev
    slot_id = (owner * capacity + slot_rank) * experts_dev + local_expert
    n_slots = n_exp * capacity * experts_dev
    selector = (slot_id[None, :] == jnp.arange(n_slots, dtype=jnp.int32)[:, None]).astype(
        jnp.bfloat16
    )
    outgoing = jnp.dot(selector, normed_ffn, preferred_element_type=jnp.float32).astype(
        jnp.bfloat16
    )
    outgoing = outgoing.reshape(n_exp * capacity, experts_dev, width)
    arrived = lax.all_to_all(outgoing, "exp", split_axis=0, concat_axis=0, tiled=True)
    gathered = lax.all_gather(arrived, "seq", axis=0, tiled=True)
    n_seq = lax.axis_size("seq")
    y_size = Y_RING if n_seq % Y_RING == 0 else n_seq
    partial = expert_terms(gathered, w_gate, w_up, w_down).astype(jnp.bfloat16)
    summed = ring_reduce(
        partial.reshape(partial.shape[0], width), n_seq // y_size, y_size
    ).reshape((-1,) + partial.shape[1:])
    returned = lax.all_to_all(summed, "exp", split_axis=0, concat_axis=0, tiled=True)
    expert_out = jnp.dot(
        jnp.transpose(selector),
        returned.reshape(n_slots, width),
        preferred_element_type=jnp.float32,
    )
    return (hidden_state + expert_out).astype(jnp.bfloat16)


def solution(mesh):
    return jax.shard_map(
        local,
        mesh=mesh,
        in_specs=(
            P(("seq", "exp"), None),
            P(("seq", "exp")),
            P(),
            P(),
            P(None, "exp"),
            P(None, "exp"),
            P(None, "exp"),
            P("exp"),
            P("exp", None),
            P(),
            P("exp", None, "seq"),
            P("exp", None, "seq"),
            P("exp", None, "seq"),
        ),
        out_specs=P(("seq", "exp"), None),
        check_vma=False,
    )
```

```python
import jax
import jax.numpy as jnp
from jax import lax
from jax.sharding import PartitionSpec as P
from jax.experimental import pallas as pl
from jax.experimental.pallas import tpu as pltpu
import functools

REACH = 3
Y_RING = 8


EPSILON = 1e-05


def passed_along(block, axis, distance):
    devices = range(lax.axis_size(axis))
    route = [((i - distance) % len(devices), i) for i in devices]
    return lax.ppermute(block, axis, route)


def ring_reduce_kernel(nx, ny, part_ref, out_ref, recv1, send1, acc, recv2, send2,
                       s1_send, s1_recv, s2_send, s2_recv):
    me = lax.axis_index("seq")
    col = lax.axis_index("exp")
    x = me // ny
    y = me % ny
    y_up = x * ny + (y + 1) % ny
    y_down = x * ny + (y + ny - 1) % ny
    x_up = ((x + 1) % nx) * ny + y
    x_down = ((x + nx - 1) % nx) * ny + y
    half_x = nx // 2
    rows = part_ref.shape[2]
    half_r = rows // 2

    barrier = pltpu.get_barrier_semaphore()
    for peer in (y_up, y_down, x_up, x_down):
        pl.semaphore_signal(barrier, inc=1, device_id=(peer, col),
                            device_id_type=pl.DeviceIdType.MESH)
    pl.semaphore_wait(barrier, 4)

    lanes = ((y_up, 0, half_x, 1), (y_down, half_x, nx, -1))
    copies1 = []
    for k in range(ny - 1):
        step_copies = []
        for d, (peer, lo, hi, sign) in enumerate(lanes):
            c = (y - sign * (k + 1) + 2 * ny) % ny
            if k == 0:
                src = part_ref.at[lo:hi, c]
            else:
                copies1[k - 1][d].wait_recv()
                send1[d, k] = (recv1[d, k - 1].astype(jnp.float32)
                               + part_ref[lo:hi, c].astype(jnp.float32)).astype(send1.dtype)
                src = send1.at[d, k]
            cp = pltpu.make_async_remote_copy(
                src_ref=src, dst_ref=recv1.at[d, k],
                send_sem=s1_send.at[d, k], recv_sem=s1_recv.at[d, k],
                device_id=(peer, col), device_id_type=pl.DeviceIdType.MESH)
            cp.start()
            step_copies.append(cp)
        copies1.append(step_copies)
    for d, (peer, lo, hi, sign) in enumerate(lanes):
        copies1[ny - 2][d].wait_recv()
        acc[lo:hi] = recv1[d, ny - 2].astype(jnp.float32) + part_ref[lo:hi, y].astype(jnp.float32)

    lanes2 = ((x_up, 0, half_r, 1), (x_down, half_r, rows, -1))
    copies2 = []
    for k in range(nx - 1):
        step_copies = []
        for d, (peer, lo, hi, sign) in enumerate(lanes2):
            c = (x - sign * (k + 1) + 2 * nx) % nx
            if k == 0:
                src = acc.at[c, lo:hi]
            else:
                copies2[k - 1][d].wait_recv()
                send2[d, k] = recv2[d, k - 1] + acc[c, lo:hi]
                src = send2.at[d, k]
            cp = pltpu.make_async_remote_copy(
                src_ref=src, dst_ref=recv2.at[d, k],
                send_sem=s2_send.at[d, k], recv_sem=s2_recv.at[d, k],
                device_id=(peer, col), device_id_type=pl.DeviceIdType.MESH)
            cp.start()
            step_copies.append(cp)
        copies2.append(step_copies)
    for d, (peer, lo, hi, sign) in enumerate(lanes2):
        copies2[nx - 2][d].wait_recv()
        out_ref[lo:hi] = (recv2[d, nx - 2] + acc[x, lo:hi]).astype(out_ref.dtype)
    for step_copies in copies1 + copies2:
        for cp in step_copies:
            cp.wait_send()


def ring_reduce(part, nx, ny):
    width = part.shape[-1]
    rows = part.shape[0] // (nx * ny)
    part = part.reshape(nx, ny, rows, width)
    half_x = nx // 2
    half_r = rows // 2
    vmem = pltpu.MemorySpace.VMEM
    return pl.pallas_call(
        functools.partial(ring_reduce_kernel, nx, ny),
        out_shape=jax.ShapeDtypeStruct((rows, width), jnp.bfloat16),
        in_specs=[pl.BlockSpec(memory_space=vmem)],
        out_specs=pl.BlockSpec(memory_space=vmem),
        scratch_shapes=[
            pltpu.VMEM((2, ny - 1, half_x, rows, width), jnp.bfloat16),
            pltpu.VMEM((2, ny - 1, half_x, rows, width), jnp.bfloat16),
            pltpu.VMEM((nx, rows, width), jnp.float32),
            pltpu.VMEM((2, nx - 1, half_r, width), jnp.float32),
            pltpu.VMEM((2, nx - 1, half_r, width), jnp.float32),
            pltpu.SemaphoreType.DMA((2, ny - 1)),
            pltpu.SemaphoreType.DMA((2, ny - 1)),
            pltpu.SemaphoreType.DMA((2, nx - 1)),
            pltpu.SemaphoreType.DMA((2, nx - 1)),
        ],
        compiler_params=pltpu.CompilerParams(
            collective_id=1, has_side_effects=True, vmem_limit_bytes=48 * 1024 * 1024
        ),
    )(part)


def shift_exchange_kernel(offsets, axis, other, block_ref, out_ref, send_sems, recv_sems):
    n = lax.axis_size(axis)
    me = lax.axis_index(axis)
    col = lax.axis_index(other)

    def dev(peer):
        return (peer, col) if axis == "seq" else (col, peer)

    targets = [(me + o + n * len(offsets)) % n for o in offsets]
    barrier = pltpu.get_barrier_semaphore()
    for peer in targets:
        pl.semaphore_signal(barrier, inc=1, device_id=dev(peer),
                            device_id_type=pl.DeviceIdType.MESH)
    pl.semaphore_wait(barrier, len(offsets))
    copies = []
    for j, peer in enumerate(targets):
        cp = pltpu.make_async_remote_copy(
            src_ref=block_ref, dst_ref=out_ref.at[j],
            send_sem=send_sems.at[j], recv_sem=recv_sems.at[j],
            device_id=dev(peer), device_id_type=pl.DeviceIdType.MESH)
        cp.start()
        copies.append(cp)
    for cp in copies:
        cp.wait()


def shift_exchange(block, offsets, axis, other, cid):
    vmem = pltpu.MemorySpace.VMEM
    k = len(offsets)
    return pl.pallas_call(
        functools.partial(shift_exchange_kernel, tuple(offsets), axis, other),
        out_shape=jax.ShapeDtypeStruct((k,) + block.shape, block.dtype),
        in_specs=[pl.BlockSpec(memory_space=vmem)],
        out_specs=pl.BlockSpec(memory_space=vmem),
        scratch_shapes=[pltpu.SemaphoreType.DMA((k,)), pltpu.SemaphoreType.DMA((k,))],
        compiler_params=pltpu.CompilerParams(collective_id=cid, has_side_effects=True),
    )(block)


def exp_all_to_all_kernel(x_ref, y_ref, send_sems, recv_sems):
    n = lax.axis_size("exp")
    me = lax.axis_index("exp")
    row = lax.axis_index("seq")
    barrier = pltpu.get_barrier_semaphore()
    for k in range(1, n):
        pl.semaphore_signal(barrier, inc=1, device_id=(row, (me + k) % n),
                            device_id_type=pl.DeviceIdType.MESH)
    pl.semaphore_wait(barrier, n - 1)
    copies = []
    for k in range(1, n):
        peer = (me + k) % n
        cp = pltpu.make_async_remote_copy(
            src_ref=x_ref.at[peer], dst_ref=y_ref.at[me],
            send_sem=send_sems.at[k - 1], recv_sem=recv_sems.at[k - 1],
            device_id=(row, peer), device_id_type=pl.DeviceIdType.MESH)
        cp.start()
        copies.append(cp)
    y_ref[me] = x_ref[me]
    for cp in copies:
        cp.wait()


def exp_all_to_all(x, cid):
    n = x.shape[0]
    vmem = pltpu.MemorySpace.VMEM
    return pl.pallas_call(
        exp_all_to_all_kernel,
        out_shape=jax.ShapeDtypeStruct(x.shape, x.dtype),
        in_specs=[pl.BlockSpec(memory_space=vmem)],
        out_specs=pl.BlockSpec(memory_space=vmem),
        scratch_shapes=[pltpu.SemaphoreType.DMA((n - 1,)), pltpu.SemaphoreType.DMA((n - 1,))],
        compiler_params=pltpu.CompilerParams(collective_id=cid, has_side_effects=True),
    )(x)


def rms_scale(matrix, gain):
    mean_square = jnp.mean(matrix * matrix, axis=-1, keepdims=True)
    return matrix * lax.rsqrt(mean_square + EPSILON) * gain


def expert_terms(block, gate_slice, up_slice, down_slice):
    gate = jnp.einsum("nek,ekf->nef", block, gate_slice, preferred_element_type=jnp.float32)
    upward = jnp.einsum("nek,ekf->nef", block, up_slice, preferred_element_type=jnp.float32)
    act = (jax.nn.silu(gate) * upward).astype(jnp.bfloat16)
    return jnp.einsum("nef,ekf->nek", act, down_slice, preferred_element_type=jnp.float32)


def local(
    tokens,
    array_type,
    block_pattern,
    gain_attn,
    w_query,
    w_key,
    w_value,
    logit_scale,
    w_out,
    gain_ffn,
    w_gate,
    w_up,
    w_down,
):
    n_exp = lax.axis_size("exp")
    row_count = tokens.shape[0]
    width = tokens.shape[1]
    head_cols = w_query.shape[1]
    heads_dev = logit_scale.shape[0]
    head_size = head_cols // heads_dev
    n_blocks = block_pattern.shape[0]
    inputs = tokens.astype(jnp.float32)
    normed_attn = rms_scale(inputs, gain_attn).astype(jnp.bfloat16)
    projector = jnp.concatenate([w_query, w_key, w_value], axis=1)
    joined_qkv = jnp.dot(
        lax.all_gather(normed_attn, "exp", axis=0, tiled=True),
        projector,
        preferred_element_type=jnp.float32,
    ).astype(jnp.bfloat16)
    block_len = joined_qkv.shape[0]
    query_heads = joined_qkv[:, :head_cols].reshape(block_len, heads_dev, head_size)
    key_value = joined_qkv[:, head_cols:]
    position = lax.axis_index("seq")
    head_scale = logit_scale[:, None, None]

    def attend(state, kv_block, source):
        row_top, weight_sum, numerator = state
        key_rows = kv_block[:, :head_cols].reshape(block_len, heads_dev, head_size)
        value_rows = kv_block[:, head_cols:].reshape(block_len, heads_dev, head_size)
        allowed = block_pattern[position, source] > 0
        scores = (
            jnp.einsum("qhd,khd->hqk", query_heads, key_rows, preferred_element_type=jnp.float32)
            * head_scale
        )
        block_top = jnp.max(scores, axis=2)
        new_top = jnp.where(allowed, jnp.maximum(row_top, block_top), row_top)
        shifted = jnp.minimum(scores - new_top[:, :, None], 0.0)
        weights = jnp.where(allowed, jnp.exp(shifted), 0.0)
        rescale = jnp.exp(row_top - new_top)
        weight_sum = weight_sum * rescale + jnp.sum(weights, axis=2)
        contrib = jnp.einsum(
            "hqk,khd->qhd",
            weights.astype(jnp.bfloat16),
            value_rows,
            preferred_element_type=jnp.float32,
        )
        numerator = numerator * jnp.transpose(rescale)[:, :, None] + contrib
        return (new_top, weight_sum, numerator)

    start_state = (
        jnp.full((heads_dev, block_len), -jnp.inf, jnp.float32),
        jnp.zeros((heads_dev, block_len), jnp.float32),
        jnp.zeros((block_len, heads_dev, head_size), jnp.float32),
    )
    state = attend(start_state, key_value, position)
    offsets = [d for d in range(1, REACH + 1)] + [-d for d in range(1, REACH + 1)]
    neighbours = shift_exchange(key_value, offsets, "seq", "exp", 2)
    for distance in range(1, REACH + 1):
        state = attend(state, neighbours[distance - 1], (position - distance) % n_blocks)
        state = attend(state, neighbours[REACH + distance - 1], (position + distance) % n_blocks)
    heads_out = (
        (state[2] / jnp.transpose(state[1])[:, :, None])
        .astype(jnp.bfloat16)
        .reshape(block_len, head_cols)
    )
    all_heads = lax.all_to_all(heads_out, "exp", split_axis=0, concat_axis=1, tiled=True)
    attn_out = jnp.dot(
        all_heads,
        lax.all_gather(w_out, "exp", axis=0, tiled=True),
        preferred_element_type=jnp.float32,
    )
    hidden_state = inputs + attn_out
    normed_ffn = rms_scale(hidden_state, gain_ffn).astype(jnp.bfloat16)
    experts_dev = w_gate.shape[0]
    n_total = experts_dev * n_exp
    capacity = 2 * row_count // n_total
    one_hot = (array_type[:, None] == jnp.arange(n_total, dtype=jnp.int32)[None, :]).astype(
        jnp.int32
    )
    slot_rank = jnp.sum(jnp.cumsum(one_hot, axis=0) * one_hot, axis=1) - 1
    owner = array_type // experts_dev
    local_expert = array_type % experts_dev
    slot_id = (owner * capacity + slot_rank) * experts_dev + local_expert
    n_slots = n_exp * capacity * experts_dev
    selector = (slot_id[None, :] == jnp.arange(n_slots, dtype=jnp.int32)[:, None]).astype(
        jnp.bfloat16
    )
    outgoing = jnp.dot(selector, normed_ffn, preferred_element_type=jnp.float32).astype(
        jnp.bfloat16
    )
    outgoing = outgoing.reshape(n_exp * capacity, experts_dev, width)
    arrived = lax.all_to_all(outgoing, "exp", split_axis=0, concat_axis=0, tiled=True)
    gathered = lax.all_gather(arrived, "seq", axis=0, tiled=True)
    n_seq = lax.axis_size("seq")
    y_size = Y_RING if n_seq % Y_RING == 0 else n_seq
    partial = expert_terms(gathered, w_gate, w_up, w_down).astype(jnp.bfloat16)
    summed = ring_reduce(
        partial.reshape(partial.shape[0], width), n_seq // y_size, y_size
    ).reshape((-1,) + partial.shape[1:])
    returned = lax.all_to_all(summed, "exp", split_axis=0, concat_axis=0, tiled=True)
    expert_out = jnp.dot(
        jnp.transpose(selector),
        returned.reshape(n_slots, width),
        preferred_element_type=jnp.float32,
    )
    return (hidden_state + expert_out).astype(jnp.bfloat16)


def solution(mesh):
    return jax.shard_map(
        local,
        mesh=mesh,
        in_specs=(
            P(("seq", "exp"), None),
            P(("seq", "exp")),
            P(),
            P(),
            P(None, "exp"),
            P(None, "exp"),
            P(None, "exp"),
            P("exp"),
            P("exp", None),
            P(),
            P("exp", None, "seq"),
            P("exp", None, "seq"),
            P("exp", None, "seq"),
        ),
        out_specs=P(("seq", "exp"), None),
        check_vma=False,
    )
```

```python
import jax
import jax.numpy as jnp
from jax import lax
from jax.sharding import PartitionSpec as P
from jax.experimental import pallas as pl
from jax.experimental.pallas import tpu as pltpu
import functools

REACH = 3
Y_RING = 8


EPSILON = 1e-05


def passed_along(block, axis, distance):
    devices = range(lax.axis_size(axis))
    route = [((i - distance) % len(devices), i) for i in devices]
    return lax.ppermute(block, axis, route)


def ring_reduce_kernel(nx, ny, part_ref, out_ref, recv1, send1, acc, recv2, send2,
                       s1_send, s1_recv, s2_send, s2_recv):
    me = lax.axis_index("seq")
    col = lax.axis_index("exp")
    x = me // ny
    y = me % ny
    y_up = x * ny + (y + 1) % ny
    y_down = x * ny + (y + ny - 1) % ny
    x_up = ((x + 1) % nx) * ny + y
    x_down = ((x + nx - 1) % nx) * ny + y
    half_x = nx // 2
    rows = part_ref.shape[2]
    half_r = rows // 2

    barrier = pltpu.get_barrier_semaphore()
    for peer in (y_up, y_down, x_up, x_down):
        pl.semaphore_signal(barrier, inc=1, device_id=(peer, col),
                            device_id_type=pl.DeviceIdType.MESH)
    pl.semaphore_wait(barrier, 4)

    lanes = ((y_up, 0, half_x, 1), (y_down, half_x, nx, -1))
    copies1 = []
    for k in range(ny - 1):
        step_copies = []
        for d, (peer, lo, hi, sign) in enumerate(lanes):
            c = (y - sign * (k + 1) + 2 * ny) % ny
            if k == 0:
                src = part_ref.at[lo:hi, c]
            else:
                copies1[k - 1][d].wait_recv()
                send1[d, k] = (recv1[d, k - 1].astype(jnp.float32)
                               + part_ref[lo:hi, c].astype(jnp.float32)).astype(send1.dtype)
                src = send1.at[d, k]
            cp = pltpu.make_async_remote_copy(
                src_ref=src, dst_ref=recv1.at[d, k],
                send_sem=s1_send.at[d, k], recv_sem=s1_recv.at[d, k],
                device_id=(peer, col), device_id_type=pl.DeviceIdType.MESH)
            cp.start()
            step_copies.append(cp)
        copies1.append(step_copies)
    for d, (peer, lo, hi, sign) in enumerate(lanes):
        copies1[ny - 2][d].wait_recv()
        acc[lo:hi] = recv1[d, ny - 2].astype(jnp.float32) + part_ref[lo:hi, y].astype(jnp.float32)

    lanes2 = ((x_up, 0, half_r, 1), (x_down, half_r, rows, -1))
    copies2 = []
    for k in range(nx - 1):
        step_copies = []
        for d, (peer, lo, hi, sign) in enumerate(lanes2):
            c = (x - sign * (k + 1) + 2 * nx) % nx
            if k == 0:
                src = acc.at[c, lo:hi]
            else:
                copies2[k - 1][d].wait_recv()
                send2[d, k] = recv2[d, k - 1] + acc[c, lo:hi]
                src = send2.at[d, k]
            cp = pltpu.make_async_remote_copy(
                src_ref=src, dst_ref=recv2.at[d, k],
                send_sem=s2_send.at[d, k], recv_sem=s2_recv.at[d, k],
                device_id=(peer, col), device_id_type=pl.DeviceIdType.MESH)
            cp.start()
            step_copies.append(cp)
        copies2.append(step_copies)
    for d, (peer, lo, hi, sign) in enumerate(lanes2):
        copies2[nx - 2][d].wait_recv()
        out_ref[lo:hi] = (recv2[d, nx - 2] + acc[x, lo:hi]).astype(out_ref.dtype)
    for step_copies in copies1 + copies2:
        for cp in step_copies:
            cp.wait_send()


def ring_reduce(part, nx, ny):
    width = part.shape[-1]
    rows = part.shape[0] // (nx * ny)
    part = part.reshape(nx, ny, rows, width)
    half_x = nx // 2
    half_r = rows // 2
    vmem = pltpu.MemorySpace.VMEM
    return pl.pallas_call(
        functools.partial(ring_reduce_kernel, nx, ny),
        out_shape=jax.ShapeDtypeStruct((rows, width), jnp.bfloat16),
        in_specs=[pl.BlockSpec(memory_space=vmem)],
        out_specs=pl.BlockSpec(memory_space=vmem),
        scratch_shapes=[
            pltpu.VMEM((2, ny - 1, half_x, rows, width), jnp.bfloat16),
            pltpu.VMEM((2, ny - 1, half_x, rows, width), jnp.bfloat16),
            pltpu.VMEM((nx, rows, width), jnp.float32),
            pltpu.VMEM((2, nx - 1, half_r, width), jnp.float32),
            pltpu.VMEM((2, nx - 1, half_r, width), jnp.float32),
            pltpu.SemaphoreType.DMA((2, ny - 1)),
            pltpu.SemaphoreType.DMA((2, ny - 1)),
            pltpu.SemaphoreType.DMA((2, nx - 1)),
            pltpu.SemaphoreType.DMA((2, nx - 1)),
        ],
        compiler_params=pltpu.CompilerParams(
            collective_id=1, has_side_effects=True, vmem_limit_bytes=48 * 1024 * 1024
        ),
    )(part)


def shift_exchange_kernel(offsets, axis, other, block_ref, out_ref, send_sems, recv_sems):
    n = lax.axis_size(axis)
    me = lax.axis_index(axis)
    col = lax.axis_index(other)

    def dev(peer):
        return (peer, col) if axis == "seq" else (col, peer)

    targets = [(me + o + n * len(offsets)) % n for o in offsets]
    barrier = pltpu.get_barrier_semaphore()
    for peer in targets:
        pl.semaphore_signal(barrier, inc=1, device_id=dev(peer),
                            device_id_type=pl.DeviceIdType.MESH)
    pl.semaphore_wait(barrier, len(offsets))
    copies = []
    for j, peer in enumerate(targets):
        cp = pltpu.make_async_remote_copy(
            src_ref=block_ref, dst_ref=out_ref.at[j],
            send_sem=send_sems.at[j], recv_sem=recv_sems.at[j],
            device_id=dev(peer), device_id_type=pl.DeviceIdType.MESH)
        cp.start()
        copies.append(cp)
    for cp in copies:
        cp.wait()


def shift_exchange(block, offsets, axis, other, cid):
    vmem = pltpu.MemorySpace.VMEM
    k = len(offsets)
    return pl.pallas_call(
        functools.partial(shift_exchange_kernel, tuple(offsets), axis, other),
        out_shape=jax.ShapeDtypeStruct((k,) + block.shape, block.dtype),
        in_specs=[pl.BlockSpec(memory_space=vmem)],
        out_specs=pl.BlockSpec(memory_space=vmem),
        scratch_shapes=[pltpu.SemaphoreType.DMA((k,)), pltpu.SemaphoreType.DMA((k,))],
        compiler_params=pltpu.CompilerParams(collective_id=cid, has_side_effects=True),
    )(block)


def exp_all_to_all_kernel(broadcast, x_ref, y_ref, send_sems, recv_sems):
    n = lax.axis_size("exp")
    me = lax.axis_index("exp")
    row = lax.axis_index("seq")
    barrier = pltpu.get_barrier_semaphore()
    for k in range(1, n):
        pl.semaphore_signal(barrier, inc=1, device_id=(row, (me + k) % n),
                            device_id_type=pl.DeviceIdType.MESH)
    pl.semaphore_wait(barrier, n - 1)
    copies = []
    for k in range(1, n):
        peer = (me + k) % n
        cp = pltpu.make_async_remote_copy(
            src_ref=x_ref if broadcast else x_ref.at[peer], dst_ref=y_ref.at[me],
            send_sem=send_sems.at[k - 1], recv_sem=recv_sems.at[k - 1],
            device_id=(row, peer), device_id_type=pl.DeviceIdType.MESH)
        cp.start()
        copies.append(cp)
    y_ref[me] = x_ref[...] if broadcast else x_ref[me]
    for cp in copies:
        cp.wait()


def exp_all_to_all(x, cid, n=None):
    broadcast = n is not None
    shape = ((n,) + x.shape) if broadcast else x.shape
    n = shape[0]
    vmem = pltpu.MemorySpace.VMEM
    return pl.pallas_call(
        functools.partial(exp_all_to_all_kernel, broadcast),
        out_shape=jax.ShapeDtypeStruct(shape, x.dtype),
        in_specs=[pl.BlockSpec(memory_space=vmem)],
        out_specs=pl.BlockSpec(memory_space=vmem),
        scratch_shapes=[pltpu.SemaphoreType.DMA((n - 1,)), pltpu.SemaphoreType.DMA((n - 1,))],
        compiler_params=pltpu.CompilerParams(collective_id=cid, has_side_effects=True),
    )(x)


def rms_scale(matrix, gain):
    mean_square = jnp.mean(matrix * matrix, axis=-1, keepdims=True)
    return matrix * lax.rsqrt(mean_square + EPSILON) * gain


def expert_terms(block, gate_slice, up_slice, down_slice):
    gate = jnp.einsum("nek,ekf->nef", block, gate_slice, preferred_element_type=jnp.float32)
    upward = jnp.einsum("nek,ekf->nef", block, up_slice, preferred_element_type=jnp.float32)
    act = (jax.nn.silu(gate) * upward).astype(jnp.bfloat16)
    return jnp.einsum("nef,ekf->nek", act, down_slice, preferred_element_type=jnp.float32)


def local(
    tokens,
    array_type,
    block_pattern,
    gain_attn,
    w_query,
    w_key,
    w_value,
    logit_scale,
    w_out,
    gain_ffn,
    w_gate,
    w_up,
    w_down,
):
    n_exp = lax.axis_size("exp")
    row_count = tokens.shape[0]
    width = tokens.shape[1]
    head_cols = w_query.shape[1]
    heads_dev = logit_scale.shape[0]
    head_size = head_cols // heads_dev
    n_blocks = block_pattern.shape[0]
    inputs = tokens.astype(jnp.float32)
    normed_attn = rms_scale(inputs, gain_attn).astype(jnp.bfloat16)
    projector = jnp.concatenate([w_query, w_key, w_value], axis=1)
    joined_qkv = jnp.dot(
        exp_all_to_all(normed_attn, 3, n_exp).reshape(n_exp * row_count, width),
        projector,
        preferred_element_type=jnp.float32,
    ).astype(jnp.bfloat16)
    block_len = joined_qkv.shape[0]
    query_heads = joined_qkv[:, :head_cols].reshape(block_len, heads_dev, head_size)
    key_value = joined_qkv[:, head_cols:]
    position = lax.axis_index("seq")
    head_scale = logit_scale[:, None, None]

    def attend(state, kv_block, source):
        row_top, weight_sum, numerator = state
        key_rows = kv_block[:, :head_cols].reshape(block_len, heads_dev, head_size)
        value_rows = kv_block[:, head_cols:].reshape(block_len, heads_dev, head_size)
        allowed = block_pattern[position, source] > 0
        scores = (
            jnp.einsum("qhd,khd->hqk", query_heads, key_rows, preferred_element_type=jnp.float32)
            * head_scale
        )
        block_top = jnp.max(scores, axis=2)
        new_top = jnp.where(allowed, jnp.maximum(row_top, block_top), row_top)
        shifted = jnp.minimum(scores - new_top[:, :, None], 0.0)
        weights = jnp.where(allowed, jnp.exp(shifted), 0.0)
        rescale = jnp.exp(row_top - new_top)
        weight_sum = weight_sum * rescale + jnp.sum(weights, axis=2)
        contrib = jnp.einsum(
            "hqk,khd->qhd",
            weights.astype(jnp.bfloat16),
            value_rows,
            preferred_element_type=jnp.float32,
        )
        numerator = numerator * jnp.transpose(rescale)[:, :, None] + contrib
        return (new_top, weight_sum, numerator)

    start_state = (
        jnp.full((heads_dev, block_len), -jnp.inf, jnp.float32),
        jnp.zeros((heads_dev, block_len), jnp.float32),
        jnp.zeros((block_len, heads_dev, head_size), jnp.float32),
    )
    state = attend(start_state, key_value, position)
    offsets = [d for d in range(1, REACH + 1)] + [-d for d in range(1, REACH + 1)]
    neighbours = shift_exchange(key_value, offsets, "seq", "exp", 2)
    for distance in range(1, REACH + 1):
        state = attend(state, neighbours[distance - 1], (position - distance) % n_blocks)
        state = attend(state, neighbours[REACH + distance - 1], (position + distance) % n_blocks)
    heads_out = (
        (state[2] / jnp.transpose(state[1])[:, :, None])
        .astype(jnp.bfloat16)
        .reshape(block_len, head_cols)
    )
    all_heads = (
        exp_all_to_all(heads_out.reshape(n_exp, row_count, head_cols), 4)
        .transpose(1, 0, 2)
        .reshape(row_count, n_exp * head_cols)
    )
    attn_out = jnp.dot(
        all_heads,
        lax.all_gather(w_out, "exp", axis=0, tiled=True),
        preferred_element_type=jnp.float32,
    )
    hidden_state = inputs + attn_out
    normed_ffn = rms_scale(hidden_state, gain_ffn).astype(jnp.bfloat16)
    experts_dev = w_gate.shape[0]
    n_total = experts_dev * n_exp
    capacity = 2 * row_count // n_total
    one_hot = (array_type[:, None] == jnp.arange(n_total, dtype=jnp.int32)[None, :]).astype(
        jnp.int32
    )
    slot_rank = jnp.sum(jnp.cumsum(one_hot, axis=0) * one_hot, axis=1) - 1
    owner = array_type // experts_dev
    local_expert = array_type % experts_dev
    slot_id = (owner * capacity + slot_rank) * experts_dev + local_expert
    n_slots = n_exp * capacity * experts_dev
    selector = (slot_id[None, :] == jnp.arange(n_slots, dtype=jnp.int32)[:, None]).astype(
        jnp.bfloat16
    )
    outgoing = jnp.dot(selector, normed_ffn, preferred_element_type=jnp.float32).astype(
        jnp.bfloat16
    )
    outgoing = outgoing.reshape(n_exp * capacity, experts_dev, width)
    arrived = exp_all_to_all(
        outgoing.reshape((n_exp, -1) + outgoing.shape[1:]), 5
    ).reshape(outgoing.shape)
    gathered = lax.all_gather(arrived, "seq", axis=0, tiled=True)
    n_seq = lax.axis_size("seq")
    y_size = Y_RING if n_seq % Y_RING == 0 else n_seq
    partial = expert_terms(gathered, w_gate, w_up, w_down).astype(jnp.bfloat16)
    summed = ring_reduce(
        partial.reshape(partial.shape[0], width), n_seq // y_size, y_size
    ).reshape((-1,) + partial.shape[1:])
    returned = exp_all_to_all(summed.reshape((n_exp, -1) + summed.shape[1:]), 6).reshape(summed.shape)
    expert_out = jnp.dot(
        jnp.transpose(selector),
        returned.reshape(n_slots, width),
        preferred_element_type=jnp.float32,
    )
    return (hidden_state + expert_out).astype(jnp.bfloat16)


def solution(mesh):
    return jax.shard_map(
        local,
        mesh=mesh,
        in_specs=(
            P(("seq", "exp"), None),
            P(("seq", "exp")),
            P(),
            P(),
            P(None, "exp"),
            P(None, "exp"),
            P(None, "exp"),
            P("exp"),
            P("exp", None),
            P(),
            P("exp", None, "seq"),
            P("exp", None, "seq"),
            P("exp", None, "seq"),
        ),
        out_specs=P(("seq", "exp"), None),
        check_vma=False,
    )
```

```python
import jax
import jax.numpy as jnp
from jax import lax
from jax.sharding import PartitionSpec as P
from jax.experimental import pallas as pl
from jax.experimental.pallas import tpu as pltpu
import functools

REACH = 3
Y_RING = 8


EPSILON = 1e-05


def passed_along(block, axis, distance):
    devices = range(lax.axis_size(axis))
    route = [((i - distance) % len(devices), i) for i in devices]
    return lax.ppermute(block, axis, route)


def ring_reduce_kernel(nx, ny, part_ref, out_ref, recv1, send1, acc, recv2, send2,
                       s1_send, s1_recv, s2_send, s2_recv):
    me = lax.axis_index("seq")
    col = lax.axis_index("exp")
    x = me // ny
    y = me % ny
    y_up = x * ny + (y + 1) % ny
    y_down = x * ny + (y + ny - 1) % ny
    x_up = ((x + 1) % nx) * ny + y
    x_down = ((x + nx - 1) % nx) * ny + y
    half_x = nx // 2
    rows = part_ref.shape[2]
    half_r = rows // 2

    barrier = pltpu.get_barrier_semaphore()
    for peer in (y_up, y_down, x_up, x_down):
        pl.semaphore_signal(barrier, inc=1, device_id=(peer, col),
                            device_id_type=pl.DeviceIdType.MESH)
    pl.semaphore_wait(barrier, 4)

    lanes = ((y_up, 0, half_x, 1), (y_down, half_x, nx, -1))
    copies1 = []
    for k in range(ny - 1):
        step_copies = []
        for d, (peer, lo, hi, sign) in enumerate(lanes):
            c = (y - sign * (k + 1) + 2 * ny) % ny
            if k == 0:
                src = part_ref.at[lo:hi, c]
            else:
                copies1[k - 1][d].wait_recv()
                send1[d, k] = (recv1[d, k - 1].astype(jnp.float32)
                               + part_ref[lo:hi, c].astype(jnp.float32)).astype(send1.dtype)
                src = send1.at[d, k]
            cp = pltpu.make_async_remote_copy(
                src_ref=src, dst_ref=recv1.at[d, k],
                send_sem=s1_send.at[d, k], recv_sem=s1_recv.at[d, k],
                device_id=(peer, col), device_id_type=pl.DeviceIdType.MESH)
            cp.start()
            step_copies.append(cp)
        copies1.append(step_copies)
    for d, (peer, lo, hi, sign) in enumerate(lanes):
        copies1[ny - 2][d].wait_recv()
        acc[lo:hi] = recv1[d, ny - 2].astype(jnp.float32) + part_ref[lo:hi, y].astype(jnp.float32)

    lanes2 = ((x_up, 0, half_r, 1), (x_down, half_r, rows, -1))
    copies2 = []
    for k in range(nx - 1):
        step_copies = []
        for d, (peer, lo, hi, sign) in enumerate(lanes2):
            c = (x - sign * (k + 1) + 2 * nx) % nx
            if k == 0:
                src = acc.at[c, lo:hi]
            else:
                copies2[k - 1][d].wait_recv()
                send2[d, k] = recv2[d, k - 1] + acc[c, lo:hi]
                src = send2.at[d, k]
            cp = pltpu.make_async_remote_copy(
                src_ref=src, dst_ref=recv2.at[d, k],
                send_sem=s2_send.at[d, k], recv_sem=s2_recv.at[d, k],
                device_id=(peer, col), device_id_type=pl.DeviceIdType.MESH)
            cp.start()
            step_copies.append(cp)
        copies2.append(step_copies)
    for d, (peer, lo, hi, sign) in enumerate(lanes2):
        copies2[nx - 2][d].wait_recv()
        out_ref[lo:hi] = (recv2[d, nx - 2] + acc[x, lo:hi]).astype(out_ref.dtype)
    for step_copies in copies1 + copies2:
        for cp in step_copies:
            cp.wait_send()


def ring_reduce(part, nx, ny):
    width = part.shape[-1]
    rows = part.shape[0] // (nx * ny)
    part = part.reshape(nx, ny, rows, width)
    half_x = nx // 2
    half_r = rows // 2
    vmem = pltpu.MemorySpace.VMEM
    return pl.pallas_call(
        functools.partial(ring_reduce_kernel, nx, ny),
        out_shape=jax.ShapeDtypeStruct((rows, width), jnp.bfloat16),
        in_specs=[pl.BlockSpec(memory_space=vmem)],
        out_specs=pl.BlockSpec(memory_space=vmem),
        scratch_shapes=[
            pltpu.VMEM((2, ny - 1, half_x, rows, width), jnp.bfloat16),
            pltpu.VMEM((2, ny - 1, half_x, rows, width), jnp.bfloat16),
            pltpu.VMEM((nx, rows, width), jnp.float32),
            pltpu.VMEM((2, nx - 1, half_r, width), jnp.float32),
            pltpu.VMEM((2, nx - 1, half_r, width), jnp.float32),
            pltpu.SemaphoreType.DMA((2, ny - 1)),
            pltpu.SemaphoreType.DMA((2, ny - 1)),
            pltpu.SemaphoreType.DMA((2, nx - 1)),
            pltpu.SemaphoreType.DMA((2, nx - 1)),
        ],
        compiler_params=pltpu.CompilerParams(
            collective_id=1, has_side_effects=True, vmem_limit_bytes=48 * 1024 * 1024
        ),
    )(part)


def shift_exchange_kernel(offsets, axis, other, block_ref, out_ref, send_sems, recv_sems):
    n = lax.axis_size(axis)
    me = lax.axis_index(axis)
    col = lax.axis_index(other)

    def dev(peer):
        return (peer, col) if axis == "seq" else (col, peer)

    targets = [(me + o + n * len(offsets)) % n for o in offsets]
    barrier = pltpu.get_barrier_semaphore()
    for peer in targets:
        pl.semaphore_signal(barrier, inc=1, device_id=dev(peer),
                            device_id_type=pl.DeviceIdType.MESH)
    pl.semaphore_wait(barrier, len(offsets))
    copies = []
    for j, peer in enumerate(targets):
        cp = pltpu.make_async_remote_copy(
            src_ref=block_ref, dst_ref=out_ref.at[j],
            send_sem=send_sems.at[j], recv_sem=recv_sems.at[j],
            device_id=dev(peer), device_id_type=pl.DeviceIdType.MESH)
        cp.start()
        copies.append(cp)
    for cp in copies:
        cp.wait()


def shift_exchange(block, offsets, axis, other, cid):
    vmem = pltpu.MemorySpace.VMEM
    k = len(offsets)
    return pl.pallas_call(
        functools.partial(shift_exchange_kernel, tuple(offsets), axis, other),
        out_shape=jax.ShapeDtypeStruct((k,) + block.shape, block.dtype),
        in_specs=[pl.BlockSpec(memory_space=vmem)],
        out_specs=pl.BlockSpec(memory_space=vmem),
        scratch_shapes=[pltpu.SemaphoreType.DMA((k,)), pltpu.SemaphoreType.DMA((k,))],
        compiler_params=pltpu.CompilerParams(collective_id=cid, has_side_effects=True),
    )(block)


def exp_all_to_all_kernel(x_ref, y_ref, send_sems, recv_sems):
    n = lax.axis_size("exp")
    me = lax.axis_index("exp")
    row = lax.axis_index("seq")
    barrier = pltpu.get_barrier_semaphore()
    for k in range(1, n):
        pl.semaphore_signal(barrier, inc=1, device_id=(row, (me + k) % n),
                            device_id_type=pl.DeviceIdType.MESH)
    pl.semaphore_wait(barrier, n - 1)
    copies = []
    for k in range(1, n):
        peer = (me + k) % n
        cp = pltpu.make_async_remote_copy(
            src_ref=x_ref.at[peer], dst_ref=y_ref.at[me],
            send_sem=send_sems.at[k - 1], recv_sem=recv_sems.at[k - 1],
            device_id=(row, peer), device_id_type=pl.DeviceIdType.MESH)
        cp.start()
        copies.append(cp)
    y_ref[me] = x_ref[me]
    for cp in copies:
        cp.wait()


def exp_all_to_all(x, cid):
    n = x.shape[0]
    vmem = pltpu.MemorySpace.VMEM
    return pl.pallas_call(
        exp_all_to_all_kernel,
        out_shape=jax.ShapeDtypeStruct(x.shape, x.dtype),
        in_specs=[pl.BlockSpec(memory_space=vmem)],
        out_specs=pl.BlockSpec(memory_space=vmem),
        scratch_shapes=[pltpu.SemaphoreType.DMA((n - 1,)), pltpu.SemaphoreType.DMA((n - 1,))],
        compiler_params=pltpu.CompilerParams(collective_id=cid, has_side_effects=True),
    )(x)


def ring_gather_kernel(nx, ny, block_ref, out_ref, local_sem, send_sems, recv_sems):
    me = lax.axis_index("seq")
    col = lax.axis_index("exp")
    x = me // ny
    y = me % ny
    rows = block_ref.shape[0]
    hr = rows // 2

    def dev(a, b):
        return ((a + nx) % nx * ny + (b + ny) % ny, col)

    peers = [dev(x, y + 1), dev(x, y - 1), dev(x + 1, y), dev(x - 1, y)]
    barrier = pltpu.get_barrier_semaphore()
    for peer in peers:
        pl.semaphore_signal(barrier, inc=1, device_id=peer, device_id_type=pl.DeviceIdType.MESH)
    pl.semaphore_wait(barrier, 4)

    own = pltpu.make_async_copy(block_ref, out_ref.at[x, y], local_sem.at[0])
    own.start()
    sem_count = [0]

    def unit(axis, stage, u, lo, hi):
        if axis == "y":
            return out_ref.at[x, u, lo:hi] if stage == 1 else out_ref.at[:, u, lo:hi]
        return out_ref.at[u, y, lo:hi] if stage == 1 else out_ref.at[u, :, lo:hi]

    def ring(axis, stage, lo, hi):
        n = ny if axis == "y" else nx
        c = y if axis == "y" else x
        half = n // 2
        mid = (lo + hi) // 2
        steps = []
        for sign in (1, -1):
            prev = None
            lane = []
            for k in range(half):
                u = (c - sign * k + 2 * n) % n
                a_lo, a_hi = lo, hi
                if k == half - 1 and n % 2 == 0:
                    a_lo, a_hi = (lo, mid) if sign == 1 else (mid, hi)
                if stage == 1 and k == 0:
                    src = block_ref.at[a_lo:a_hi]
                else:
                    src = unit(axis, stage, u, a_lo, a_hi)
                dst = unit(axis, stage, u, a_lo, a_hi)
                target = dev(x, y + sign) if axis == "y" else dev(x + sign, y)
                j = sem_count[0]
                sem_count[0] += 1
                cp = pltpu.make_async_remote_copy(
                    src_ref=src, dst_ref=dst, send_sem=send_sems.at[j], recv_sem=recv_sems.at[j],
                    device_id=target, device_id_type=pl.DeviceIdType.MESH)
                lane.append((prev, cp))
                prev = cp
            steps.append(lane)
        return steps

    plans = []
    for lo, hi, first, second in ((0, hr, "y", "x"), (hr, rows, "x", "y")):
        s1 = ring(first, 1, lo, hi)
        s2 = ring(second, 2, lo, hi)
        plans.append((s1, s2))

    started = []

    def run(lane_list):
        depth = max(len(l) for l in lane_list)
        for k in range(depth):
            for lane in lane_list:
                if k < len(lane):
                    prev, cp = lane[k]
                    if prev is not None:
                        prev.wait_recv()
                    cp.start()
                    started.append(cp)

    run([lane for s1, _ in plans for lane in s1])
    for s1, _ in plans:
        for lane in s1:
            lane[-1][1].wait_recv()
    own.wait()
    run([lane for _, s2 in plans for lane in s2])
    for _, s2 in plans:
        for lane in s2:
            lane[-1][1].wait_recv()
    for cp in started:
        cp.wait_send()


def ring_gather(block, nx, ny):
    vmem = pltpu.MemorySpace.VMEM
    n_sems = 4 * (nx // 2 + ny // 2) + 4
    return pl.pallas_call(
        functools.partial(ring_gather_kernel, nx, ny),
        out_shape=jax.ShapeDtypeStruct((nx, ny) + block.shape, block.dtype),
        in_specs=[pl.BlockSpec(memory_space=vmem)],
        out_specs=pl.BlockSpec(memory_space=vmem),
        scratch_shapes=[
            pltpu.SemaphoreType.DMA((1,)),
            pltpu.SemaphoreType.DMA((n_sems,)),
            pltpu.SemaphoreType.DMA((n_sems,)),
        ],
        compiler_params=pltpu.CompilerParams(
            collective_id=3, has_side_effects=True, vmem_limit_bytes=48 * 1024 * 1024
        ),
    )(block)


def rms_scale(matrix, gain):
    mean_square = jnp.mean(matrix * matrix, axis=-1, keepdims=True)
    return matrix * lax.rsqrt(mean_square + EPSILON) * gain


def expert_terms(block, gate_slice, up_slice, down_slice):
    gate = jnp.einsum("nek,ekf->nef", block, gate_slice, preferred_element_type=jnp.float32)
    upward = jnp.einsum("nek,ekf->nef", block, up_slice, preferred_element_type=jnp.float32)
    act = (jax.nn.silu(gate) * upward).astype(jnp.bfloat16)
    return jnp.einsum("nef,ekf->nek", act, down_slice, preferred_element_type=jnp.float32)


def local(
    tokens,
    array_type,
    block_pattern,
    gain_attn,
    w_query,
    w_key,
    w_value,
    logit_scale,
    w_out,
    gain_ffn,
    w_gate,
    w_up,
    w_down,
):
    n_exp = lax.axis_size("exp")
    row_count = tokens.shape[0]
    width = tokens.shape[1]
    head_cols = w_query.shape[1]
    heads_dev = logit_scale.shape[0]
    head_size = head_cols // heads_dev
    n_blocks = block_pattern.shape[0]
    inputs = tokens.astype(jnp.float32)
    normed_attn = rms_scale(inputs, gain_attn).astype(jnp.bfloat16)
    projector = jnp.concatenate([w_query, w_key, w_value], axis=1)
    joined_qkv = jnp.dot(
        lax.all_gather(normed_attn, "exp", axis=0, tiled=True),
        projector,
        preferred_element_type=jnp.float32,
    ).astype(jnp.bfloat16)
    block_len = joined_qkv.shape[0]
    query_heads = joined_qkv[:, :head_cols].reshape(block_len, heads_dev, head_size)
    key_value = joined_qkv[:, head_cols:]
    position = lax.axis_index("seq")
    head_scale = logit_scale[:, None, None]

    def attend(state, kv_block, source):
        row_top, weight_sum, numerator = state
        key_rows = kv_block[:, :head_cols].reshape(block_len, heads_dev, head_size)
        value_rows = kv_block[:, head_cols:].reshape(block_len, heads_dev, head_size)
        allowed = block_pattern[position, source] > 0
        scores = (
            jnp.einsum("qhd,khd->hqk", query_heads, key_rows, preferred_element_type=jnp.float32)
            * head_scale
        )
        block_top = jnp.max(scores, axis=2)
        new_top = jnp.where(allowed, jnp.maximum(row_top, block_top), row_top)
        shifted = jnp.minimum(scores - new_top[:, :, None], 0.0)
        weights = jnp.where(allowed, jnp.exp(shifted), 0.0)
        rescale = jnp.exp(row_top - new_top)
        weight_sum = weight_sum * rescale + jnp.sum(weights, axis=2)
        contrib = jnp.einsum(
            "hqk,khd->qhd",
            weights.astype(jnp.bfloat16),
            value_rows,
            preferred_element_type=jnp.float32,
        )
        numerator = numerator * jnp.transpose(rescale)[:, :, None] + contrib
        return (new_top, weight_sum, numerator)

    start_state = (
        jnp.full((heads_dev, block_len), -jnp.inf, jnp.float32),
        jnp.zeros((heads_dev, block_len), jnp.float32),
        jnp.zeros((block_len, heads_dev, head_size), jnp.float32),
    )
    state = attend(start_state, key_value, position)
    offsets = [d for d in range(1, REACH + 1)] + [-d for d in range(1, REACH + 1)]
    neighbours = shift_exchange(key_value, offsets, "seq", "exp", 2)
    for distance in range(1, REACH + 1):
        state = attend(state, neighbours[distance - 1], (position - distance) % n_blocks)
        state = attend(state, neighbours[REACH + distance - 1], (position + distance) % n_blocks)
    heads_out = (
        (state[2] / jnp.transpose(state[1])[:, :, None])
        .astype(jnp.bfloat16)
        .reshape(block_len, head_cols)
    )
    all_heads = lax.all_to_all(heads_out, "exp", split_axis=0, concat_axis=1, tiled=True)
    attn_out = jnp.dot(
        all_heads,
        lax.all_gather(w_out, "exp", axis=0, tiled=True),
        preferred_element_type=jnp.float32,
    )
    hidden_state = inputs + attn_out
    normed_ffn = rms_scale(hidden_state, gain_ffn).astype(jnp.bfloat16)
    experts_dev = w_gate.shape[0]
    n_total = experts_dev * n_exp
    capacity = 2 * row_count // n_total
    one_hot = (array_type[:, None] == jnp.arange(n_total, dtype=jnp.int32)[None, :]).astype(
        jnp.int32
    )
    slot_rank = jnp.sum(jnp.cumsum(one_hot, axis=0) * one_hot, axis=1) - 1
    owner = array_type // experts_dev
    local_expert = array_type % experts_dev
    slot_id = (owner * capacity + slot_rank) * experts_dev + local_expert
    n_slots = n_exp * capacity * experts_dev
    selector = (slot_id[None, :] == jnp.arange(n_slots, dtype=jnp.int32)[:, None]).astype(
        jnp.bfloat16
    )
    outgoing = jnp.dot(selector, normed_ffn, preferred_element_type=jnp.float32).astype(
        jnp.bfloat16
    )
    outgoing = outgoing.reshape(n_exp * capacity, experts_dev, width)
    arrived = lax.all_to_all(outgoing, "exp", split_axis=0, concat_axis=0, tiled=True)
    n_seq = lax.axis_size("seq")
    y_size = Y_RING if n_seq % Y_RING == 0 else n_seq
    gathered = ring_gather(
        arrived.reshape(arrived.shape[0], width), n_seq // y_size, y_size
    ).reshape((n_seq * arrived.shape[0],) + arrived.shape[1:])
    n_seq = lax.axis_size("seq")
    y_size = Y_RING if n_seq % Y_RING == 0 else n_seq
    partial = expert_terms(gathered, w_gate, w_up, w_down).astype(jnp.bfloat16)
    summed = ring_reduce(
        partial.reshape(partial.shape[0], width), n_seq // y_size, y_size
    ).reshape((-1,) + partial.shape[1:])
    returned = lax.all_to_all(summed, "exp", split_axis=0, concat_axis=0, tiled=True)
    expert_out = jnp.dot(
        jnp.transpose(selector),
        returned.reshape(n_slots, width),
        preferred_element_type=jnp.float32,
    )
    return (hidden_state + expert_out).astype(jnp.bfloat16)


def solution(mesh):
    return jax.shard_map(
        local,
        mesh=mesh,
        in_specs=(
            P(("seq", "exp"), None),
            P(("seq", "exp")),
            P(),
            P(),
            P(None, "exp"),
            P(None, "exp"),
            P(None, "exp"),
            P("exp"),
            P("exp", None),
            P(),
            P("exp", None, "seq"),
            P("exp", None, "seq"),
            P("exp", None, "seq"),
        ),
        out_specs=P(("seq", "exp"), None),
        check_vma=False,
    )
```

```python
import jax
import jax.numpy as jnp
from jax import lax
from jax.sharding import PartitionSpec as P
from jax.experimental import pallas as pl
from jax.experimental.pallas import tpu as pltpu
import functools

REACH = 3
Y_RING = 8
CORES = 2


EPSILON = 1e-05


def passed_along(block, axis, distance):
    devices = range(lax.axis_size(axis))
    route = [((i - distance) % len(devices), i) for i in devices]
    return lax.ppermute(block, axis, route)


def ring_reduce_kernel(nx, ny, part_ref, out_ref, recv1, send1, acc, recv2, send2,
                       s1_send, s1_recv, s2_send, s2_recv):
    me = lax.axis_index("seq")
    col = lax.axis_index("exp")
    x = me // ny
    y = me % ny
    y_up = x * ny + (y + 1) % ny
    y_down = x * ny + (y + ny - 1) % ny
    x_up = ((x + 1) % nx) * ny + y
    x_down = ((x + nx - 1) % nx) * ny + y
    half_x = nx // 2
    rows = part_ref.shape[2]
    half_r = rows // 2

    barrier = pltpu.get_barrier_semaphore()
    for peer in (y_up, y_down, x_up, x_down):
        pl.semaphore_signal(barrier, inc=1, device_id=(peer, col),
                            device_id_type=pl.DeviceIdType.MESH)
    pl.semaphore_wait(barrier, 4)

    lanes = ((y_up, 0, half_x, 1), (y_down, half_x, nx, -1))
    copies1 = []
    for k in range(ny - 1):
        step_copies = []
        for d, (peer, lo, hi, sign) in enumerate(lanes):
            c = (y - sign * (k + 1) + 2 * ny) % ny
            if k == 0:
                src = part_ref.at[lo:hi, c]
            else:
                copies1[k - 1][d].wait_recv()
                send1[d, k] = (recv1[d, k - 1].astype(jnp.float32)
                               + part_ref[lo:hi, c].astype(jnp.float32)).astype(send1.dtype)
                src = send1.at[d, k]
            cp = pltpu.make_async_remote_copy(
                src_ref=src, dst_ref=recv1.at[d, k],
                send_sem=s1_send.at[d, k], recv_sem=s1_recv.at[d, k],
                device_id=(peer, col), device_id_type=pl.DeviceIdType.MESH)
            cp.start()
            step_copies.append(cp)
        copies1.append(step_copies)
    for d, (peer, lo, hi, sign) in enumerate(lanes):
        copies1[ny - 2][d].wait_recv()
        acc[lo:hi] = recv1[d, ny - 2].astype(jnp.float32) + part_ref[lo:hi, y].astype(jnp.float32)

    lanes2 = ((x_up, 0, half_r, 1), (x_down, half_r, rows, -1))
    copies2 = []
    for k in range(nx - 1):
        step_copies = []
        for d, (peer, lo, hi, sign) in enumerate(lanes2):
            c = (x - sign * (k + 1) + 2 * nx) % nx
            if k == 0:
                src = acc.at[c, lo:hi]
            else:
                copies2[k - 1][d].wait_recv()
                send2[d, k] = recv2[d, k - 1] + acc[c, lo:hi]
                src = send2.at[d, k]
            cp = pltpu.make_async_remote_copy(
                src_ref=src, dst_ref=recv2.at[d, k],
                send_sem=s2_send.at[d, k], recv_sem=s2_recv.at[d, k],
                device_id=(peer, col), device_id_type=pl.DeviceIdType.MESH)
            cp.start()
            step_copies.append(cp)
        copies2.append(step_copies)
    for d, (peer, lo, hi, sign) in enumerate(lanes2):
        copies2[nx - 2][d].wait_recv()
        out_ref[lo:hi] = (recv2[d, nx - 2] + acc[x, lo:hi]).astype(out_ref.dtype)
    for step_copies in copies1 + copies2:
        for cp in step_copies:
            cp.wait_send()


def ring_reduce(part, nx, ny):
    width = part.shape[-1]
    rows = part.shape[0] // (nx * ny)
    part = part.reshape(nx, ny, rows, width)
    half_x = nx // 2
    half_r = rows // 2
    vmem = pltpu.MemorySpace.VMEM
    return pl.pallas_call(
        functools.partial(ring_reduce_kernel, nx, ny),
        out_shape=jax.ShapeDtypeStruct((rows, width), jnp.bfloat16),
        in_specs=[pl.BlockSpec(memory_space=vmem)],
        out_specs=pl.BlockSpec(memory_space=vmem),
        scratch_shapes=[
            pltpu.VMEM((2, ny - 1, half_x, rows, width), jnp.bfloat16),
            pltpu.VMEM((2, ny - 1, half_x, rows, width), jnp.bfloat16),
            pltpu.VMEM((nx, rows, width), jnp.float32),
            pltpu.VMEM((2, nx - 1, half_r, width), jnp.float32),
            pltpu.VMEM((2, nx - 1, half_r, width), jnp.float32),
            pltpu.SemaphoreType.DMA((2, ny - 1)),
            pltpu.SemaphoreType.DMA((2, ny - 1)),
            pltpu.SemaphoreType.DMA((2, nx - 1)),
            pltpu.SemaphoreType.DMA((2, nx - 1)),
        ],
        compiler_params=pltpu.CompilerParams(
            collective_id=1, has_side_effects=True, vmem_limit_bytes=48 * 1024 * 1024
        ),
    )(part)


def shift_exchange_kernel(offsets, axis, other, block_ref, out_ref, send_sems, recv_sems):
    n = lax.axis_size(axis)
    me = lax.axis_index(axis)
    col = lax.axis_index(other)

    def dev(peer):
        return (peer, col) if axis == "seq" else (col, peer)

    targets = [(me + o + n * len(offsets)) % n for o in offsets]
    barrier = pltpu.get_barrier_semaphore()
    for peer in targets:
        pl.semaphore_signal(barrier, inc=1, device_id=dev(peer),
                            device_id_type=pl.DeviceIdType.MESH)
    pl.semaphore_wait(barrier, len(offsets))
    copies = []
    for j, peer in enumerate(targets):
        cp = pltpu.make_async_remote_copy(
            src_ref=block_ref, dst_ref=out_ref.at[j],
            send_sem=send_sems.at[j], recv_sem=recv_sems.at[j],
            device_id=dev(peer), device_id_type=pl.DeviceIdType.MESH)
        cp.start()
        copies.append(cp)
    for cp in copies:
        cp.wait()


def shift_exchange(block, offsets, axis, other, cid):
    vmem = pltpu.MemorySpace.VMEM
    k = len(offsets)
    return pl.pallas_call(
        functools.partial(shift_exchange_kernel, tuple(offsets), axis, other),
        out_shape=jax.ShapeDtypeStruct((k,) + block.shape, block.dtype),
        in_specs=[pl.BlockSpec(memory_space=vmem)],
        out_specs=pl.BlockSpec(memory_space=vmem),
        scratch_shapes=[pltpu.SemaphoreType.DMA((k,)), pltpu.SemaphoreType.DMA((k,))],
        compiler_params=pltpu.CompilerParams(collective_id=cid, has_side_effects=True),
    )(block)


def exp_all_to_all_kernel(x_ref, y_ref, send_sems, recv_sems):
    n = lax.axis_size("exp")
    me = lax.axis_index("exp")
    row = lax.axis_index("seq")
    barrier = pltpu.get_barrier_semaphore()
    for k in range(1, n):
        pl.semaphore_signal(barrier, inc=1, device_id=(row, (me + k) % n),
                            device_id_type=pl.DeviceIdType.MESH)
    pl.semaphore_wait(barrier, n - 1)
    copies = []
    for k in range(1, n):
        peer = (me + k) % n
        cp = pltpu.make_async_remote_copy(
            src_ref=x_ref.at[peer], dst_ref=y_ref.at[me],
            send_sem=send_sems.at[k - 1], recv_sem=recv_sems.at[k - 1],
            device_id=(row, peer), device_id_type=pl.DeviceIdType.MESH)
        cp.start()
        copies.append(cp)
    y_ref[me] = x_ref[me]
    for cp in copies:
        cp.wait()


def exp_all_to_all(x, cid):
    n = x.shape[0]
    vmem = pltpu.MemorySpace.VMEM
    return pl.pallas_call(
        exp_all_to_all_kernel,
        out_shape=jax.ShapeDtypeStruct(x.shape, x.dtype),
        in_specs=[pl.BlockSpec(memory_space=vmem)],
        out_specs=pl.BlockSpec(memory_space=vmem),
        scratch_shapes=[pltpu.SemaphoreType.DMA((n - 1,)), pltpu.SemaphoreType.DMA((n - 1,))],
        compiler_params=pltpu.CompilerParams(collective_id=cid, has_side_effects=True),
    )(x)


def ring_gather_kernel(nx, ny, axis, other, block_ref, out_ref, local_sem, send_sems, recv_sems):
    me = lax.axis_index(axis)
    col = lax.axis_index(other)
    x = me // ny
    y = me % ny
    rows = block_ref.shape[0]
    hr = rows // 2

    def dev(a, b):
        idx = (a + nx) % nx * ny + (b + ny) % ny
        return (idx, col) if axis == "seq" else (col, idx)

    peers = [dev(x, y + 1), dev(x, y - 1), dev(x + 1, y), dev(x - 1, y)]
    barrier = pltpu.get_barrier_semaphore()
    for peer in peers:
        pl.semaphore_signal(barrier, inc=1, device_id=peer, device_id_type=pl.DeviceIdType.MESH)
    pl.semaphore_wait(barrier, 4)

    own = pltpu.make_async_copy(block_ref, out_ref.at[x, y], local_sem.at[0])
    own.start()
    sem_count = [0]

    def unit(axis, stage, u, lo, hi):
        if axis == "y":
            return out_ref.at[x, u, lo:hi] if stage == 1 else out_ref.at[:, u, lo:hi]
        return out_ref.at[u, y, lo:hi] if stage == 1 else out_ref.at[u, :, lo:hi]

    def ring(axis, stage, lo, hi):
        n = ny if axis == "y" else nx
        c = y if axis == "y" else x
        half = n // 2
        mid = (lo + hi) // 2
        steps = []
        for sign in (1, -1):
            prev = None
            lane = []
            for k in range(half):
                u = (c - sign * k + 2 * n) % n
                a_lo, a_hi = lo, hi
                if k == half - 1 and n % 2 == 0:
                    a_lo, a_hi = (lo, mid) if sign == 1 else (mid, hi)
                if stage == 1 and k == 0:
                    src = block_ref.at[a_lo:a_hi]
                else:
                    src = unit(axis, stage, u, a_lo, a_hi)
                dst = unit(axis, stage, u, a_lo, a_hi)
                target = dev(x, y + sign) if axis == "y" else dev(x + sign, y)
                j = sem_count[0]
                sem_count[0] += 1
                cp = pltpu.make_async_remote_copy(
                    src_ref=src, dst_ref=dst, send_sem=send_sems.at[j], recv_sem=recv_sems.at[j],
                    device_id=target, device_id_type=pl.DeviceIdType.MESH)
                lane.append((prev, cp))
                prev = cp
            steps.append(lane)
        return steps

    plans = []
    for lo, hi, first, second in ((0, hr, "y", "x"), (hr, rows, "x", "y")):
        s1 = ring(first, 1, lo, hi)
        s2 = ring(second, 2, lo, hi)
        plans.append((s1, s2))

    started = []

    def run(lane_list):
        depth = max(len(l) for l in lane_list)
        for k in range(depth):
            for lane in lane_list:
                if k < len(lane):
                    prev, cp = lane[k]
                    if prev is not None:
                        prev.wait_recv()
                    cp.start()
                    started.append(cp)

    run([lane for s1, _ in plans for lane in s1])
    for s1, _ in plans:
        for lane in s1:
            lane[-1][1].wait_recv()
    own.wait()
    run([lane for _, s2 in plans for lane in s2])
    for _, s2 in plans:
        for lane in s2:
            lane[-1][1].wait_recv()
    for cp in started:
        cp.wait_send()


def ring_gather(block, nx, ny, axis="seq", other="exp", cid=3):
    vmem = pltpu.MemorySpace.VMEM
    n_sems = 4 * (nx // 2 + ny // 2) + 4
    return pl.pallas_call(
        functools.partial(ring_gather_kernel, nx, ny, axis, other),
        out_shape=jax.ShapeDtypeStruct((nx, ny) + block.shape, block.dtype),
        in_specs=[pl.BlockSpec(memory_space=vmem)],
        out_specs=pl.BlockSpec(memory_space=vmem),
        scratch_shapes=[
            pltpu.SemaphoreType.DMA((1,)),
            pltpu.SemaphoreType.DMA((n_sems,)),
            pltpu.SemaphoreType.DMA((n_sems,)),
        ],
        compiler_params=pltpu.CompilerParams(
            collective_id=cid, has_side_effects=True, vmem_limit_bytes=48 * 1024 * 1024
        ),
    )(block)


def rms_scale(matrix, gain):
    mean_square = jnp.mean(matrix * matrix, axis=-1, keepdims=True)
    return matrix * lax.rsqrt(mean_square + EPSILON) * gain


def expert_terms(block, gate_slice, up_slice, down_slice):
    gate = jnp.einsum("nek,ekf->nef", block, gate_slice, preferred_element_type=jnp.float32)
    upward = jnp.einsum("nek,ekf->nef", block, up_slice, preferred_element_type=jnp.float32)
    act = (jax.nn.silu(gate) * upward).astype(jnp.bfloat16)
    return jnp.einsum("nef,ekf->nek", act, down_slice, preferred_element_type=jnp.float32)


def local(
    tokens,
    array_type,
    block_pattern,
    gain_attn,
    w_query,
    w_key,
    w_value,
    logit_scale,
    w_out,
    gain_ffn,
    w_gate,
    w_up,
    w_down,
):
    n_exp = lax.axis_size("exp")
    row_count = tokens.shape[0]
    width = tokens.shape[1]
    head_cols = w_query.shape[1]
    heads_dev = logit_scale.shape[0]
    head_size = head_cols // heads_dev
    n_blocks = block_pattern.shape[0]
    inputs = tokens.astype(jnp.float32)
    normed_attn = rms_scale(inputs, gain_attn).astype(jnp.bfloat16)
    projector = jnp.concatenate([w_query, w_key, w_value], axis=1)
    joined_qkv = jnp.dot(
        ring_gather(normed_attn, n_exp // CORES, CORES, "exp", "seq", 4).reshape(n_exp * row_count, width),
        projector,
        preferred_element_type=jnp.float32,
    ).astype(jnp.bfloat16)
    block_len = joined_qkv.shape[0]
    query_heads = joined_qkv[:, :head_cols].reshape(block_len, heads_dev, head_size)
    key_value = joined_qkv[:, head_cols:]
    position = lax.axis_index("seq")
    head_scale = logit_scale[:, None, None]

    def attend(state, kv_block, source):
        row_top, weight_sum, numerator = state
        key_rows = kv_block[:, :head_cols].reshape(block_len, heads_dev, head_size)
        value_rows = kv_block[:, head_cols:].reshape(block_len, heads_dev, head_size)
        allowed = block_pattern[position, source] > 0
        scores = (
            jnp.einsum("qhd,khd->hqk", query_heads, key_rows, preferred_element_type=jnp.float32)
            * head_scale
        )
        block_top = jnp.max(scores, axis=2)
        new_top = jnp.where(allowed, jnp.maximum(row_top, block_top), row_top)
        shifted = jnp.minimum(scores - new_top[:, :, None], 0.0)
        weights = jnp.where(allowed, jnp.exp(shifted), 0.0)
        rescale = jnp.exp(row_top - new_top)
        weight_sum = weight_sum * rescale + jnp.sum(weights, axis=2)
        contrib = jnp.einsum(
            "hqk,khd->qhd",
            weights.astype(jnp.bfloat16),
            value_rows,
            preferred_element_type=jnp.float32,
        )
        numerator = numerator * jnp.transpose(rescale)[:, :, None] + contrib
        return (new_top, weight_sum, numerator)

    start_state = (
        jnp.full((heads_dev, block_len), -jnp.inf, jnp.float32),
        jnp.zeros((heads_dev, block_len), jnp.float32),
        jnp.zeros((block_len, heads_dev, head_size), jnp.float32),
    )
    state = attend(start_state, key_value, position)
    offsets = [d for d in range(1, REACH + 1)] + [-d for d in range(1, REACH + 1)]
    neighbours = shift_exchange(key_value, offsets, "seq", "exp", 2)
    for distance in range(1, REACH + 1):
        state = attend(state, neighbours[distance - 1], (position - distance) % n_blocks)
        state = attend(state, neighbours[REACH + distance - 1], (position + distance) % n_blocks)
    heads_out = (
        (state[2] / jnp.transpose(state[1])[:, :, None])
        .astype(jnp.bfloat16)
        .reshape(block_len, head_cols)
    )
    all_heads = lax.all_to_all(heads_out, "exp", split_axis=0, concat_axis=1, tiled=True)
    attn_out = jnp.dot(
        all_heads,
        lax.all_gather(w_out, "exp", axis=0, tiled=True),
        preferred_element_type=jnp.float32,
    )
    hidden_state = inputs + attn_out
    normed_ffn = rms_scale(hidden_state, gain_ffn).astype(jnp.bfloat16)
    experts_dev = w_gate.shape[0]
    n_total = experts_dev * n_exp
    capacity = 2 * row_count // n_total
    one_hot = (array_type[:, None] == jnp.arange(n_total, dtype=jnp.int32)[None, :]).astype(
        jnp.int32
    )
    slot_rank = jnp.sum(jnp.cumsum(one_hot, axis=0) * one_hot, axis=1) - 1
    owner = array_type // experts_dev
    local_expert = array_type % experts_dev
    slot_id = (owner * capacity + slot_rank) * experts_dev + local_expert
    n_slots = n_exp * capacity * experts_dev
    selector = (slot_id[None, :] == jnp.arange(n_slots, dtype=jnp.int32)[:, None]).astype(
        jnp.bfloat16
    )
    outgoing = jnp.dot(selector, normed_ffn, preferred_element_type=jnp.float32).astype(
        jnp.bfloat16
    )
    outgoing = outgoing.reshape(n_exp * capacity, experts_dev, width)
    arrived = lax.all_to_all(outgoing, "exp", split_axis=0, concat_axis=0, tiled=True)
    n_seq = lax.axis_size("seq")
    y_size = Y_RING if n_seq % Y_RING == 0 else n_seq
    gathered = ring_gather(
        arrived.reshape(arrived.shape[0], width), n_seq // y_size, y_size
    ).reshape((n_seq * arrived.shape[0],) + arrived.shape[1:])
    n_seq = lax.axis_size("seq")
    y_size = Y_RING if n_seq % Y_RING == 0 else n_seq
    partial = expert_terms(gathered, w_gate, w_up, w_down).astype(jnp.bfloat16)
    summed = ring_reduce(
        partial.reshape(partial.shape[0], width), n_seq // y_size, y_size
    ).reshape((-1,) + partial.shape[1:])
    returned = lax.all_to_all(summed, "exp", split_axis=0, concat_axis=0, tiled=True)
    expert_out = jnp.dot(
        jnp.transpose(selector),
        returned.reshape(n_slots, width),
        preferred_element_type=jnp.float32,
    )
    return (hidden_state + expert_out).astype(jnp.bfloat16)


def solution(mesh):
    return jax.shard_map(
        local,
        mesh=mesh,
        in_specs=(
            P(("seq", "exp"), None),
            P(("seq", "exp")),
            P(),
            P(),
            P(None, "exp"),
            P(None, "exp"),
            P(None, "exp"),
            P("exp"),
            P("exp", None),
            P(),
            P("exp", None, "seq"),
            P("exp", None, "seq"),
            P("exp", None, "seq"),
        ),
        out_specs=P(("seq", "exp"), None),
        check_vma=False,
    )
```

```python
import jax
import jax.numpy as jnp
from jax import lax
from jax.sharding import PartitionSpec as P
from jax.experimental import pallas as pl
from jax.experimental.pallas import tpu as pltpu
import functools

REACH = 3
Y_RING = 8
CORES = 2


EPSILON = 1e-05


def passed_along(block, axis, distance):
    devices = range(lax.axis_size(axis))
    route = [((i - distance) % len(devices), i) for i in devices]
    return lax.ppermute(block, axis, route)


def ring_reduce_kernel(nx, ny, splits, part_ref, out_ref, recv1, send1, acc, recv2, send2,
                       s1_send, s1_recv, s2_send, s2_recv):
    me = lax.axis_index("seq")
    col = lax.axis_index("exp")
    x = me // ny
    y = me % ny
    y_up = x * ny + (y + 1) % ny
    y_down = x * ny + (y + ny - 1) % ny
    x_up = ((x + 1) % nx) * ny + y
    x_down = ((x + nx - 1) % nx) * ny + y
    rows = part_ref.shape[2]
    piece = rows // splits
    quarter = rows // 4

    barrier = pltpu.get_barrier_semaphore()
    for peer in (y_up, y_down, x_up, x_down):
        pl.semaphore_signal(barrier, inc=1, device_id=(peer, col),
                            device_id_type=pl.DeviceIdType.MESH)
    pl.semaphore_wait(barrier, 4)

    lanes = []
    for a in range(nx):
        for p in range(splits):
            if a < nx // 2:
                lanes.append((y_up, 1, a, p * piece))
            else:
                lanes.append((y_down, -1, a, p * piece))
    copies1 = []
    for k in range(ny - 1):
        step_copies = []
        for d, (peer, sign, a, r0) in enumerate(lanes):
            c = (y - sign * (k + 1) + 2 * ny) % ny
            if k == 0:
                src = part_ref.at[a, c, r0:r0 + piece]
            else:
                copies1[k - 1][d].wait_recv()
                send1[d, k] = (recv1[d, k - 1].astype(jnp.float32)
                               + part_ref[a, c, r0:r0 + piece].astype(jnp.float32)).astype(send1.dtype)
                src = send1.at[d, k]
            cp = pltpu.make_async_remote_copy(
                src_ref=src, dst_ref=recv1.at[d, k],
                send_sem=s1_send.at[d, k], recv_sem=s1_recv.at[d, k],
                device_id=(peer, col), device_id_type=pl.DeviceIdType.MESH)
            cp.start()
            step_copies.append(cp)
        copies1.append(step_copies)
    for d, (peer, sign, a, r0) in enumerate(lanes):
        copies1[ny - 2][d].wait_recv()
        acc[a, r0:r0 + piece] = (recv1[d, ny - 2].astype(jnp.float32)
                                 + part_ref[a, y, r0:r0 + piece].astype(jnp.float32))

    lanes2 = [(x_up, 1, 0), (x_up, 1, quarter), (x_down, -1, 2 * quarter), (x_down, -1, 3 * quarter)]
    copies2 = []
    for k in range(nx - 1):
        step_copies = []
        for d, (peer, sign, r0) in enumerate(lanes2):
            c = (x - sign * (k + 1) + 2 * nx) % nx
            if k == 0:
                src = acc.at[c, r0:r0 + quarter]
            else:
                copies2[k - 1][d].wait_recv()
                send2[d, k] = recv2[d, k - 1] + acc[c, r0:r0 + quarter]
                src = send2.at[d, k]
            cp = pltpu.make_async_remote_copy(
                src_ref=src, dst_ref=recv2.at[d, k],
                send_sem=s2_send.at[d, k], recv_sem=s2_recv.at[d, k],
                device_id=(peer, col), device_id_type=pl.DeviceIdType.MESH)
            cp.start()
            step_copies.append(cp)
        copies2.append(step_copies)
    for d, (peer, sign, r0) in enumerate(lanes2):
        copies2[nx - 2][d].wait_recv()
        out_ref[r0:r0 + quarter] = (recv2[d, nx - 2] + acc[x, r0:r0 + quarter]).astype(out_ref.dtype)
    for step_copies in copies1 + copies2:
        for cp in step_copies:
            cp.wait_send()


def ring_reduce(part, nx, ny, splits=2):
    width = part.shape[-1]
    rows = part.shape[0] // (nx * ny)
    part = part.reshape(nx, ny, rows, width)
    n1 = nx * splits
    vmem = pltpu.MemorySpace.VMEM
    return pl.pallas_call(
        functools.partial(ring_reduce_kernel, nx, ny, splits),
        out_shape=jax.ShapeDtypeStruct((rows, width), jnp.bfloat16),
        in_specs=[pl.BlockSpec(memory_space=vmem)],
        out_specs=pl.BlockSpec(memory_space=vmem),
        scratch_shapes=[
            pltpu.VMEM((n1, ny - 1, rows // splits, width), jnp.bfloat16),
            pltpu.VMEM((n1, ny - 1, rows // splits, width), jnp.bfloat16),
            pltpu.VMEM((nx, rows, width), jnp.float32),
            pltpu.VMEM((4, nx - 1, rows // 4, width), jnp.float32),
            pltpu.VMEM((4, nx - 1, rows // 4, width), jnp.float32),
            pltpu.SemaphoreType.DMA((n1, ny - 1)),
            pltpu.SemaphoreType.DMA((n1, ny - 1)),
            pltpu.SemaphoreType.DMA((4, nx - 1)),
            pltpu.SemaphoreType.DMA((4, nx - 1)),
        ],
        compiler_params=pltpu.CompilerParams(
            collective_id=1, has_side_effects=True, vmem_limit_bytes=48 * 1024 * 1024
        ),
    )(part)


def shift_exchange_kernel(offsets, axis, other, block_ref, out_ref, send_sems, recv_sems):
    n = lax.axis_size(axis)
    me = lax.axis_index(axis)
    col = lax.axis_index(other)

    def dev(peer):
        return (peer, col) if axis == "seq" else (col, peer)

    targets = [(me + o + n * len(offsets)) % n for o in offsets]
    barrier = pltpu.get_barrier_semaphore()
    for peer in targets:
        pl.semaphore_signal(barrier, inc=1, device_id=dev(peer),
                            device_id_type=pl.DeviceIdType.MESH)
    pl.semaphore_wait(barrier, len(offsets))
    copies = []
    for j, peer in enumerate(targets):
        cp = pltpu.make_async_remote_copy(
            src_ref=block_ref, dst_ref=out_ref.at[j],
            send_sem=send_sems.at[j], recv_sem=recv_sems.at[j],
            device_id=dev(peer), device_id_type=pl.DeviceIdType.MESH)
        cp.start()
        copies.append(cp)
    for cp in copies:
        cp.wait()


def shift_exchange(block, offsets, axis, other, cid):
    vmem = pltpu.MemorySpace.VMEM
    k = len(offsets)
    return pl.pallas_call(
        functools.partial(shift_exchange_kernel, tuple(offsets), axis, other),
        out_shape=jax.ShapeDtypeStruct((k,) + block.shape, block.dtype),
        in_specs=[pl.BlockSpec(memory_space=vmem)],
        out_specs=pl.BlockSpec(memory_space=vmem),
        scratch_shapes=[pltpu.SemaphoreType.DMA((k,)), pltpu.SemaphoreType.DMA((k,))],
        compiler_params=pltpu.CompilerParams(collective_id=cid, has_side_effects=True),
    )(block)


def exp_all_to_all_kernel(x_ref, y_ref, send_sems, recv_sems):
    n = lax.axis_size("exp")
    me = lax.axis_index("exp")
    row = lax.axis_index("seq")
    barrier = pltpu.get_barrier_semaphore()
    for k in range(1, n):
        pl.semaphore_signal(barrier, inc=1, device_id=(row, (me + k) % n),
                            device_id_type=pl.DeviceIdType.MESH)
    pl.semaphore_wait(barrier, n - 1)
    copies = []
    for k in range(1, n):
        peer = (me + k) % n
        cp = pltpu.make_async_remote_copy(
            src_ref=x_ref.at[peer], dst_ref=y_ref.at[me],
            send_sem=send_sems.at[k - 1], recv_sem=recv_sems.at[k - 1],
            device_id=(row, peer), device_id_type=pl.DeviceIdType.MESH)
        cp.start()
        copies.append(cp)
    y_ref[me] = x_ref[me]
    for cp in copies:
        cp.wait()


def exp_all_to_all(x, cid):
    n = x.shape[0]
    vmem = pltpu.MemorySpace.VMEM
    return pl.pallas_call(
        exp_all_to_all_kernel,
        out_shape=jax.ShapeDtypeStruct(x.shape, x.dtype),
        in_specs=[pl.BlockSpec(memory_space=vmem)],
        out_specs=pl.BlockSpec(memory_space=vmem),
        scratch_shapes=[pltpu.SemaphoreType.DMA((n - 1,)), pltpu.SemaphoreType.DMA((n - 1,))],
        compiler_params=pltpu.CompilerParams(collective_id=cid, has_side_effects=True),
    )(x)


def ring_gather_kernel(nx, ny, axis, other, block_ref, out_ref, local_sem, send_sems, recv_sems):
    me = lax.axis_index(axis)
    col = lax.axis_index(other)
    x = me // ny
    y = me % ny
    rows = block_ref.shape[0]
    hr = rows // 2

    def dev(a, b):
        idx = (a + nx) % nx * ny + (b + ny) % ny
        return (idx, col) if axis == "seq" else (col, idx)

    peers = [dev(x, y + 1), dev(x, y - 1), dev(x + 1, y), dev(x - 1, y)]
    barrier = pltpu.get_barrier_semaphore()
    for peer in peers:
        pl.semaphore_signal(barrier, inc=1, device_id=peer, device_id_type=pl.DeviceIdType.MESH)
    pl.semaphore_wait(barrier, 4)

    own = pltpu.make_async_copy(block_ref, out_ref.at[x, y], local_sem.at[0])
    own.start()
    sem_count = [0]

    def unit(axis, stage, u, lo, hi):
        if axis == "y":
            return out_ref.at[x, u, lo:hi] if stage == 1 else out_ref.at[:, u, lo:hi]
        return out_ref.at[u, y, lo:hi] if stage == 1 else out_ref.at[u, :, lo:hi]

    def ring(axis, stage, lo, hi):
        n = ny if axis == "y" else nx
        c = y if axis == "y" else x
        half = n // 2
        mid = (lo + hi) // 2
        steps = []
        for sign in (1, -1):
            prev = None
            lane = []
            for k in range(half):
                u = (c - sign * k + 2 * n) % n
                a_lo, a_hi = lo, hi
                if k == half - 1 and n % 2 == 0:
                    a_lo, a_hi = (lo, mid) if sign == 1 else (mid, hi)
                if stage == 1 and k == 0:
                    src = block_ref.at[a_lo:a_hi]
                else:
                    src = unit(axis, stage, u, a_lo, a_hi)
                dst = unit(axis, stage, u, a_lo, a_hi)
                target = dev(x, y + sign) if axis == "y" else dev(x + sign, y)
                j = sem_count[0]
                sem_count[0] += 1
                cp = pltpu.make_async_remote_copy(
                    src_ref=src, dst_ref=dst, send_sem=send_sems.at[j], recv_sem=recv_sems.at[j],
                    device_id=target, device_id_type=pl.DeviceIdType.MESH)
                lane.append((prev, cp))
                prev = cp
            steps.append(lane)
        return steps

    plans = []
    for lo, hi, first, second in ((0, hr, "y", "x"), (hr, rows, "x", "y")):
        s1 = ring(first, 1, lo, hi)
        s2 = ring(second, 2, lo, hi)
        plans.append((s1, s2))

    started = []

    def run(lane_list):
        depth = max(len(l) for l in lane_list)
        for k in range(depth):
            for lane in lane_list:
                if k < len(lane):
                    prev, cp = lane[k]
                    if prev is not None:
                        prev.wait_recv()
                    cp.start()
                    started.append(cp)

    run([lane for s1, _ in plans for lane in s1])
    for s1, _ in plans:
        for lane in s1:
            lane[-1][1].wait_recv()
    own.wait()
    run([lane for _, s2 in plans for lane in s2])
    for _, s2 in plans:
        for lane in s2:
            lane[-1][1].wait_recv()
    for cp in started:
        cp.wait_send()


def ring_gather(block, nx, ny, axis="seq", other="exp", cid=3):
    vmem = pltpu.MemorySpace.VMEM
    n_sems = 4 * (nx // 2 + ny // 2) + 4
    return pl.pallas_call(
        functools.partial(ring_gather_kernel, nx, ny, axis, other),
        out_shape=jax.ShapeDtypeStruct((nx, ny) + block.shape, block.dtype),
        in_specs=[pl.BlockSpec(memory_space=vmem)],
        out_specs=pl.BlockSpec(memory_space=vmem),
        scratch_shapes=[
            pltpu.SemaphoreType.DMA((1,)),
            pltpu.SemaphoreType.DMA((n_sems,)),
            pltpu.SemaphoreType.DMA((n_sems,)),
        ],
        compiler_params=pltpu.CompilerParams(
            collective_id=cid, has_side_effects=True, vmem_limit_bytes=48 * 1024 * 1024
        ),
    )(block)


def rms_scale(matrix, gain):
    mean_square = jnp.mean(matrix * matrix, axis=-1, keepdims=True)
    return matrix * lax.rsqrt(mean_square + EPSILON) * gain


def expert_terms(block, gate_slice, up_slice, down_slice):
    gate = jnp.einsum("nek,ekf->nef", block, gate_slice, preferred_element_type=jnp.float32)
    upward = jnp.einsum("nek,ekf->nef", block, up_slice, preferred_element_type=jnp.float32)
    act = (jax.nn.silu(gate) * upward).astype(jnp.bfloat16)
    return jnp.einsum("nef,ekf->nek", act, down_slice, preferred_element_type=jnp.float32)


def local(
    tokens,
    array_type,
    block_pattern,
    gain_attn,
    w_query,
    w_key,
    w_value,
    logit_scale,
    w_out,
    gain_ffn,
    w_gate,
    w_up,
    w_down,
):
    n_exp = lax.axis_size("exp")
    row_count = tokens.shape[0]
    width = tokens.shape[1]
    head_cols = w_query.shape[1]
    heads_dev = logit_scale.shape[0]
    head_size = head_cols // heads_dev
    n_blocks = block_pattern.shape[0]
    inputs = tokens.astype(jnp.float32)
    normed_attn = rms_scale(inputs, gain_attn).astype(jnp.bfloat16)
    projector = jnp.concatenate([w_query, w_key, w_value], axis=1)
    joined_qkv = jnp.dot(
        ring_gather(normed_attn, n_exp // CORES, CORES, "exp", "seq", 4).reshape(n_exp * row_count, width),
        projector,
        preferred_element_type=jnp.float32,
    ).astype(jnp.bfloat16)
    block_len = joined_qkv.shape[0]
    query_heads = joined_qkv[:, :head_cols].reshape(block_len, heads_dev, head_size)
    key_value = joined_qkv[:, head_cols:]
    position = lax.axis_index("seq")
    head_scale = logit_scale[:, None, None]

    def attend(state, kv_block, source):
        row_top, weight_sum, numerator = state
        key_rows = kv_block[:, :head_cols].reshape(block_len, heads_dev, head_size)
        value_rows = kv_block[:, head_cols:].reshape(block_len, heads_dev, head_size)
        allowed = block_pattern[position, source] > 0
        scores = (
            jnp.einsum("qhd,khd->hqk", query_heads, key_rows, preferred_element_type=jnp.float32)
            * head_scale
        )
        block_top = jnp.max(scores, axis=2)
        new_top = jnp.where(allowed, jnp.maximum(row_top, block_top), row_top)
        shifted = jnp.minimum(scores - new_top[:, :, None], 0.0)
        weights = jnp.where(allowed, jnp.exp(shifted), 0.0)
        rescale = jnp.exp(row_top - new_top)
        weight_sum = weight_sum * rescale + jnp.sum(weights, axis=2)
        contrib = jnp.einsum(
            "hqk,khd->qhd",
            weights.astype(jnp.bfloat16),
            value_rows,
            preferred_element_type=jnp.float32,
        )
        numerator = numerator * jnp.transpose(rescale)[:, :, None] + contrib
        return (new_top, weight_sum, numerator)

    start_state = (
        jnp.full((heads_dev, block_len), -jnp.inf, jnp.float32),
        jnp.zeros((heads_dev, block_len), jnp.float32),
        jnp.zeros((block_len, heads_dev, head_size), jnp.float32),
    )
    state = attend(start_state, key_value, position)
    offsets = [d for d in range(1, REACH + 1)] + [-d for d in range(1, REACH + 1)]
    neighbours = shift_exchange(key_value, offsets, "seq", "exp", 2)
    for distance in range(1, REACH + 1):
        state = attend(state, neighbours[distance - 1], (position - distance) % n_blocks)
        state = attend(state, neighbours[REACH + distance - 1], (position + distance) % n_blocks)
    heads_out = (
        (state[2] / jnp.transpose(state[1])[:, :, None])
        .astype(jnp.bfloat16)
        .reshape(block_len, head_cols)
    )
    all_heads = lax.all_to_all(heads_out, "exp", split_axis=0, concat_axis=1, tiled=True)
    attn_out = jnp.dot(
        all_heads,
        lax.all_gather(w_out, "exp", axis=0, tiled=True),
        preferred_element_type=jnp.float32,
    )
    hidden_state = inputs + attn_out
    normed_ffn = rms_scale(hidden_state, gain_ffn).astype(jnp.bfloat16)
    experts_dev = w_gate.shape[0]
    n_total = experts_dev * n_exp
    capacity = 2 * row_count // n_total
    one_hot = (array_type[:, None] == jnp.arange(n_total, dtype=jnp.int32)[None, :]).astype(
        jnp.int32
    )
    slot_rank = jnp.sum(jnp.cumsum(one_hot, axis=0) * one_hot, axis=1) - 1
    owner = array_type // experts_dev
    local_expert = array_type % experts_dev
    slot_id = (owner * capacity + slot_rank) * experts_dev + local_expert
    n_slots = n_exp * capacity * experts_dev
    selector = (slot_id[None, :] == jnp.arange(n_slots, dtype=jnp.int32)[:, None]).astype(
        jnp.bfloat16
    )
    outgoing = jnp.dot(selector, normed_ffn, preferred_element_type=jnp.float32).astype(
        jnp.bfloat16
    )
    outgoing = outgoing.reshape(n_exp * capacity, experts_dev, width)
    arrived = lax.all_to_all(outgoing, "exp", split_axis=0, concat_axis=0, tiled=True)
    n_seq = lax.axis_size("seq")
    y_size = Y_RING if n_seq % Y_RING == 0 else n_seq
    gathered = ring_gather(
        arrived.reshape(arrived.shape[0], width), n_seq // y_size, y_size
    ).reshape((n_seq * arrived.shape[0],) + arrived.shape[1:])
    n_seq = lax.axis_size("seq")
    y_size = Y_RING if n_seq % Y_RING == 0 else n_seq
    partial = expert_terms(gathered, w_gate, w_up, w_down).astype(jnp.bfloat16)
    summed = ring_reduce(
        partial.reshape(partial.shape[0], width), n_seq // y_size, y_size
    ).reshape((-1,) + partial.shape[1:])
    returned = lax.all_to_all(summed, "exp", split_axis=0, concat_axis=0, tiled=True)
    expert_out = jnp.dot(
        jnp.transpose(selector),
        returned.reshape(n_slots, width),
        preferred_element_type=jnp.float32,
    )
    return (hidden_state + expert_out).astype(jnp.bfloat16)


def solution(mesh):
    return jax.shard_map(
        local,
        mesh=mesh,
        in_specs=(
            P(("seq", "exp"), None),
            P(("seq", "exp")),
            P(),
            P(),
            P(None, "exp"),
            P(None, "exp"),
            P(None, "exp"),
            P("exp"),
            P("exp", None),
            P(),
            P("exp", None, "seq"),
            P("exp", None, "seq"),
            P("exp", None, "seq"),
        ),
        out_specs=P(("seq", "exp"), None),
        check_vma=False,
    )
```

```python
import jax
import jax.numpy as jnp
from jax import lax
from jax.sharding import PartitionSpec as P
from jax.experimental import pallas as pl
from jax.experimental.pallas import tpu as pltpu
import functools

REACH = 3
Y_RING = 8
CORES = 2


EPSILON = 1e-05


def passed_along(block, axis, distance):
    devices = range(lax.axis_size(axis))
    route = [((i - distance) % len(devices), i) for i in devices]
    return lax.ppermute(block, axis, route)


def ring_reduce_kernel(nx, ny, splits, part_ref, out_ref, recv1, send1, acc, recv2, send2,
                       s1_send, s1_recv, s2_send, s2_recv):
    me = lax.axis_index("seq")
    col = lax.axis_index("exp")
    x = me // ny
    y = me % ny
    y_up = x * ny + (y + 1) % ny
    y_down = x * ny + (y + ny - 1) % ny
    x_up = ((x + 1) % nx) * ny + y
    x_down = ((x + nx - 1) % nx) * ny + y
    rows = part_ref.shape[2]
    piece = rows // splits
    quarter = rows // 4

    barrier = pltpu.get_barrier_semaphore()
    for peer in (y_up, y_down, x_up, x_down):
        pl.semaphore_signal(barrier, inc=1, device_id=(peer, col),
                            device_id_type=pl.DeviceIdType.MESH)
    pl.semaphore_wait(barrier, 4)

    lanes = []
    for a in range(nx):
        for p in range(splits):
            if a < nx // 2:
                lanes.append((y_up, 1, a, p * piece))
            else:
                lanes.append((y_down, -1, a, p * piece))
    copies1 = []
    for k in range(ny - 1):
        step_copies = []
        for d, (peer, sign, a, r0) in enumerate(lanes):
            c = (y - sign * (k + 1) + 2 * ny) % ny
            if k == 0:
                src = part_ref.at[a, c, r0:r0 + piece]
            else:
                copies1[k - 1][d].wait_recv()
                send1[d, k] = (recv1[d, k - 1].astype(jnp.float32)
                               + part_ref[a, c, r0:r0 + piece].astype(jnp.float32)).astype(send1.dtype)
                src = send1.at[d, k]
            cp = pltpu.make_async_remote_copy(
                src_ref=src, dst_ref=recv1.at[d, k],
                send_sem=s1_send.at[d, k], recv_sem=s1_recv.at[d, k],
                device_id=(peer, col), device_id_type=pl.DeviceIdType.MESH)
            cp.start()
            step_copies.append(cp)
        copies1.append(step_copies)
    for d, (peer, sign, a, r0) in enumerate(lanes):
        copies1[ny - 2][d].wait_recv()
        acc[a, r0:r0 + piece] = (recv1[d, ny - 2].astype(jnp.float32)
                                 + part_ref[a, y, r0:r0 + piece].astype(jnp.float32))

    lanes2 = [(x_up, 1, 0), (x_up, 1, quarter), (x_down, -1, 2 * quarter), (x_down, -1, 3 * quarter)]
    copies2 = []
    for k in range(nx - 1):
        step_copies = []
        for d, (peer, sign, r0) in enumerate(lanes2):
            c = (x - sign * (k + 1) + 2 * nx) % nx
            if k == 0:
                src = acc.at[c, r0:r0 + quarter]
            else:
                copies2[k - 1][d].wait_recv()
                send2[d, k] = recv2[d, k - 1] + acc[c, r0:r0 + quarter]
                src = send2.at[d, k]
            cp = pltpu.make_async_remote_copy(
                src_ref=src, dst_ref=recv2.at[d, k],
                send_sem=s2_send.at[d, k], recv_sem=s2_recv.at[d, k],
                device_id=(peer, col), device_id_type=pl.DeviceIdType.MESH)
            cp.start()
            step_copies.append(cp)
        copies2.append(step_copies)
    for d, (peer, sign, r0) in enumerate(lanes2):
        copies2[nx - 2][d].wait_recv()
        out_ref[r0:r0 + quarter] = (recv2[d, nx - 2] + acc[x, r0:r0 + quarter]).astype(out_ref.dtype)
    for step_copies in copies1 + copies2:
        for cp in step_copies:
            cp.wait_send()


def ring_reduce(part, nx, ny, splits=2):
    width = part.shape[-1]
    rows = part.shape[0] // (nx * ny)
    part = part.reshape(nx, ny, rows, width)
    n1 = nx * splits
    vmem = pltpu.MemorySpace.VMEM
    return pl.pallas_call(
        functools.partial(ring_reduce_kernel, nx, ny, splits),
        out_shape=jax.ShapeDtypeStruct((rows, width), jnp.bfloat16),
        in_specs=[pl.BlockSpec(memory_space=vmem)],
        out_specs=pl.BlockSpec(memory_space=vmem),
        scratch_shapes=[
            pltpu.VMEM((n1, ny - 1, rows // splits, width), jnp.bfloat16),
            pltpu.VMEM((n1, ny - 1, rows // splits, width), jnp.bfloat16),
            pltpu.VMEM((nx, rows, width), jnp.float32),
            pltpu.VMEM((4, nx - 1, rows // 4, width), jnp.float32),
            pltpu.VMEM((4, nx - 1, rows // 4, width), jnp.float32),
            pltpu.SemaphoreType.DMA((n1, ny - 1)),
            pltpu.SemaphoreType.DMA((n1, ny - 1)),
            pltpu.SemaphoreType.DMA((4, nx - 1)),
            pltpu.SemaphoreType.DMA((4, nx - 1)),
        ],
        compiler_params=pltpu.CompilerParams(
            collective_id=1, has_side_effects=True, vmem_limit_bytes=48 * 1024 * 1024
        ),
    )(part)


def shift_exchange_kernel(offsets, axis, other, block_ref, out_ref, send_sems, recv_sems):
    n = lax.axis_size(axis)
    me = lax.axis_index(axis)
    col = lax.axis_index(other)

    def dev(peer):
        return (peer, col) if axis == "seq" else (col, peer)

    targets = [(me + o + n * len(offsets)) % n for o in offsets]
    barrier = pltpu.get_barrier_semaphore()
    for peer in targets:
        pl.semaphore_signal(barrier, inc=1, device_id=dev(peer),
                            device_id_type=pl.DeviceIdType.MESH)
    pl.semaphore_wait(barrier, len(offsets))
    copies = []
    for j, peer in enumerate(targets):
        cp = pltpu.make_async_remote_copy(
            src_ref=block_ref, dst_ref=out_ref.at[j],
            send_sem=send_sems.at[j], recv_sem=recv_sems.at[j],
            device_id=dev(peer), device_id_type=pl.DeviceIdType.MESH)
        cp.start()
        copies.append(cp)
    for cp in copies:
        cp.wait()


def shift_exchange(block, offsets, axis, other, cid):
    vmem = pltpu.MemorySpace.VMEM
    k = len(offsets)
    return pl.pallas_call(
        functools.partial(shift_exchange_kernel, tuple(offsets), axis, other),
        out_shape=jax.ShapeDtypeStruct((k,) + block.shape, block.dtype),
        in_specs=[pl.BlockSpec(memory_space=vmem)],
        out_specs=pl.BlockSpec(memory_space=vmem),
        scratch_shapes=[pltpu.SemaphoreType.DMA((k,)), pltpu.SemaphoreType.DMA((k,))],
        compiler_params=pltpu.CompilerParams(collective_id=cid, has_side_effects=True),
    )(block)


def exp_all_to_all_kernel(x_ref, y_ref, send_sems, recv_sems):
    n = lax.axis_size("exp")
    me = lax.axis_index("exp")
    row = lax.axis_index("seq")
    barrier = pltpu.get_barrier_semaphore()
    for k in range(1, n):
        pl.semaphore_signal(barrier, inc=1, device_id=(row, (me + k) % n),
                            device_id_type=pl.DeviceIdType.MESH)
    pl.semaphore_wait(barrier, n - 1)
    copies = []
    for k in range(1, n):
        peer = (me + k) % n
        cp = pltpu.make_async_remote_copy(
            src_ref=x_ref.at[peer], dst_ref=y_ref.at[me],
            send_sem=send_sems.at[k - 1], recv_sem=recv_sems.at[k - 1],
            device_id=(row, peer), device_id_type=pl.DeviceIdType.MESH)
        cp.start()
        copies.append(cp)
    y_ref[me] = x_ref[me]
    for cp in copies:
        cp.wait()


def exp_all_to_all(x, cid):
    n = x.shape[0]
    vmem = pltpu.MemorySpace.VMEM
    return pl.pallas_call(
        exp_all_to_all_kernel,
        out_shape=jax.ShapeDtypeStruct(x.shape, x.dtype),
        in_specs=[pl.BlockSpec(memory_space=vmem)],
        out_specs=pl.BlockSpec(memory_space=vmem),
        scratch_shapes=[pltpu.SemaphoreType.DMA((n - 1,)), pltpu.SemaphoreType.DMA((n - 1,))],
        compiler_params=pltpu.CompilerParams(collective_id=cid, has_side_effects=True),
    )(x)


def ring_gather_kernel(nx, ny, axis, other, pieces, block_ref, out_ref, local_sem, send_sems, recv_sems):
    me = lax.axis_index(axis)
    col = lax.axis_index(other)
    x = me // ny
    y = me % ny
    rows = block_ref.shape[0]
    hr = rows // 2

    def dev(a, b):
        idx = (a + nx) % nx * ny + (b + ny) % ny
        return (idx, col) if axis == "seq" else (col, idx)

    peers = [dev(x, y + 1), dev(x, y - 1), dev(x + 1, y), dev(x - 1, y)]
    barrier = pltpu.get_barrier_semaphore()
    for peer in peers:
        pl.semaphore_signal(barrier, inc=1, device_id=peer, device_id_type=pl.DeviceIdType.MESH)
    pl.semaphore_wait(barrier, 4)

    own = pltpu.make_async_copy(block_ref, out_ref.at[x, y], local_sem.at[0])
    own.start()
    sem_count = [0]

    def unit(axis, stage, u, lo, hi):
        if axis == "y":
            return out_ref.at[x, u, lo:hi] if stage == 1 else out_ref.at[:, u, lo:hi]
        return out_ref.at[u, y, lo:hi] if stage == 1 else out_ref.at[u, :, lo:hi]

    def ring(axis, stage, lo, hi):
        n = ny if axis == "y" else nx
        c = y if axis == "y" else x
        half = n // 2
        mid = (lo + hi) // 2
        steps = []
        for sign in (1, -1):
            prev = None
            lane = []
            for k in range(half):
                u = (c - sign * k + 2 * n) % n
                a_lo, a_hi = lo, hi
                if k == half - 1 and n % 2 == 0:
                    a_lo, a_hi = (lo, mid) if sign == 1 else (mid, hi)
                if stage == 1 and k == 0:
                    src = block_ref.at[a_lo:a_hi]
                else:
                    src = unit(axis, stage, u, a_lo, a_hi)
                dst = unit(axis, stage, u, a_lo, a_hi)
                target = dev(x, y + sign) if axis == "y" else dev(x + sign, y)
                j = sem_count[0]
                sem_count[0] += 1
                cp = pltpu.make_async_remote_copy(
                    src_ref=src, dst_ref=dst, send_sem=send_sems.at[j], recv_sem=recv_sems.at[j],
                    device_id=target, device_id_type=pl.DeviceIdType.MESH)
                lane.append((prev, cp))
                prev = cp
            steps.append(lane)
        return steps

    plans = []
    step = hr // pieces
    for p in range(pieces):
        for base, first, second in ((0, "y", "x"), (hr, "x", "y")):
            lo = base + p * step
            s1 = ring(first, 1, lo, lo + step)
            s2 = ring(second, 2, lo, lo + step)
            plans.append((s1, s2))

    started = []

    def run(lane_list):
        depth = max(len(l) for l in lane_list)
        for k in range(depth):
            for lane in lane_list:
                if k < len(lane):
                    prev, cp = lane[k]
                    if prev is not None:
                        prev.wait_recv()
                    cp.start()
                    started.append(cp)

    run([lane for s1, _ in plans for lane in s1])
    for s1, _ in plans:
        for lane in s1:
            lane[-1][1].wait_recv()
    own.wait()
    run([lane for _, s2 in plans for lane in s2])
    for _, s2 in plans:
        for lane in s2:
            lane[-1][1].wait_recv()
    for cp in started:
        cp.wait_send()


def ring_gather(block, nx, ny, axis="seq", other="exp", cid=3, pieces=1):
    vmem = pltpu.MemorySpace.VMEM
    n_sems = 4 * pieces * (nx // 2 + ny // 2) + 4
    return pl.pallas_call(
        functools.partial(ring_gather_kernel, nx, ny, axis, other, pieces),
        out_shape=jax.ShapeDtypeStruct((nx, ny) + block.shape, block.dtype),
        in_specs=[pl.BlockSpec(memory_space=vmem)],
        out_specs=pl.BlockSpec(memory_space=vmem),
        scratch_shapes=[
            pltpu.SemaphoreType.DMA((1,)),
            pltpu.SemaphoreType.DMA((n_sems,)),
            pltpu.SemaphoreType.DMA((n_sems,)),
        ],
        compiler_params=pltpu.CompilerParams(
            collective_id=cid, has_side_effects=True, vmem_limit_bytes=48 * 1024 * 1024
        ),
    )(block)


def rms_scale(matrix, gain):
    mean_square = jnp.mean(matrix * matrix, axis=-1, keepdims=True)
    return matrix * lax.rsqrt(mean_square + EPSILON) * gain


def expert_terms(block, gate_slice, up_slice, down_slice):
    gate = jnp.einsum("nek,ekf->nef", block, gate_slice, preferred_element_type=jnp.float32)
    upward = jnp.einsum("nek,ekf->nef", block, up_slice, preferred_element_type=jnp.float32)
    act = (jax.nn.silu(gate) * upward).astype(jnp.bfloat16)
    return jnp.einsum("nef,ekf->nek", act, down_slice, preferred_element_type=jnp.float32)


def local(
    tokens,
    array_type,
    block_pattern,
    gain_attn,
    w_query,
    w_key,
    w_value,
    logit_scale,
    w_out,
    gain_ffn,
    w_gate,
    w_up,
    w_down,
):
    n_exp = lax.axis_size("exp")
    row_count = tokens.shape[0]
    width = tokens.shape[1]
    head_cols = w_query.shape[1]
    heads_dev = logit_scale.shape[0]
    head_size = head_cols // heads_dev
    n_blocks = block_pattern.shape[0]
    inputs = tokens.astype(jnp.float32)
    normed_attn = rms_scale(inputs, gain_attn).astype(jnp.bfloat16)
    projector = jnp.concatenate([w_query, w_key, w_value], axis=1)
    joined_qkv = jnp.dot(
        ring_gather(normed_attn, n_exp // CORES, CORES, "exp", "seq", 4).reshape(n_exp * row_count, width),
        projector,
        preferred_element_type=jnp.float32,
    ).astype(jnp.bfloat16)
    block_len = joined_qkv.shape[0]
    query_heads = joined_qkv[:, :head_cols].reshape(block_len, heads_dev, head_size)
    key_value = joined_qkv[:, head_cols:]
    position = lax.axis_index("seq")
    head_scale = logit_scale[:, None, None]

    def attend(state, kv_block, source):
        row_top, weight_sum, numerator = state
        key_rows = kv_block[:, :head_cols].reshape(block_len, heads_dev, head_size)
        value_rows = kv_block[:, head_cols:].reshape(block_len, heads_dev, head_size)
        allowed = block_pattern[position, source] > 0
        scores = (
            jnp.einsum("qhd,khd->hqk", query_heads, key_rows, preferred_element_type=jnp.float32)
            * head_scale
        )
        block_top = jnp.max(scores, axis=2)
        new_top = jnp.where(allowed, jnp.maximum(row_top, block_top), row_top)
        shifted = jnp.minimum(scores - new_top[:, :, None], 0.0)
        weights = jnp.where(allowed, jnp.exp(shifted), 0.0)
        rescale = jnp.exp(row_top - new_top)
        weight_sum = weight_sum * rescale + jnp.sum(weights, axis=2)
        contrib = jnp.einsum(
            "hqk,khd->qhd",
            weights.astype(jnp.bfloat16),
            value_rows,
            preferred_element_type=jnp.float32,
        )
        numerator = numerator * jnp.transpose(rescale)[:, :, None] + contrib
        return (new_top, weight_sum, numerator)

    start_state = (
        jnp.full((heads_dev, block_len), -jnp.inf, jnp.float32),
        jnp.zeros((heads_dev, block_len), jnp.float32),
        jnp.zeros((block_len, heads_dev, head_size), jnp.float32),
    )
    state = attend(start_state, key_value, position)
    offsets = [d for d in range(1, REACH + 1)] + [-d for d in range(1, REACH + 1)]
    neighbours = shift_exchange(key_value, offsets, "seq", "exp", 2)
    for distance in range(1, REACH + 1):
        state = attend(state, neighbours[distance - 1], (position - distance) % n_blocks)
        state = attend(state, neighbours[REACH + distance - 1], (position + distance) % n_blocks)
    heads_out = (
        (state[2] / jnp.transpose(state[1])[:, :, None])
        .astype(jnp.bfloat16)
        .reshape(block_len, head_cols)
    )
    all_heads = lax.all_to_all(heads_out, "exp", split_axis=0, concat_axis=1, tiled=True)
    attn_out = jnp.dot(
        all_heads,
        lax.all_gather(w_out, "exp", axis=0, tiled=True),
        preferred_element_type=jnp.float32,
    )
    hidden_state = inputs + attn_out
    normed_ffn = rms_scale(hidden_state, gain_ffn).astype(jnp.bfloat16)
    experts_dev = w_gate.shape[0]
    n_total = experts_dev * n_exp
    capacity = 2 * row_count // n_total
    one_hot = (array_type[:, None] == jnp.arange(n_total, dtype=jnp.int32)[None, :]).astype(
        jnp.int32
    )
    slot_rank = jnp.sum(jnp.cumsum(one_hot, axis=0) * one_hot, axis=1) - 1
    owner = array_type // experts_dev
    local_expert = array_type % experts_dev
    slot_id = (owner * capacity + slot_rank) * experts_dev + local_expert
    n_slots = n_exp * capacity * experts_dev
    selector = (slot_id[None, :] == jnp.arange(n_slots, dtype=jnp.int32)[:, None]).astype(
        jnp.bfloat16
    )
    outgoing = jnp.dot(selector, normed_ffn, preferred_element_type=jnp.float32).astype(
        jnp.bfloat16
    )
    outgoing = outgoing.reshape(n_exp * capacity, experts_dev, width)
    arrived = lax.all_to_all(outgoing, "exp", split_axis=0, concat_axis=0, tiled=True)
    n_seq = lax.axis_size("seq")
    y_size = Y_RING if n_seq % Y_RING == 0 else n_seq
    gathered = ring_gather(
        arrived.reshape(arrived.shape[0], width), n_seq // y_size, y_size, pieces=2
    ).reshape((n_seq * arrived.shape[0],) + arrived.shape[1:])
    n_seq = lax.axis_size("seq")
    y_size = Y_RING if n_seq % Y_RING == 0 else n_seq
    partial = expert_terms(gathered, w_gate, w_up, w_down).astype(jnp.bfloat16)
    summed = ring_reduce(
        partial.reshape(partial.shape[0], width), n_seq // y_size, y_size
    ).reshape((-1,) + partial.shape[1:])
    returned = lax.all_to_all(summed, "exp", split_axis=0, concat_axis=0, tiled=True)
    expert_out = jnp.dot(
        jnp.transpose(selector),
        returned.reshape(n_slots, width),
        preferred_element_type=jnp.float32,
    )
    return (hidden_state + expert_out).astype(jnp.bfloat16)


def solution(mesh):
    return jax.shard_map(
        local,
        mesh=mesh,
        in_specs=(
            P(("seq", "exp"), None),
            P(("seq", "exp")),
            P(),
            P(),
            P(None, "exp"),
            P(None, "exp"),
            P(None, "exp"),
            P("exp"),
            P("exp", None),
            P(),
            P("exp", None, "seq"),
            P("exp", None, "seq"),
            P("exp", None, "seq"),
        ),
        out_specs=P(("seq", "exp"), None),
        check_vma=False,
    )
```

```python
import jax
import jax.numpy as jnp
from jax import lax
from jax.sharding import PartitionSpec as P
from jax.experimental import pallas as pl
from jax.experimental.pallas import tpu as pltpu
import functools

REACH = 3
Y_RING = 8
CORES = 2


EPSILON = 1e-05


def passed_along(block, axis, distance):
    devices = range(lax.axis_size(axis))
    route = [((i - distance) % len(devices), i) for i in devices]
    return lax.ppermute(block, axis, route)


def ring_reduce_kernel(nx, ny, splits, part_ref, out_ref, recv1, send1, acc, recv2, send2,
                       s1_send, s1_recv, s2_send, s2_recv):
    me = lax.axis_index("seq")
    col = lax.axis_index("exp")
    x = me // ny
    y = me % ny
    y_up = x * ny + (y + 1) % ny
    y_down = x * ny + (y + ny - 1) % ny
    x_up = ((x + 1) % nx) * ny + y
    x_down = ((x + nx - 1) % nx) * ny + y
    rows = part_ref.shape[2]
    piece = rows // splits
    quarter = rows // 4

    barrier = pltpu.get_barrier_semaphore()
    for peer in (y_up, y_down, x_up, x_down):
        pl.semaphore_signal(barrier, inc=1, device_id=(peer, col),
                            device_id_type=pl.DeviceIdType.MESH)
    pl.semaphore_wait(barrier, 4)

    lanes = []
    for a in range(nx):
        for p in range(splits):
            if a < nx // 2:
                lanes.append((y_up, 1, a, p * piece))
            else:
                lanes.append((y_down, -1, a, p * piece))
    copies1 = []
    for k in range(ny - 1):
        step_copies = []
        for d, (peer, sign, a, r0) in enumerate(lanes):
            c = (y - sign * (k + 1) + 2 * ny) % ny
            if k == 0:
                src = part_ref.at[a, c, r0:r0 + piece]
            else:
                copies1[k - 1][d].wait_recv()
                send1[d, k] = (recv1[d, k - 1].astype(jnp.float32)
                               + part_ref[a, c, r0:r0 + piece].astype(jnp.float32)).astype(send1.dtype)
                src = send1.at[d, k]
            cp = pltpu.make_async_remote_copy(
                src_ref=src, dst_ref=recv1.at[d, k],
                send_sem=s1_send.at[d, k], recv_sem=s1_recv.at[d, k],
                device_id=(peer, col), device_id_type=pl.DeviceIdType.MESH)
            cp.start()
            step_copies.append(cp)
        copies1.append(step_copies)
    for d, (peer, sign, a, r0) in enumerate(lanes):
        copies1[ny - 2][d].wait_recv()
        acc[a, r0:r0 + piece] = (recv1[d, ny - 2].astype(jnp.float32)
                                 + part_ref[a, y, r0:r0 + piece].astype(jnp.float32))

    lanes2 = [(x_up, 1, 0), (x_up, 1, quarter), (x_down, -1, 2 * quarter), (x_down, -1, 3 * quarter)]
    copies2 = []
    for k in range(nx - 1):
        step_copies = []
        for d, (peer, sign, r0) in enumerate(lanes2):
            c = (x - sign * (k + 1) + 2 * nx) % nx
            if k == 0:
                src = acc.at[c, r0:r0 + quarter]
            else:
                copies2[k - 1][d].wait_recv()
                send2[d, k] = recv2[d, k - 1] + acc[c, r0:r0 + quarter]
                src = send2.at[d, k]
            cp = pltpu.make_async_remote_copy(
                src_ref=src, dst_ref=recv2.at[d, k],
                send_sem=s2_send.at[d, k], recv_sem=s2_recv.at[d, k],
                device_id=(peer, col), device_id_type=pl.DeviceIdType.MESH)
            cp.start()
            step_copies.append(cp)
        copies2.append(step_copies)
    for d, (peer, sign, r0) in enumerate(lanes2):
        copies2[nx - 2][d].wait_recv()
        out_ref[r0:r0 + quarter] = (recv2[d, nx - 2] + acc[x, r0:r0 + quarter]).astype(out_ref.dtype)
    for step_copies in copies1 + copies2:
        for cp in step_copies:
            cp.wait_send()


def ring_reduce(part, nx, ny, splits=2):
    width = part.shape[-1]
    rows = part.shape[0] // (nx * ny)
    part = part.reshape(nx, ny, rows, width)
    n1 = nx * splits
    vmem = pltpu.MemorySpace.VMEM
    return pl.pallas_call(
        functools.partial(ring_reduce_kernel, nx, ny, splits),
        out_shape=jax.ShapeDtypeStruct((rows, width), jnp.bfloat16),
        in_specs=[pl.BlockSpec(memory_space=vmem)],
        out_specs=pl.BlockSpec(memory_space=vmem),
        scratch_shapes=[
            pltpu.VMEM((n1, ny - 1, rows // splits, width), jnp.bfloat16),
            pltpu.VMEM((n1, ny - 1, rows // splits, width), jnp.bfloat16),
            pltpu.VMEM((nx, rows, width), jnp.float32),
            pltpu.VMEM((4, nx - 1, rows // 4, width), jnp.float32),
            pltpu.VMEM((4, nx - 1, rows // 4, width), jnp.float32),
            pltpu.SemaphoreType.DMA((n1, ny - 1)),
            pltpu.SemaphoreType.DMA((n1, ny - 1)),
            pltpu.SemaphoreType.DMA((4, nx - 1)),
            pltpu.SemaphoreType.DMA((4, nx - 1)),
        ],
        compiler_params=pltpu.CompilerParams(
            collective_id=1, has_side_effects=True, vmem_limit_bytes=48 * 1024 * 1024
        ),
    )(part)


def ring_ffn_kernel(nx, ny, splits, tok_ref, wg_ref, wu_ref, wd_ref, out_ref, pbuf, recv1, send1,
                    acc, recv2, send2, s1_send, s1_recv, s2_send, s2_recv):
    me = lax.axis_index("seq")
    col = lax.axis_index("exp")
    x = me // ny
    y = me % ny
    y_up = x * ny + (y + 1) % ny
    y_down = x * ny + (y + ny - 1) % ny
    x_up = ((x + 1) % nx) * ny + y
    x_down = ((x + nx - 1) % nx) * ny + y
    rows = tok_ref.shape[2]
    width = tok_ref.shape[3]
    piece = rows // splits
    quarter = rows // 4
    half_x = nx // 2

    def partials(c_up, c_down):
        tok = jnp.concatenate(
            [tok_ref[0:half_x, c_up].reshape(half_x * rows, width),
             tok_ref[half_x:nx, c_down].reshape((nx - half_x) * rows, width)], axis=0)
        gate = jnp.dot(tok, wg_ref[...], preferred_element_type=jnp.float32)
        upward = jnp.dot(tok, wu_ref[...], preferred_element_type=jnp.float32)
        act = (gate / (1.0 + jnp.exp(-gate)) * upward).astype(jnp.bfloat16)
        down = lax.dot_general(act, wd_ref[...], (((1,), (1,)), ((), ())),
                               preferred_element_type=jnp.float32)
        pbuf[...] = down.astype(jnp.bfloat16).reshape(nx, rows, width)

    barrier = pltpu.get_barrier_semaphore()
    for peer in (y_up, y_down, x_up, x_down):
        pl.semaphore_signal(barrier, inc=1, device_id=(peer, col),
                            device_id_type=pl.DeviceIdType.MESH)
    pl.semaphore_wait(barrier, 4)

    lanes = []
    for a in range(nx):
        for p in range(splits):
            if a < half_x:
                lanes.append((y_up, 1, a, p * piece))
            else:
                lanes.append((y_down, -1, a, p * piece))
    copies1 = []
    for k in range(ny - 1):
        partials((y - k - 1 + ny) % ny, (y + k + 1) % ny)
        step_copies = []
        for d, (peer, sign, a, r0) in enumerate(lanes):
            if k == 0:
                send1[d, k] = pbuf[a, r0:r0 + piece]
            else:
                copies1[k - 1][d].wait_recv()
                send1[d, k] = (recv1[d, k - 1].astype(jnp.float32)
                               + pbuf[a, r0:r0 + piece].astype(jnp.float32)).astype(send1.dtype)
            cp = pltpu.make_async_remote_copy(
                src_ref=send1.at[d, k], dst_ref=recv1.at[d, k],
                send_sem=s1_send.at[d, k], recv_sem=s1_recv.at[d, k],
                device_id=(peer, col), device_id_type=pl.DeviceIdType.MESH)
            cp.start()
            step_copies.append(cp)
        copies1.append(step_copies)
    partials(y, y)
    for d, (peer, sign, a, r0) in enumerate(lanes):
        copies1[ny - 2][d].wait_recv()
        acc[a, r0:r0 + piece] = (recv1[d, ny - 2].astype(jnp.float32)
                                 + pbuf[a, r0:r0 + piece].astype(jnp.float32))

    lanes2 = [(x_up, 1, 0), (x_up, 1, quarter), (x_down, -1, 2 * quarter), (x_down, -1, 3 * quarter)]
    copies2 = []
    for k in range(nx - 1):
        step_copies = []
        for d, (peer, sign, r0) in enumerate(lanes2):
            c = (x - sign * (k + 1) + 2 * nx) % nx
            if k == 0:
                src = acc.at[c, r0:r0 + quarter]
            else:
                copies2[k - 1][d].wait_recv()
                send2[d, k] = recv2[d, k - 1] + acc[c, r0:r0 + quarter]
                src = send2.at[d, k]
            cp = pltpu.make_async_remote_copy(
                src_ref=src, dst_ref=recv2.at[d, k],
                send_sem=s2_send.at[d, k], recv_sem=s2_recv.at[d, k],
                device_id=(peer, col), device_id_type=pl.DeviceIdType.MESH)
            cp.start()
            step_copies.append(cp)
        copies2.append(step_copies)
    for d, (peer, sign, r0) in enumerate(lanes2):
        copies2[nx - 2][d].wait_recv()
        out_ref[r0:r0 + quarter] = (recv2[d, nx - 2] + acc[x, r0:r0 + quarter]).astype(out_ref.dtype)
    for step_copies in copies1 + copies2:
        for cp in step_copies:
            cp.wait_send()


def ring_ffn(tokens, w_gate, w_up, w_down, nx, ny, splits=2):
    width = tokens.shape[-1]
    rows = tokens.shape[0] // (nx * ny)
    tokens = tokens.reshape(nx, ny, rows, width)
    n1 = nx * splits
    vmem = pltpu.MemorySpace.VMEM
    return pl.pallas_call(
        functools.partial(ring_ffn_kernel, nx, ny, splits),
        out_shape=jax.ShapeDtypeStruct((rows, width), jnp.bfloat16),
        in_specs=[pl.BlockSpec(memory_space=vmem)] * 4,
        out_specs=pl.BlockSpec(memory_space=vmem),
        scratch_shapes=[
            pltpu.VMEM((nx, rows, width), jnp.bfloat16),
            pltpu.VMEM((n1, ny - 1, rows // splits, width), jnp.bfloat16),
            pltpu.VMEM((n1, ny - 1, rows // splits, width), jnp.bfloat16),
            pltpu.VMEM((nx, rows, width), jnp.float32),
            pltpu.VMEM((4, nx - 1, rows // 4, width), jnp.float32),
            pltpu.VMEM((4, nx - 1, rows // 4, width), jnp.float32),
            pltpu.SemaphoreType.DMA((n1, ny - 1)),
            pltpu.SemaphoreType.DMA((n1, ny - 1)),
            pltpu.SemaphoreType.DMA((4, nx - 1)),
            pltpu.SemaphoreType.DMA((4, nx - 1)),
        ],
        compiler_params=pltpu.CompilerParams(
            collective_id=5, has_side_effects=True, vmem_limit_bytes=56 * 1024 * 1024
        ),
    )(tokens, w_gate, w_up, w_down)


def shift_exchange_kernel(offsets, axis, other, block_ref, out_ref, send_sems, recv_sems):
    n = lax.axis_size(axis)
    me = lax.axis_index(axis)
    col = lax.axis_index(other)

    def dev(peer):
        return (peer, col) if axis == "seq" else (col, peer)

    targets = [(me + o + n * len(offsets)) % n for o in offsets]
    barrier = pltpu.get_barrier_semaphore()
    for peer in targets:
        pl.semaphore_signal(barrier, inc=1, device_id=dev(peer),
                            device_id_type=pl.DeviceIdType.MESH)
    pl.semaphore_wait(barrier, len(offsets))
    copies = []
    for j, peer in enumerate(targets):
        cp = pltpu.make_async_remote_copy(
            src_ref=block_ref, dst_ref=out_ref.at[j],
            send_sem=send_sems.at[j], recv_sem=recv_sems.at[j],
            device_id=dev(peer), device_id_type=pl.DeviceIdType.MESH)
        cp.start()
        copies.append(cp)
    for cp in copies:
        cp.wait()


def shift_exchange(block, offsets, axis, other, cid):
    vmem = pltpu.MemorySpace.VMEM
    k = len(offsets)
    return pl.pallas_call(
        functools.partial(shift_exchange_kernel, tuple(offsets), axis, other),
        out_shape=jax.ShapeDtypeStruct((k,) + block.shape, block.dtype),
        in_specs=[pl.BlockSpec(memory_space=vmem)],
        out_specs=pl.BlockSpec(memory_space=vmem),
        scratch_shapes=[pltpu.SemaphoreType.DMA((k,)), pltpu.SemaphoreType.DMA((k,))],
        compiler_params=pltpu.CompilerParams(collective_id=cid, has_side_effects=True),
    )(block)


def exp_all_to_all_kernel(x_ref, y_ref, send_sems, recv_sems):
    n = lax.axis_size("exp")
    me = lax.axis_index("exp")
    row = lax.axis_index("seq")
    barrier = pltpu.get_barrier_semaphore()
    for k in range(1, n):
        pl.semaphore_signal(barrier, inc=1, device_id=(row, (me + k) % n),
                            device_id_type=pl.DeviceIdType.MESH)
    pl.semaphore_wait(barrier, n - 1)
    copies = []
    for k in range(1, n):
        peer = (me + k) % n
        cp = pltpu.make_async_remote_copy(
            src_ref=x_ref.at[peer], dst_ref=y_ref.at[me],
            send_sem=send_sems.at[k - 1], recv_sem=recv_sems.at[k - 1],
            device_id=(row, peer), device_id_type=pl.DeviceIdType.MESH)
        cp.start()
        copies.append(cp)
    y_ref[me] = x_ref[me]
    for cp in copies:
        cp.wait()


def exp_all_to_all(x, cid):
    n = x.shape[0]
    vmem = pltpu.MemorySpace.VMEM
    return pl.pallas_call(
        exp_all_to_all_kernel,
        out_shape=jax.ShapeDtypeStruct(x.shape, x.dtype),
        in_specs=[pl.BlockSpec(memory_space=vmem)],
        out_specs=pl.BlockSpec(memory_space=vmem),
        scratch_shapes=[pltpu.SemaphoreType.DMA((n - 1,)), pltpu.SemaphoreType.DMA((n - 1,))],
        compiler_params=pltpu.CompilerParams(collective_id=cid, has_side_effects=True),
    )(x)


def ring_gather_kernel(nx, ny, axis, other, pieces, block_ref, out_ref, local_sem, send_sems, recv_sems):
    me = lax.axis_index(axis)
    col = lax.axis_index(other)
    x = me // ny
    y = me % ny
    rows = block_ref.shape[0]
    hr = rows // 2

    def dev(a, b):
        idx = (a + nx) % nx * ny + (b + ny) % ny
        return (idx, col) if axis == "seq" else (col, idx)

    peers = [dev(x, y + 1), dev(x, y - 1), dev(x + 1, y), dev(x - 1, y)]
    barrier = pltpu.get_barrier_semaphore()
    for peer in peers:
        pl.semaphore_signal(barrier, inc=1, device_id=peer, device_id_type=pl.DeviceIdType.MESH)
    pl.semaphore_wait(barrier, 4)

    own = pltpu.make_async_copy(block_ref, out_ref.at[x, y], local_sem.at[0])
    own.start()
    sem_count = [0]

    def unit(axis, stage, u, lo, hi):
        if axis == "y":
            return out_ref.at[x, u, lo:hi] if stage == 1 else out_ref.at[:, u, lo:hi]
        return out_ref.at[u, y, lo:hi] if stage == 1 else out_ref.at[u, :, lo:hi]

    def ring(axis, stage, lo, hi):
        n = ny if axis == "y" else nx
        c = y if axis == "y" else x
        half = n // 2
        mid = (lo + hi) // 2
        steps = []
        for sign in (1, -1):
            prev = None
            lane = []
            for k in range(half):
                u = (c - sign * k + 2 * n) % n
                a_lo, a_hi = lo, hi
                if k == half - 1 and n % 2 == 0:
                    a_lo, a_hi = (lo, mid) if sign == 1 else (mid, hi)
                if stage == 1 and k == 0:
                    src = block_ref.at[a_lo:a_hi]
                else:
                    src = unit(axis, stage, u, a_lo, a_hi)
                dst = unit(axis, stage, u, a_lo, a_hi)
                target = dev(x, y + sign) if axis == "y" else dev(x + sign, y)
                j = sem_count[0]
                sem_count[0] += 1
                cp = pltpu.make_async_remote_copy(
                    src_ref=src, dst_ref=dst, send_sem=send_sems.at[j], recv_sem=recv_sems.at[j],
                    device_id=target, device_id_type=pl.DeviceIdType.MESH)
                lane.append((prev, cp))
                prev = cp
            steps.append(lane)
        return steps

    plans = []
    step = hr // pieces
    for p in range(pieces):
        for base, first, second in ((0, "y", "x"), (hr, "x", "y")):
            lo = base + p * step
            s1 = ring(first, 1, lo, lo + step)
            s2 = ring(second, 2, lo, lo + step)
            plans.append((s1, s2))

    started = []

    def run(lane_list):
        depth = max(len(l) for l in lane_list)
        for k in range(depth):
            for lane in lane_list:
                if k < len(lane):
                    prev, cp = lane[k]
                    if prev is not None:
                        prev.wait_recv()
                    cp.start()
                    started.append(cp)

    run([lane for s1, _ in plans for lane in s1])
    for s1, _ in plans:
        for lane in s1:
            lane[-1][1].wait_recv()
    own.wait()
    run([lane for _, s2 in plans for lane in s2])
    for _, s2 in plans:
        for lane in s2:
            lane[-1][1].wait_recv()
    for cp in started:
        cp.wait_send()


def ring_gather(block, nx, ny, axis="seq", other="exp", cid=3, pieces=1):
    vmem = pltpu.MemorySpace.VMEM
    n_sems = 4 * pieces * (nx // 2 + ny // 2) + 4
    return pl.pallas_call(
        functools.partial(ring_gather_kernel, nx, ny, axis, other, pieces),
        out_shape=jax.ShapeDtypeStruct((nx, ny) + block.shape, block.dtype),
        in_specs=[pl.BlockSpec(memory_space=vmem)],
        out_specs=pl.BlockSpec(memory_space=vmem),
        scratch_shapes=[
            pltpu.SemaphoreType.DMA((1,)),
            pltpu.SemaphoreType.DMA((n_sems,)),
            pltpu.SemaphoreType.DMA((n_sems,)),
        ],
        compiler_params=pltpu.CompilerParams(
            collective_id=cid, has_side_effects=True, vmem_limit_bytes=48 * 1024 * 1024
        ),
    )(block)


def rms_scale(matrix, gain):
    mean_square = jnp.mean(matrix * matrix, axis=-1, keepdims=True)
    return matrix * lax.rsqrt(mean_square + EPSILON) * gain


def expert_terms(block, gate_slice, up_slice, down_slice):
    gate = jnp.einsum("nek,ekf->nef", block, gate_slice, preferred_element_type=jnp.float32)
    upward = jnp.einsum("nek,ekf->nef", block, up_slice, preferred_element_type=jnp.float32)
    act = (jax.nn.silu(gate) * upward).astype(jnp.bfloat16)
    return jnp.einsum("nef,ekf->nek", act, down_slice, preferred_element_type=jnp.float32)


def local(
    tokens,
    array_type,
    block_pattern,
    gain_attn,
    w_query,
    w_key,
    w_value,
    logit_scale,
    w_out,
    gain_ffn,
    w_gate,
    w_up,
    w_down,
):
    n_exp = lax.axis_size("exp")
    row_count = tokens.shape[0]
    width = tokens.shape[1]
    head_cols = w_query.shape[1]
    heads_dev = logit_scale.shape[0]
    head_size = head_cols // heads_dev
    n_blocks = block_pattern.shape[0]
    inputs = tokens.astype(jnp.float32)
    normed_attn = rms_scale(inputs, gain_attn).astype(jnp.bfloat16)
    projector = jnp.concatenate([w_query, w_key, w_value], axis=1)
    joined_qkv = jnp.dot(
        ring_gather(normed_attn, n_exp // CORES, CORES, "exp", "seq", 4).reshape(n_exp * row_count, width),
        projector,
        preferred_element_type=jnp.float32,
    ).astype(jnp.bfloat16)
    block_len = joined_qkv.shape[0]
    query_heads = joined_qkv[:, :head_cols].reshape(block_len, heads_dev, head_size)
    key_value = joined_qkv[:, head_cols:]
    position = lax.axis_index("seq")
    head_scale = logit_scale[:, None, None]

    def attend(state, kv_block, source):
        row_top, weight_sum, numerator = state
        key_rows = kv_block[:, :head_cols].reshape(block_len, heads_dev, head_size)
        value_rows = kv_block[:, head_cols:].reshape(block_len, heads_dev, head_size)
        allowed = block_pattern[position, source] > 0
        scores = (
            jnp.einsum("qhd,khd->hqk", query_heads, key_rows, preferred_element_type=jnp.float32)
            * head_scale
        )
        block_top = jnp.max(scores, axis=2)
        new_top = jnp.where(allowed, jnp.maximum(row_top, block_top), row_top)
        shifted = jnp.minimum(scores - new_top[:, :, None], 0.0)
        weights = jnp.where(allowed, jnp.exp(shifted), 0.0)
        rescale = jnp.exp(row_top - new_top)
        weight_sum = weight_sum * rescale + jnp.sum(weights, axis=2)
        contrib = jnp.einsum(
            "hqk,khd->qhd",
            weights.astype(jnp.bfloat16),
            value_rows,
            preferred_element_type=jnp.float32,
        )
        numerator = numerator * jnp.transpose(rescale)[:, :, None] + contrib
        return (new_top, weight_sum, numerator)

    start_state = (
        jnp.full((heads_dev, block_len), -jnp.inf, jnp.float32),
        jnp.zeros((heads_dev, block_len), jnp.float32),
        jnp.zeros((block_len, heads_dev, head_size), jnp.float32),
    )
    state = attend(start_state, key_value, position)
    offsets = [d for d in range(1, REACH + 1)] + [-d for d in range(1, REACH + 1)]
    neighbours = shift_exchange(key_value, offsets, "seq", "exp", 2)
    for distance in range(1, REACH + 1):
        state = attend(state, neighbours[distance - 1], (position - distance) % n_blocks)
        state = attend(state, neighbours[REACH + distance - 1], (position + distance) % n_blocks)
    heads_out = (
        (state[2] / jnp.transpose(state[1])[:, :, None])
        .astype(jnp.bfloat16)
        .reshape(block_len, head_cols)
    )
    all_heads = lax.all_to_all(heads_out, "exp", split_axis=0, concat_axis=1, tiled=True)
    attn_out = jnp.dot(
        all_heads,
        lax.all_gather(w_out, "exp", axis=0, tiled=True),
        preferred_element_type=jnp.float32,
    )
    hidden_state = inputs + attn_out
    normed_ffn = rms_scale(hidden_state, gain_ffn).astype(jnp.bfloat16)
    experts_dev = w_gate.shape[0]
    n_total = experts_dev * n_exp
    capacity = 2 * row_count // n_total
    one_hot = (array_type[:, None] == jnp.arange(n_total, dtype=jnp.int32)[None, :]).astype(
        jnp.int32
    )
    slot_rank = jnp.sum(jnp.cumsum(one_hot, axis=0) * one_hot, axis=1) - 1
    owner = array_type // experts_dev
    local_expert = array_type % experts_dev
    slot_id = (owner * capacity + slot_rank) * experts_dev + local_expert
    n_slots = n_exp * capacity * experts_dev
    selector = (slot_id[None, :] == jnp.arange(n_slots, dtype=jnp.int32)[:, None]).astype(
        jnp.bfloat16
    )
    outgoing = jnp.dot(selector, normed_ffn, preferred_element_type=jnp.float32).astype(
        jnp.bfloat16
    )
    outgoing = outgoing.reshape(n_exp * capacity, experts_dev, width)
    arrived = lax.all_to_all(outgoing, "exp", split_axis=0, concat_axis=0, tiled=True)
    n_seq = lax.axis_size("seq")
    y_size = Y_RING if n_seq % Y_RING == 0 else n_seq
    gathered = ring_gather(
        arrived.reshape(arrived.shape[0], width), n_seq // y_size, y_size, pieces=2
    ).reshape((n_seq * arrived.shape[0],) + arrived.shape[1:])
    n_seq = lax.axis_size("seq")
    y_size = Y_RING if n_seq % Y_RING == 0 else n_seq
    summed = ring_ffn(
        gathered.reshape(gathered.shape[0], width),
        w_gate[0], w_up[0], w_down[0], n_seq // y_size, y_size,
    ).reshape((-1,) + gathered.shape[1:])
    returned = lax.all_to_all(summed, "exp", split_axis=0, concat_axis=0, tiled=True)
    expert_out = jnp.dot(
        jnp.transpose(selector),
        returned.reshape(n_slots, width),
        preferred_element_type=jnp.float32,
    )
    return (hidden_state + expert_out).astype(jnp.bfloat16)


def solution(mesh):
    return jax.shard_map(
        local,
        mesh=mesh,
        in_specs=(
            P(("seq", "exp"), None),
            P(("seq", "exp")),
            P(),
            P(),
            P(None, "exp"),
            P(None, "exp"),
            P(None, "exp"),
            P("exp"),
            P("exp", None),
            P(),
            P("exp", None, "seq"),
            P("exp", None, "seq"),
            P("exp", None, "seq"),
        ),
        out_specs=P(("seq", "exp"), None),
        check_vma=False,
    )
```

```python
import jax
import jax.numpy as jnp
from jax import lax
from jax.sharding import PartitionSpec as P
from jax.experimental import pallas as pl
from jax.experimental.pallas import tpu as pltpu
import functools

REACH = 3
Y_RING = 8
CORES = 2


EPSILON = 1e-05


def passed_along(block, axis, distance):
    devices = range(lax.axis_size(axis))
    route = [((i - distance) % len(devices), i) for i in devices]
    return lax.ppermute(block, axis, route)


def ring_reduce_kernel(nx, ny, splits, part_ref, out_ref, recv1, send1, acc, recv2, send2,
                       s1_send, s1_recv, s2_send, s2_recv):
    me = lax.axis_index("seq")
    col = lax.axis_index("exp")
    x = me // ny
    y = me % ny
    y_up = x * ny + (y + 1) % ny
    y_down = x * ny + (y + ny - 1) % ny
    x_up = ((x + 1) % nx) * ny + y
    x_down = ((x + nx - 1) % nx) * ny + y
    rows = part_ref.shape[2]
    piece = rows // splits
    quarter = rows // 4

    barrier = pltpu.get_barrier_semaphore()
    for peer in (y_up, y_down, x_up, x_down):
        pl.semaphore_signal(barrier, inc=1, device_id=(peer, col),
                            device_id_type=pl.DeviceIdType.MESH)
    pl.semaphore_wait(barrier, 4)

    lanes = []
    for a in range(nx):
        for p in range(splits):
            if a < nx // 2:
                lanes.append((y_up, 1, a, p * piece))
            else:
                lanes.append((y_down, -1, a, p * piece))
    copies1 = []
    for k in range(ny - 1):
        step_copies = []
        for d, (peer, sign, a, r0) in enumerate(lanes):
            c = (y - sign * (k + 1) + 2 * ny) % ny
            if k == 0:
                src = part_ref.at[a, c, r0:r0 + piece]
            else:
                copies1[k - 1][d].wait_recv()
                send1[d, k] = (recv1[d, k - 1].astype(jnp.float32)
                               + part_ref[a, c, r0:r0 + piece].astype(jnp.float32)).astype(send1.dtype)
                src = send1.at[d, k]
            cp = pltpu.make_async_remote_copy(
                src_ref=src, dst_ref=recv1.at[d, k],
                send_sem=s1_send.at[d, k], recv_sem=s1_recv.at[d, k],
                device_id=(peer, col), device_id_type=pl.DeviceIdType.MESH)
            cp.start()
            step_copies.append(cp)
        copies1.append(step_copies)
    for d, (peer, sign, a, r0) in enumerate(lanes):
        copies1[ny - 2][d].wait_recv()
        acc[a, r0:r0 + piece] = (recv1[d, ny - 2].astype(jnp.float32)
                                 + part_ref[a, y, r0:r0 + piece].astype(jnp.float32))

    lanes2 = [(x_up, 1, 0), (x_up, 1, quarter), (x_down, -1, 2 * quarter), (x_down, -1, 3 * quarter)]
    copies2 = []
    for k in range(nx - 1):
        step_copies = []
        for d, (peer, sign, r0) in enumerate(lanes2):
            c = (x - sign * (k + 1) + 2 * nx) % nx
            if k == 0:
                src = acc.at[c, r0:r0 + quarter]
            else:
                copies2[k - 1][d].wait_recv()
                send2[d, k] = recv2[d, k - 1] + acc[c, r0:r0 + quarter]
                src = send2.at[d, k]
            cp = pltpu.make_async_remote_copy(
                src_ref=src, dst_ref=recv2.at[d, k],
                send_sem=s2_send.at[d, k], recv_sem=s2_recv.at[d, k],
                device_id=(peer, col), device_id_type=pl.DeviceIdType.MESH)
            cp.start()
            step_copies.append(cp)
        copies2.append(step_copies)
    for d, (peer, sign, r0) in enumerate(lanes2):
        copies2[nx - 2][d].wait_recv()
        out_ref[r0:r0 + quarter] = (recv2[d, nx - 2] + acc[x, r0:r0 + quarter]).astype(out_ref.dtype)
    for step_copies in copies1 + copies2:
        for cp in step_copies:
            cp.wait_send()


def ring_reduce(part, nx, ny, splits=2):
    width = part.shape[-1]
    rows = part.shape[0] // (nx * ny)
    part = part.reshape(nx, ny, rows, width)
    n1 = nx * splits
    vmem = pltpu.MemorySpace.VMEM
    return pl.pallas_call(
        functools.partial(ring_reduce_kernel, nx, ny, splits),
        out_shape=jax.ShapeDtypeStruct((rows, width), jnp.bfloat16),
        in_specs=[pl.BlockSpec(memory_space=vmem)],
        out_specs=pl.BlockSpec(memory_space=vmem),
        scratch_shapes=[
            pltpu.VMEM((n1, ny - 1, rows // splits, width), jnp.bfloat16),
            pltpu.VMEM((n1, ny - 1, rows // splits, width), jnp.bfloat16),
            pltpu.VMEM((nx, rows, width), jnp.float32),
            pltpu.VMEM((4, nx - 1, rows // 4, width), jnp.float32),
            pltpu.VMEM((4, nx - 1, rows // 4, width), jnp.float32),
            pltpu.SemaphoreType.DMA((n1, ny - 1)),
            pltpu.SemaphoreType.DMA((n1, ny - 1)),
            pltpu.SemaphoreType.DMA((4, nx - 1)),
            pltpu.SemaphoreType.DMA((4, nx - 1)),
        ],
        compiler_params=pltpu.CompilerParams(
            collective_id=1, has_side_effects=True, vmem_limit_bytes=48 * 1024 * 1024
        ),
    )(part)


def ring_ffn_kernel(nx, ny, splits, tok_ref, wg_ref, wu_ref, wd_ref, out_ref, pbuf, recv1, send1,
                    acc, recv2, send2, s1_send, s1_recv, s2_send, s2_recv):
    me = lax.axis_index("seq")
    col = lax.axis_index("exp")
    x = me // ny
    y = me % ny
    y_up = x * ny + (y + 1) % ny
    y_down = x * ny + (y + ny - 1) % ny
    x_up = ((x + 1) % nx) * ny + y
    x_down = ((x + nx - 1) % nx) * ny + y
    rows = tok_ref.shape[2]
    width = tok_ref.shape[3]
    piece = rows // splits
    quarter = rows // 4
    half_x = nx // 2

    def partials(c_up, c_down):
        tok = jnp.concatenate(
            [tok_ref[0:half_x, c_up].reshape(half_x * rows, width),
             tok_ref[half_x:nx, c_down].reshape((nx - half_x) * rows, width)], axis=0)
        gate = jnp.dot(tok, wg_ref[...], preferred_element_type=jnp.float32)
        upward = jnp.dot(tok, wu_ref[...], preferred_element_type=jnp.float32)
        act = (gate / (1.0 + jnp.exp(-gate)) * upward).astype(jnp.bfloat16)
        down = lax.dot_general(act, wd_ref[...], (((1,), (1,)), ((), ())),
                               preferred_element_type=jnp.float32)
        pbuf[...] = down.astype(jnp.bfloat16).reshape(nx, rows, width)

    barrier = pltpu.get_barrier_semaphore()
    for peer in (y_up, y_down, x_up, x_down):
        pl.semaphore_signal(barrier, inc=1, device_id=(peer, col),
                            device_id_type=pl.DeviceIdType.MESH)
    pl.semaphore_wait(barrier, 4)

    lanes = []
    for a in range(nx):
        for p in range(splits):
            if a < half_x:
                lanes.append((y_up, 1, a, p * piece))
            else:
                lanes.append((y_down, -1, a, p * piece))
    copies1 = []
    for k in range(ny - 1):
        partials((y - k - 1 + ny) % ny, (y + k + 1) % ny)
        step_copies = []
        for d, (peer, sign, a, r0) in enumerate(lanes):
            if k == 0:
                send1[d, k] = pbuf[a, r0:r0 + piece]
            else:
                copies1[k - 1][d].wait_recv()
                send1[d, k] = (recv1[d, k - 1].astype(jnp.float32)
                               + pbuf[a, r0:r0 + piece].astype(jnp.float32)).astype(send1.dtype)
            cp = pltpu.make_async_remote_copy(
                src_ref=send1.at[d, k], dst_ref=recv1.at[d, k],
                send_sem=s1_send.at[d, k], recv_sem=s1_recv.at[d, k],
                device_id=(peer, col), device_id_type=pl.DeviceIdType.MESH)
            cp.start()
            step_copies.append(cp)
        copies1.append(step_copies)
    partials(y, y)
    for d, (peer, sign, a, r0) in enumerate(lanes):
        copies1[ny - 2][d].wait_recv()
        acc[a, r0:r0 + piece] = (recv1[d, ny - 2].astype(jnp.float32)
                                 + pbuf[a, r0:r0 + piece].astype(jnp.float32))

    lanes2 = [(x_up, 1, 0), (x_up, 1, quarter), (x_down, -1, 2 * quarter), (x_down, -1, 3 * quarter)]
    copies2 = []
    for k in range(nx - 1):
        step_copies = []
        for d, (peer, sign, r0) in enumerate(lanes2):
            c = (x - sign * (k + 1) + 2 * nx) % nx
            if k == 0:
                src = acc.at[c, r0:r0 + quarter]
            else:
                copies2[k - 1][d].wait_recv()
                send2[d, k] = recv2[d, k - 1] + acc[c, r0:r0 + quarter]
                src = send2.at[d, k]
            cp = pltpu.make_async_remote_copy(
                src_ref=src, dst_ref=recv2.at[d, k],
                send_sem=s2_send.at[d, k], recv_sem=s2_recv.at[d, k],
                device_id=(peer, col), device_id_type=pl.DeviceIdType.MESH)
            cp.start()
            step_copies.append(cp)
        copies2.append(step_copies)
    for d, (peer, sign, r0) in enumerate(lanes2):
        copies2[nx - 2][d].wait_recv()
        out_ref[r0:r0 + quarter] = (recv2[d, nx - 2] + acc[x, r0:r0 + quarter]).astype(out_ref.dtype)
    for step_copies in copies1 + copies2:
        for cp in step_copies:
            cp.wait_send()


def ring_ffn(tokens, w_gate, w_up, w_down, nx, ny, splits=2):
    width = tokens.shape[-1]
    rows = tokens.shape[0] // (nx * ny)
    tokens = tokens.reshape(nx, ny, rows, width)
    n1 = nx * splits
    vmem = pltpu.MemorySpace.VMEM
    return pl.pallas_call(
        functools.partial(ring_ffn_kernel, nx, ny, splits),
        out_shape=jax.ShapeDtypeStruct((rows, width), jnp.bfloat16),
        in_specs=[pl.BlockSpec(memory_space=vmem)] * 4,
        out_specs=pl.BlockSpec(memory_space=vmem),
        scratch_shapes=[
            pltpu.VMEM((nx, rows, width), jnp.bfloat16),
            pltpu.VMEM((n1, ny - 1, rows // splits, width), jnp.bfloat16),
            pltpu.VMEM((n1, ny - 1, rows // splits, width), jnp.bfloat16),
            pltpu.VMEM((nx, rows, width), jnp.float32),
            pltpu.VMEM((4, nx - 1, rows // 4, width), jnp.float32),
            pltpu.VMEM((4, nx - 1, rows // 4, width), jnp.float32),
            pltpu.SemaphoreType.DMA((n1, ny - 1)),
            pltpu.SemaphoreType.DMA((n1, ny - 1)),
            pltpu.SemaphoreType.DMA((4, nx - 1)),
            pltpu.SemaphoreType.DMA((4, nx - 1)),
        ],
        compiler_params=pltpu.CompilerParams(
            collective_id=5, has_side_effects=True, vmem_limit_bytes=56 * 1024 * 1024
        ),
    )(tokens, w_gate, w_up, w_down)


def shift_exchange_kernel(offsets, axis, other, block_ref, out_ref, send_sems, recv_sems):
    n = lax.axis_size(axis)
    me = lax.axis_index(axis)
    col = lax.axis_index(other)

    def dev(peer):
        return (peer, col) if axis == "seq" else (col, peer)

    targets = [(me + o + n * len(offsets)) % n for o in offsets]
    barrier = pltpu.get_barrier_semaphore()
    for peer in targets:
        pl.semaphore_signal(barrier, inc=1, device_id=dev(peer),
                            device_id_type=pl.DeviceIdType.MESH)
    pl.semaphore_wait(barrier, len(offsets))
    copies = []
    for j, peer in enumerate(targets):
        cp = pltpu.make_async_remote_copy(
            src_ref=block_ref, dst_ref=out_ref.at[j],
            send_sem=send_sems.at[j], recv_sem=recv_sems.at[j],
            device_id=dev(peer), device_id_type=pl.DeviceIdType.MESH)
        cp.start()
        copies.append(cp)
    for cp in copies:
        cp.wait()


def shift_exchange(block, offsets, axis, other, cid):
    vmem = pltpu.MemorySpace.VMEM
    k = len(offsets)
    return pl.pallas_call(
        functools.partial(shift_exchange_kernel, tuple(offsets), axis, other),
        out_shape=jax.ShapeDtypeStruct((k,) + block.shape, block.dtype),
        in_specs=[pl.BlockSpec(memory_space=vmem)],
        out_specs=pl.BlockSpec(memory_space=vmem),
        scratch_shapes=[pltpu.SemaphoreType.DMA((k,)), pltpu.SemaphoreType.DMA((k,))],
        compiler_params=pltpu.CompilerParams(collective_id=cid, has_side_effects=True),
    )(block)


def exp_all_to_all_kernel(x_ref, y_ref, send_sems, recv_sems):
    n = lax.axis_size("exp")
    me = lax.axis_index("exp")
    row = lax.axis_index("seq")
    barrier = pltpu.get_barrier_semaphore()
    for k in range(1, n):
        pl.semaphore_signal(barrier, inc=1, device_id=(row, (me + k) % n),
                            device_id_type=pl.DeviceIdType.MESH)
    pl.semaphore_wait(barrier, n - 1)
    copies = []
    for k in range(1, n):
        peer = (me + k) % n
        cp = pltpu.make_async_remote_copy(
            src_ref=x_ref.at[peer], dst_ref=y_ref.at[me],
            send_sem=send_sems.at[k - 1], recv_sem=recv_sems.at[k - 1],
            device_id=(row, peer), device_id_type=pl.DeviceIdType.MESH)
        cp.start()
        copies.append(cp)
    y_ref[me] = x_ref[me]
    for cp in copies:
        cp.wait()


def exp_all_to_all(x, cid):
    n = x.shape[0]
    vmem = pltpu.MemorySpace.VMEM
    return pl.pallas_call(
        exp_all_to_all_kernel,
        out_shape=jax.ShapeDtypeStruct(x.shape, x.dtype),
        in_specs=[pl.BlockSpec(memory_space=vmem)],
        out_specs=pl.BlockSpec(memory_space=vmem),
        scratch_shapes=[pltpu.SemaphoreType.DMA((n - 1,)), pltpu.SemaphoreType.DMA((n - 1,))],
        compiler_params=pltpu.CompilerParams(collective_id=cid, has_side_effects=True),
    )(x)


def ring_gather_kernel(nx, ny, axis, other, pieces, block_ref, out_ref, local_sem, send_sems, recv_sems):
    me = lax.axis_index(axis)
    col = lax.axis_index(other)
    x = me // ny
    y = me % ny
    rows = block_ref.shape[0]
    hr = rows // 2

    def dev(a, b):
        idx = (a + nx) % nx * ny + (b + ny) % ny
        return (idx, col) if axis == "seq" else (col, idx)

    peers = [dev(x, y + 1), dev(x, y - 1), dev(x + 1, y), dev(x - 1, y)]
    barrier = pltpu.get_barrier_semaphore()
    for peer in peers:
        pl.semaphore_signal(barrier, inc=1, device_id=peer, device_id_type=pl.DeviceIdType.MESH)
    pl.semaphore_wait(barrier, 4)

    own = pltpu.make_async_copy(block_ref, out_ref.at[x, y], local_sem.at[0])
    own.start()
    sem_count = [0]

    def unit(axis, stage, u, lo, hi):
        if axis == "y":
            return out_ref.at[x, u, lo:hi] if stage == 1 else out_ref.at[:, u, lo:hi]
        return out_ref.at[u, y, lo:hi] if stage == 1 else out_ref.at[u, :, lo:hi]

    def ring(axis, stage, lo, hi):
        n = ny if axis == "y" else nx
        c = y if axis == "y" else x
        half = n // 2
        mid = (lo + hi) // 2
        steps = []
        for sign in (1, -1):
            prev = None
            lane = []
            for k in range(half):
                u = (c - sign * k + 2 * n) % n
                a_lo, a_hi = lo, hi
                if k == half - 1 and n % 2 == 0:
                    a_lo, a_hi = (lo, mid) if sign == 1 else (mid, hi)
                if stage == 1 and k == 0:
                    src = block_ref.at[a_lo:a_hi]
                else:
                    src = unit(axis, stage, u, a_lo, a_hi)
                dst = unit(axis, stage, u, a_lo, a_hi)
                target = dev(x, y + sign) if axis == "y" else dev(x + sign, y)
                j = sem_count[0]
                sem_count[0] += 1
                cp = pltpu.make_async_remote_copy(
                    src_ref=src, dst_ref=dst, send_sem=send_sems.at[j], recv_sem=recv_sems.at[j],
                    device_id=target, device_id_type=pl.DeviceIdType.MESH)
                lane.append((prev, cp))
                prev = cp
            steps.append(lane)
        return steps

    plans = []
    step = hr // pieces
    for p in range(pieces):
        for base, first, second in ((0, "y", "x"), (hr, "x", "y")):
            lo = base + p * step
            s1 = ring(first, 1, lo, lo + step)
            s2 = ring(second, 2, lo, lo + step)
            plans.append((s1, s2))

    started = []

    def run(lane_list):
        depth = max(len(l) for l in lane_list)
        for k in range(depth):
            for lane in lane_list:
                if k < len(lane):
                    prev, cp = lane[k]
                    if prev is not None:
                        prev.wait_recv()
                    cp.start()
                    started.append(cp)

    run([lane for s1, _ in plans for lane in s1])
    for s1, _ in plans:
        for lane in s1:
            lane[-1][1].wait_recv()
    own.wait()
    run([lane for _, s2 in plans for lane in s2])
    for _, s2 in plans:
        for lane in s2:
            lane[-1][1].wait_recv()
    for cp in started:
        cp.wait_send()


def ring_gather(block, nx, ny, axis="seq", other="exp", cid=3, pieces=1):
    vmem = pltpu.MemorySpace.VMEM
    n_sems = 4 * pieces * (nx // 2 + ny // 2) + 4
    return pl.pallas_call(
        functools.partial(ring_gather_kernel, nx, ny, axis, other, pieces),
        out_shape=jax.ShapeDtypeStruct((nx, ny) + block.shape, block.dtype),
        in_specs=[pl.BlockSpec(memory_space=vmem)],
        out_specs=pl.BlockSpec(memory_space=vmem),
        scratch_shapes=[
            pltpu.SemaphoreType.DMA((1,)),
            pltpu.SemaphoreType.DMA((n_sems,)),
            pltpu.SemaphoreType.DMA((n_sems,)),
        ],
        compiler_params=pltpu.CompilerParams(
            collective_id=cid, has_side_effects=True, vmem_limit_bytes=48 * 1024 * 1024
        ),
    )(block)


def rms_scale(matrix, gain):
    mean_square = jnp.mean(matrix * matrix, axis=-1, keepdims=True)
    return matrix * lax.rsqrt(mean_square + EPSILON) * gain


def expert_terms(block, gate_slice, up_slice, down_slice):
    gate = jnp.einsum("nek,ekf->nef", block, gate_slice, preferred_element_type=jnp.float32)
    upward = jnp.einsum("nek,ekf->nef", block, up_slice, preferred_element_type=jnp.float32)
    act = (jax.nn.silu(gate) * upward).astype(jnp.bfloat16)
    return jnp.einsum("nef,ekf->nek", act, down_slice, preferred_element_type=jnp.float32)


def local(
    tokens,
    array_type,
    block_pattern,
    gain_attn,
    w_query,
    w_key,
    w_value,
    logit_scale,
    w_out,
    gain_ffn,
    w_gate,
    w_up,
    w_down,
):
    n_exp = lax.axis_size("exp")
    row_count = tokens.shape[0]
    width = tokens.shape[1]
    head_cols = w_query.shape[1]
    heads_dev = logit_scale.shape[0]
    head_size = head_cols // heads_dev
    n_blocks = block_pattern.shape[0]
    inputs = tokens.astype(jnp.float32)
    normed_attn = rms_scale(inputs, gain_attn).astype(jnp.bfloat16)
    projector = jnp.concatenate([w_query, w_key, w_value], axis=1)
    joined_qkv = jnp.dot(
        ring_gather(normed_attn, n_exp // CORES, CORES, "exp", "seq", 4).reshape(n_exp * row_count, width),
        projector,
        preferred_element_type=jnp.float32,
    ).astype(jnp.bfloat16)
    block_len = joined_qkv.shape[0]
    query_heads = joined_qkv[:, :head_cols].reshape(block_len, heads_dev, head_size)
    key_value = joined_qkv[:, head_cols:]
    position = lax.axis_index("seq")
    head_scale = logit_scale[:, None, None]

    offsets = [d for d in range(1, REACH + 1)] + [-d for d in range(1, REACH + 1)]
    neighbours = shift_exchange(key_value, offsets, "seq", "exp", 2)
    band = jnp.concatenate([key_value[None], neighbours], axis=0)
    n_band = band.shape[0]
    sources = jnp.stack([position] + [(position - o) % n_blocks for o in offsets])
    allowed = jnp.repeat(block_pattern[position, sources] > 0, block_len)
    key_band = band[:, :, :head_cols].reshape(n_band * block_len, heads_dev, head_size)
    value_band = band[:, :, head_cols:].reshape(n_band * block_len, heads_dev, head_size)
    scores = (
        jnp.einsum("qhd,khd->hqk", query_heads, key_band, preferred_element_type=jnp.float32)
        * head_scale
    )
    scores = jnp.where(allowed[None, None, :], scores, -jnp.inf)
    row_top = jnp.max(scores, axis=2, keepdims=True)
    weights = jnp.exp(scores - row_top)
    weight_sum = jnp.sum(weights, axis=2)
    weighted = jnp.einsum(
        "hqk,khd->qhd",
        weights.astype(jnp.bfloat16),
        value_band,
        preferred_element_type=jnp.float32,
    )
    heads_out = (
        (weighted / jnp.transpose(weight_sum)[:, :, None])
        .astype(jnp.bfloat16)
        .reshape(block_len, head_cols)
    )
    all_heads = lax.all_to_all(heads_out, "exp", split_axis=0, concat_axis=1, tiled=True)
    attn_out = jnp.dot(
        all_heads,
        lax.all_gather(w_out, "exp", axis=0, tiled=True),
        preferred_element_type=jnp.float32,
    )
    hidden_state = inputs + attn_out
    normed_ffn = rms_scale(hidden_state, gain_ffn).astype(jnp.bfloat16)
    experts_dev = w_gate.shape[0]
    n_total = experts_dev * n_exp
    capacity = 2 * row_count // n_total
    one_hot = (array_type[:, None] == jnp.arange(n_total, dtype=jnp.int32)[None, :]).astype(
        jnp.int32
    )
    slot_rank = jnp.sum(jnp.cumsum(one_hot, axis=0) * one_hot, axis=1) - 1
    owner = array_type // experts_dev
    local_expert = array_type % experts_dev
    slot_id = (owner * capacity + slot_rank) * experts_dev + local_expert
    n_slots = n_exp * capacity * experts_dev
    selector = (slot_id[None, :] == jnp.arange(n_slots, dtype=jnp.int32)[:, None]).astype(
        jnp.bfloat16
    )
    outgoing = jnp.dot(selector, normed_ffn, preferred_element_type=jnp.float32).astype(
        jnp.bfloat16
    )
    outgoing = outgoing.reshape(n_exp * capacity, experts_dev, width)
    arrived = lax.all_to_all(outgoing, "exp", split_axis=0, concat_axis=0, tiled=True)
    n_seq = lax.axis_size("seq")
    y_size = Y_RING if n_seq % Y_RING == 0 else n_seq
    gathered = ring_gather(
        arrived.reshape(arrived.shape[0], width), n_seq // y_size, y_size, pieces=2
    ).reshape((n_seq * arrived.shape[0],) + arrived.shape[1:])
    n_seq = lax.axis_size("seq")
    y_size = Y_RING if n_seq % Y_RING == 0 else n_seq
    summed = ring_ffn(
        gathered.reshape(gathered.shape[0], width),
        w_gate[0], w_up[0], w_down[0], n_seq // y_size, y_size,
    ).reshape((-1,) + gathered.shape[1:])
    returned = lax.all_to_all(summed, "exp", split_axis=0, concat_axis=0, tiled=True)
    expert_out = jnp.dot(
        jnp.transpose(selector),
        returned.reshape(n_slots, width),
        preferred_element_type=jnp.float32,
    )
    return (hidden_state + expert_out).astype(jnp.bfloat16)


def solution(mesh):
    return jax.shard_map(
        local,
        mesh=mesh,
        in_specs=(
            P(("seq", "exp"), None),
            P(("seq", "exp")),
            P(),
            P(),
            P(None, "exp"),
            P(None, "exp"),
            P(None, "exp"),
            P("exp"),
            P("exp", None),
            P(),
            P("exp", None, "seq"),
            P("exp", None, "seq"),
            P("exp", None, "seq"),
        ),
        out_specs=P(("seq", "exp"), None),
        check_vma=False,
    )
```

```python
import jax
import jax.numpy as jnp
from jax import lax
from jax.sharding import PartitionSpec as P
from jax.experimental import pallas as pl
from jax.experimental.pallas import tpu as pltpu
import functools

REACH = 3
Y_RING = 8
CORES = 2


EPSILON = 1e-05


def passed_along(block, axis, distance):
    devices = range(lax.axis_size(axis))
    route = [((i - distance) % len(devices), i) for i in devices]
    return lax.ppermute(block, axis, route)


def ring_reduce_kernel(nx, ny, splits, part_ref, out_ref, recv1, send1, acc, recv2, send2,
                       s1_send, s1_recv, s2_send, s2_recv):
    me = lax.axis_index("seq")
    col = lax.axis_index("exp")
    x = me // ny
    y = me % ny
    y_up = x * ny + (y + 1) % ny
    y_down = x * ny + (y + ny - 1) % ny
    x_up = ((x + 1) % nx) * ny + y
    x_down = ((x + nx - 1) % nx) * ny + y
    rows = part_ref.shape[2]
    piece = rows // splits
    quarter = rows // 4

    barrier = pltpu.get_barrier_semaphore()
    for peer in (y_up, y_down, x_up, x_down):
        pl.semaphore_signal(barrier, inc=1, device_id=(peer, col),
                            device_id_type=pl.DeviceIdType.MESH)
    pl.semaphore_wait(barrier, 4)

    lanes = []
    for a in range(nx):
        for p in range(splits):
            if a < nx // 2:
                lanes.append((y_up, 1, a, p * piece))
            else:
                lanes.append((y_down, -1, a, p * piece))
    copies1 = []
    for k in range(ny - 1):
        step_copies = []
        for d, (peer, sign, a, r0) in enumerate(lanes):
            c = (y - sign * (k + 1) + 2 * ny) % ny
            if k == 0:
                src = part_ref.at[a, c, r0:r0 + piece]
            else:
                copies1[k - 1][d].wait_recv()
                send1[d, k] = (recv1[d, k - 1].astype(jnp.float32)
                               + part_ref[a, c, r0:r0 + piece].astype(jnp.float32)).astype(send1.dtype)
                src = send1.at[d, k]
            cp = pltpu.make_async_remote_copy(
                src_ref=src, dst_ref=recv1.at[d, k],
                send_sem=s1_send.at[d, k], recv_sem=s1_recv.at[d, k],
                device_id=(peer, col), device_id_type=pl.DeviceIdType.MESH)
            cp.start()
            step_copies.append(cp)
        copies1.append(step_copies)
    for d, (peer, sign, a, r0) in enumerate(lanes):
        copies1[ny - 2][d].wait_recv()
        acc[a, r0:r0 + piece] = (recv1[d, ny - 2].astype(jnp.float32)
                                 + part_ref[a, y, r0:r0 + piece].astype(jnp.float32))

    lanes2 = [(x_up, 1, 0), (x_up, 1, quarter), (x_down, -1, 2 * quarter), (x_down, -1, 3 * quarter)]
    copies2 = []
    for k in range(nx - 1):
        step_copies = []
        for d, (peer, sign, r0) in enumerate(lanes2):
            c = (x - sign * (k + 1) + 2 * nx) % nx
            if k == 0:
                src = acc.at[c, r0:r0 + quarter]
            else:
                copies2[k - 1][d].wait_recv()
                send2[d, k] = recv2[d, k - 1] + acc[c, r0:r0 + quarter]
                src = send2.at[d, k]
            cp = pltpu.make_async_remote_copy(
                src_ref=src, dst_ref=recv2.at[d, k],
                send_sem=s2_send.at[d, k], recv_sem=s2_recv.at[d, k],
                device_id=(peer, col), device_id_type=pl.DeviceIdType.MESH)
            cp.start()
            step_copies.append(cp)
        copies2.append(step_copies)
    for d, (peer, sign, r0) in enumerate(lanes2):
        copies2[nx - 2][d].wait_recv()
        out_ref[r0:r0 + quarter] = (recv2[d, nx - 2] + acc[x, r0:r0 + quarter]).astype(out_ref.dtype)
    for step_copies in copies1 + copies2:
        for cp in step_copies:
            cp.wait_send()


def ring_reduce(part, nx, ny, splits=2):
    width = part.shape[-1]
    rows = part.shape[0] // (nx * ny)
    part = part.reshape(nx, ny, rows, width)
    n1 = nx * splits
    vmem = pltpu.MemorySpace.VMEM
    return pl.pallas_call(
        functools.partial(ring_reduce_kernel, nx, ny, splits),
        out_shape=jax.ShapeDtypeStruct((rows, width), jnp.bfloat16),
        in_specs=[pl.BlockSpec(memory_space=vmem)],
        out_specs=pl.BlockSpec(memory_space=vmem),
        scratch_shapes=[
            pltpu.VMEM((n1, ny - 1, rows // splits, width), jnp.bfloat16),
            pltpu.VMEM((n1, ny - 1, rows // splits, width), jnp.bfloat16),
            pltpu.VMEM((nx, rows, width), jnp.float32),
            pltpu.VMEM((4, nx - 1, rows // 4, width), jnp.float32),
            pltpu.VMEM((4, nx - 1, rows // 4, width), jnp.float32),
            pltpu.SemaphoreType.DMA((n1, ny - 1)),
            pltpu.SemaphoreType.DMA((n1, ny - 1)),
            pltpu.SemaphoreType.DMA((4, nx - 1)),
            pltpu.SemaphoreType.DMA((4, nx - 1)),
        ],
        compiler_params=pltpu.CompilerParams(
            collective_id=1, has_side_effects=True, vmem_limit_bytes=48 * 1024 * 1024
        ),
    )(part)


def ring_ffn_kernel(nx, ny, splits, tok_ref, wg_ref, wu_ref, wd_ref, out_ref, pbuf, recv1, send1,
                    acc, recv2, send2, s1_send, s1_recv, s2_send, s2_recv):
    me = lax.axis_index("seq")
    col = lax.axis_index("exp")
    x = me // ny
    y = me % ny
    y_up = x * ny + (y + 1) % ny
    y_down = x * ny + (y + ny - 1) % ny
    x_up = ((x + 1) % nx) * ny + y
    x_down = ((x + nx - 1) % nx) * ny + y
    rows = tok_ref.shape[2]
    width = tok_ref.shape[3]
    piece = rows // splits
    quarter = rows // 4
    half_x = nx // 2

    def partials(c_up, c_down):
        tok = jnp.concatenate(
            [tok_ref[0:half_x, c_up].reshape(half_x * rows, width),
             tok_ref[half_x:nx, c_down].reshape((nx - half_x) * rows, width)], axis=0)
        gate = jnp.dot(tok, wg_ref[...], preferred_element_type=jnp.float32)
        upward = jnp.dot(tok, wu_ref[...], preferred_element_type=jnp.float32)
        act = (gate / (1.0 + jnp.exp(-gate)) * upward).astype(jnp.bfloat16)
        down = lax.dot_general(act, wd_ref[...], (((1,), (1,)), ((), ())),
                               preferred_element_type=jnp.float32)
        pbuf[...] = down.astype(jnp.bfloat16).reshape(nx, rows, width)

    barrier = pltpu.get_barrier_semaphore()
    for peer in (y_up, y_down, x_up, x_down):
        pl.semaphore_signal(barrier, inc=1, device_id=(peer, col),
                            device_id_type=pl.DeviceIdType.MESH)
    pl.semaphore_wait(barrier, 4)

    lanes = []
    for a in range(nx):
        for p in range(splits):
            if a < half_x:
                lanes.append((y_up, 1, a, p * piece))
            else:
                lanes.append((y_down, -1, a, p * piece))
    copies1 = []
    for k in range(ny - 1):
        partials((y - k - 1 + ny) % ny, (y + k + 1) % ny)
        step_copies = []
        for d, (peer, sign, a, r0) in enumerate(lanes):
            if k == 0:
                send1[d, k] = pbuf[a, r0:r0 + piece]
            else:
                copies1[k - 1][d].wait_recv()
                send1[d, k] = (recv1[d, k - 1].astype(jnp.float32)
                               + pbuf[a, r0:r0 + piece].astype(jnp.float32)).astype(send1.dtype)
            cp = pltpu.make_async_remote_copy(
                src_ref=send1.at[d, k], dst_ref=recv1.at[d, k],
                send_sem=s1_send.at[d, k], recv_sem=s1_recv.at[d, k],
                device_id=(peer, col), device_id_type=pl.DeviceIdType.MESH)
            cp.start()
            step_copies.append(cp)
        copies1.append(step_copies)
    partials(y, y)
    for d, (peer, sign, a, r0) in enumerate(lanes):
        copies1[ny - 2][d].wait_recv()
        acc[a, r0:r0 + piece] = (recv1[d, ny - 2].astype(jnp.float32)
                                 + pbuf[a, r0:r0 + piece].astype(jnp.float32))

    lanes2 = [(x_up, 1, 0), (x_up, 1, quarter), (x_down, -1, 2 * quarter), (x_down, -1, 3 * quarter)]
    copies2 = []
    for k in range(nx - 1):
        step_copies = []
        for d, (peer, sign, r0) in enumerate(lanes2):
            c = (x - sign * (k + 1) + 2 * nx) % nx
            if k == 0:
                src = acc.at[c, r0:r0 + quarter]
            else:
                copies2[k - 1][d].wait_recv()
                send2[d, k] = recv2[d, k - 1] + acc[c, r0:r0 + quarter]
                src = send2.at[d, k]
            cp = pltpu.make_async_remote_copy(
                src_ref=src, dst_ref=recv2.at[d, k],
                send_sem=s2_send.at[d, k], recv_sem=s2_recv.at[d, k],
                device_id=(peer, col), device_id_type=pl.DeviceIdType.MESH)
            cp.start()
            step_copies.append(cp)
        copies2.append(step_copies)
    for d, (peer, sign, r0) in enumerate(lanes2):
        copies2[nx - 2][d].wait_recv()
        out_ref[r0:r0 + quarter] = (recv2[d, nx - 2] + acc[x, r0:r0 + quarter]).astype(out_ref.dtype)
    for step_copies in copies1 + copies2:
        for cp in step_copies:
            cp.wait_send()


def ring_ffn(tokens, w_gate, w_up, w_down, nx, ny, splits=2):
    width = tokens.shape[-1]
    rows = tokens.shape[0] // (nx * ny)
    tokens = tokens.reshape(nx, ny, rows, width)
    n1 = nx * splits
    vmem = pltpu.MemorySpace.VMEM
    return pl.pallas_call(
        functools.partial(ring_ffn_kernel, nx, ny, splits),
        out_shape=jax.ShapeDtypeStruct((rows, width), jnp.bfloat16),
        in_specs=[pl.BlockSpec(memory_space=vmem)] * 4,
        out_specs=pl.BlockSpec(memory_space=vmem),
        scratch_shapes=[
            pltpu.VMEM((nx, rows, width), jnp.bfloat16),
            pltpu.VMEM((n1, ny - 1, rows // splits, width), jnp.bfloat16),
            pltpu.VMEM((n1, ny - 1, rows // splits, width), jnp.bfloat16),
            pltpu.VMEM((nx, rows, width), jnp.float32),
            pltpu.VMEM((4, nx - 1, rows // 4, width), jnp.float32),
            pltpu.VMEM((4, nx - 1, rows // 4, width), jnp.float32),
            pltpu.SemaphoreType.DMA((n1, ny - 1)),
            pltpu.SemaphoreType.DMA((n1, ny - 1)),
            pltpu.SemaphoreType.DMA((4, nx - 1)),
            pltpu.SemaphoreType.DMA((4, nx - 1)),
        ],
        compiler_params=pltpu.CompilerParams(
            collective_id=5, has_side_effects=True, vmem_limit_bytes=56 * 1024 * 1024
        ),
    )(tokens, w_gate, w_up, w_down)


def shift_exchange_kernel(offsets, axis, other, block_ref, out_ref, send_sems, recv_sems):
    n = lax.axis_size(axis)
    me = lax.axis_index(axis)
    col = lax.axis_index(other)

    def dev(peer):
        return (peer, col) if axis == "seq" else (col, peer)

    targets = [(me + o + n * len(offsets)) % n for o in offsets]
    barrier = pltpu.get_barrier_semaphore()
    for peer in targets:
        pl.semaphore_signal(barrier, inc=1, device_id=dev(peer),
                            device_id_type=pl.DeviceIdType.MESH)
    pl.semaphore_wait(barrier, len(offsets))
    copies = []
    for j, peer in enumerate(targets):
        cp = pltpu.make_async_remote_copy(
            src_ref=block_ref, dst_ref=out_ref.at[j],
            send_sem=send_sems.at[j], recv_sem=recv_sems.at[j],
            device_id=dev(peer), device_id_type=pl.DeviceIdType.MESH)
        cp.start()
        copies.append(cp)
    for cp in copies:
        cp.wait()


def shift_exchange(block, offsets, axis, other, cid):
    vmem = pltpu.MemorySpace.VMEM
    k = len(offsets)
    return pl.pallas_call(
        functools.partial(shift_exchange_kernel, tuple(offsets), axis, other),
        out_shape=jax.ShapeDtypeStruct((k,) + block.shape, block.dtype),
        in_specs=[pl.BlockSpec(memory_space=vmem)],
        out_specs=pl.BlockSpec(memory_space=vmem),
        scratch_shapes=[pltpu.SemaphoreType.DMA((k,)), pltpu.SemaphoreType.DMA((k,))],
        compiler_params=pltpu.CompilerParams(collective_id=cid, has_side_effects=True),
    )(block)


def exp_all_to_all_kernel(x_ref, y_ref, send_sems, recv_sems):
    n = lax.axis_size("exp")
    me = lax.axis_index("exp")
    row = lax.axis_index("seq")
    barrier = pltpu.get_barrier_semaphore()
    for k in range(1, n):
        pl.semaphore_signal(barrier, inc=1, device_id=(row, (me + k) % n),
                            device_id_type=pl.DeviceIdType.MESH)
    pl.semaphore_wait(barrier, n - 1)
    copies = []
    for k in range(1, n):
        peer = (me + k) % n
        cp = pltpu.make_async_remote_copy(
            src_ref=x_ref.at[peer], dst_ref=y_ref.at[me],
            send_sem=send_sems.at[k - 1], recv_sem=recv_sems.at[k - 1],
            device_id=(row, peer), device_id_type=pl.DeviceIdType.MESH)
        cp.start()
        copies.append(cp)
    y_ref[me] = x_ref[me]
    for cp in copies:
        cp.wait()


def exp_all_to_all(x, cid):
    n = x.shape[0]
    vmem = pltpu.MemorySpace.VMEM
    return pl.pallas_call(
        exp_all_to_all_kernel,
        out_shape=jax.ShapeDtypeStruct(x.shape, x.dtype),
        in_specs=[pl.BlockSpec(memory_space=vmem)],
        out_specs=pl.BlockSpec(memory_space=vmem),
        scratch_shapes=[pltpu.SemaphoreType.DMA((n - 1,)), pltpu.SemaphoreType.DMA((n - 1,))],
        compiler_params=pltpu.CompilerParams(collective_id=cid, has_side_effects=True),
    )(x)


def ring_gather_kernel(nx, ny, axis, other, pieces, block_ref, out_ref, local_sem, send_sems, recv_sems):
    me = lax.axis_index(axis)
    col = lax.axis_index(other)
    x = me // ny
    y = me % ny
    rows = block_ref.shape[0]
    hr = rows // 2

    def dev(a, b):
        idx = (a + nx) % nx * ny + (b + ny) % ny
        return (idx, col) if axis == "seq" else (col, idx)

    peers = [dev(x, y + 1), dev(x, y - 1), dev(x + 1, y), dev(x - 1, y)]
    barrier = pltpu.get_barrier_semaphore()
    for peer in peers:
        pl.semaphore_signal(barrier, inc=1, device_id=peer, device_id_type=pl.DeviceIdType.MESH)
    pl.semaphore_wait(barrier, 4)

    own = pltpu.make_async_copy(block_ref, out_ref.at[x, y], local_sem.at[0])
    own.start()
    sem_count = [0]

    def unit(axis, stage, u, lo, hi):
        if axis == "y":
            return out_ref.at[x, u, lo:hi] if stage == 1 else out_ref.at[:, u, lo:hi]
        return out_ref.at[u, y, lo:hi] if stage == 1 else out_ref.at[u, :, lo:hi]

    def ring(axis, stage, lo, hi):
        n = ny if axis == "y" else nx
        c = y if axis == "y" else x
        half = n // 2
        mid = (lo + hi) // 2
        steps = []
        for sign in (1, -1):
            prev = None
            lane = []
            for k in range(half):
                u = (c - sign * k + 2 * n) % n
                a_lo, a_hi = lo, hi
                if k == half - 1 and n % 2 == 0:
                    a_lo, a_hi = (lo, mid) if sign == 1 else (mid, hi)
                if stage == 1 and k == 0:
                    src = block_ref.at[a_lo:a_hi]
                else:
                    src = unit(axis, stage, u, a_lo, a_hi)
                dst = unit(axis, stage, u, a_lo, a_hi)
                target = dev(x, y + sign) if axis == "y" else dev(x + sign, y)
                j = sem_count[0]
                sem_count[0] += 1
                cp = pltpu.make_async_remote_copy(
                    src_ref=src, dst_ref=dst, send_sem=send_sems.at[j], recv_sem=recv_sems.at[j],
                    device_id=target, device_id_type=pl.DeviceIdType.MESH)
                lane.append((prev, cp))
                prev = cp
            steps.append(lane)
        return steps

    plans = []
    step = hr // pieces
    for p in range(pieces):
        for base, first, second in ((0, "y", "x"), (hr, "x", "y")):
            lo = base + p * step
            s1 = ring(first, 1, lo, lo + step)
            s2 = ring(second, 2, lo, lo + step)
            plans.append((s1, s2))

    started = []

    def run(lane_list):
        depth = max(len(l) for l in lane_list)
        for k in range(depth):
            for lane in lane_list:
                if k < len(lane):
                    prev, cp = lane[k]
                    if prev is not None:
                        prev.wait_recv()
                    cp.start()
                    started.append(cp)

    run([lane for s1, _ in plans for lane in s1])
    for s1, _ in plans:
        for lane in s1:
            lane[-1][1].wait_recv()
    own.wait()
    run([lane for _, s2 in plans for lane in s2])
    for _, s2 in plans:
        for lane in s2:
            lane[-1][1].wait_recv()
    for cp in started:
        cp.wait_send()


def ring_gather(block, nx, ny, axis="seq", other="exp", cid=3, pieces=1):
    vmem = pltpu.MemorySpace.VMEM
    n_sems = 4 * pieces * (nx // 2 + ny // 2) + 4
    return pl.pallas_call(
        functools.partial(ring_gather_kernel, nx, ny, axis, other, pieces),
        out_shape=jax.ShapeDtypeStruct((nx, ny) + block.shape, block.dtype),
        in_specs=[pl.BlockSpec(memory_space=vmem)],
        out_specs=pl.BlockSpec(memory_space=vmem),
        scratch_shapes=[
            pltpu.SemaphoreType.DMA((1,)),
            pltpu.SemaphoreType.DMA((n_sems,)),
            pltpu.SemaphoreType.DMA((n_sems,)),
        ],
        compiler_params=pltpu.CompilerParams(
            collective_id=cid, has_side_effects=True, vmem_limit_bytes=48 * 1024 * 1024
        ),
    )(block)


def rms_scale(matrix, gain):
    mean_square = jnp.mean(matrix * matrix, axis=-1, keepdims=True)
    return matrix * lax.rsqrt(mean_square + EPSILON) * gain


def expert_terms(block, gate_slice, up_slice, down_slice):
    gate = jnp.einsum("nek,ekf->nef", block, gate_slice, preferred_element_type=jnp.float32)
    upward = jnp.einsum("nek,ekf->nef", block, up_slice, preferred_element_type=jnp.float32)
    act = (jax.nn.silu(gate) * upward).astype(jnp.bfloat16)
    return jnp.einsum("nef,ekf->nek", act, down_slice, preferred_element_type=jnp.float32)


def local(
    tokens,
    array_type,
    block_pattern,
    gain_attn,
    w_query,
    w_key,
    w_value,
    logit_scale,
    w_out,
    gain_ffn,
    w_gate,
    w_up,
    w_down,
):
    n_exp = lax.axis_size("exp")
    row_count = tokens.shape[0]
    width = tokens.shape[1]
    head_cols = w_query.shape[1]
    heads_dev = logit_scale.shape[0]
    head_size = head_cols // heads_dev
    n_blocks = block_pattern.shape[0]
    inputs = tokens.astype(jnp.float32)
    normed_attn = rms_scale(inputs, gain_attn).astype(jnp.bfloat16)
    projector = jnp.concatenate([w_query, w_key, w_value], axis=1)
    joined_qkv = jnp.dot(
        ring_gather(normed_attn, n_exp // CORES, CORES, "exp", "seq", 4, pieces=2).reshape(n_exp * row_count, width),
        projector,
        preferred_element_type=jnp.float32,
    ).astype(jnp.bfloat16)
    block_len = joined_qkv.shape[0]
    query_heads = joined_qkv[:, :head_cols].reshape(block_len, heads_dev, head_size)
    key_value = joined_qkv[:, head_cols:]
    position = lax.axis_index("seq")
    head_scale = logit_scale[:, None, None]

    offsets = [d for d in range(1, REACH + 1)] + [-d for d in range(1, REACH + 1)]
    neighbours = shift_exchange(key_value, offsets, "seq", "exp", 2)
    band = jnp.concatenate([key_value[None], neighbours], axis=0)
    n_band = band.shape[0]
    sources = jnp.stack([position] + [(position - o) % n_blocks for o in offsets])
    allowed = jnp.repeat(block_pattern[position, sources] > 0, block_len)
    key_band = band[:, :, :head_cols].reshape(n_band * block_len, heads_dev, head_size)
    value_band = band[:, :, head_cols:].reshape(n_band * block_len, heads_dev, head_size)
    scores = (
        jnp.einsum("qhd,khd->hqk", query_heads, key_band, preferred_element_type=jnp.float32)
        * head_scale
    )
    scores = jnp.where(allowed[None, None, :], scores, -jnp.inf)
    row_top = jnp.max(scores, axis=2, keepdims=True)
    weights = jnp.exp(scores - row_top)
    weight_sum = jnp.sum(weights, axis=2)
    weighted = jnp.einsum(
        "hqk,khd->qhd",
        weights.astype(jnp.bfloat16),
        value_band,
        preferred_element_type=jnp.float32,
    )
    heads_out = (
        (weighted / jnp.transpose(weight_sum)[:, :, None])
        .astype(jnp.bfloat16)
        .reshape(block_len, head_cols)
    )
    all_heads = lax.all_to_all(heads_out, "exp", split_axis=0, concat_axis=1, tiled=True)
    attn_out = jnp.dot(
        all_heads,
        lax.all_gather(w_out, "exp", axis=0, tiled=True),
        preferred_element_type=jnp.float32,
    )
    hidden_state = inputs + attn_out
    normed_ffn = rms_scale(hidden_state, gain_ffn).astype(jnp.bfloat16)
    experts_dev = w_gate.shape[0]
    n_total = experts_dev * n_exp
    capacity = 2 * row_count // n_total
    one_hot = (array_type[:, None] == jnp.arange(n_total, dtype=jnp.int32)[None, :]).astype(
        jnp.int32
    )
    slot_rank = jnp.sum(jnp.cumsum(one_hot, axis=0) * one_hot, axis=1) - 1
    owner = array_type // experts_dev
    local_expert = array_type % experts_dev
    slot_id = (owner * capacity + slot_rank) * experts_dev + local_expert
    n_slots = n_exp * capacity * experts_dev
    selector = (slot_id[None, :] == jnp.arange(n_slots, dtype=jnp.int32)[:, None]).astype(
        jnp.bfloat16
    )
    outgoing = jnp.dot(selector, normed_ffn, preferred_element_type=jnp.float32).astype(
        jnp.bfloat16
    )
    outgoing = outgoing.reshape(n_exp * capacity, experts_dev, width)
    arrived = lax.all_to_all(outgoing, "exp", split_axis=0, concat_axis=0, tiled=True)
    n_seq = lax.axis_size("seq")
    y_size = Y_RING if n_seq % Y_RING == 0 else n_seq
    gathered = ring_gather(
        arrived.reshape(arrived.shape[0], width), n_seq // y_size, y_size, pieces=2
    ).reshape((n_seq * arrived.shape[0],) + arrived.shape[1:])
    n_seq = lax.axis_size("seq")
    y_size = Y_RING if n_seq % Y_RING == 0 else n_seq
    summed = ring_ffn(
        gathered.reshape(gathered.shape[0], width),
        w_gate[0], w_up[0], w_down[0], n_seq // y_size, y_size, splits=4,
    ).reshape((-1,) + gathered.shape[1:])
    returned = lax.all_to_all(summed, "exp", split_axis=0, concat_axis=0, tiled=True)
    expert_out = jnp.dot(
        jnp.transpose(selector),
        returned.reshape(n_slots, width),
        preferred_element_type=jnp.float32,
    )
    return (hidden_state + expert_out).astype(jnp.bfloat16)


def solution(mesh):
    return jax.shard_map(
        local,
        mesh=mesh,
        in_specs=(
            P(("seq", "exp"), None),
            P(("seq", "exp")),
            P(),
            P(),
            P(None, "exp"),
            P(None, "exp"),
            P(None, "exp"),
            P("exp"),
            P("exp", None),
            P(),
            P("exp", None, "seq"),
            P("exp", None, "seq"),
            P("exp", None, "seq"),
        ),
        out_specs=P(("seq", "exp"), None),
        check_vma=False,
    )
```

```python
import jax
import jax.numpy as jnp
from jax import lax
from jax.sharding import PartitionSpec as P
from jax.experimental import pallas as pl
from jax.experimental.pallas import tpu as pltpu
import functools

REACH = 3
Y_RING = 8
CORES = 2


EPSILON = 1e-05


def passed_along(block, axis, distance):
    devices = range(lax.axis_size(axis))
    route = [((i - distance) % len(devices), i) for i in devices]
    return lax.ppermute(block, axis, route)


def ring_reduce_kernel(nx, ny, splits, part_ref, out_ref, recv1, send1, acc, recv2, send2,
                       s1_send, s1_recv, s2_send, s2_recv):
    me = lax.axis_index("seq")
    col = lax.axis_index("exp")
    x = me // ny
    y = me % ny
    y_up = x * ny + (y + 1) % ny
    y_down = x * ny + (y + ny - 1) % ny
    x_up = ((x + 1) % nx) * ny + y
    x_down = ((x + nx - 1) % nx) * ny + y
    rows = part_ref.shape[2]
    piece = rows // splits
    quarter = rows // 4

    barrier = pltpu.get_barrier_semaphore()
    for peer in (y_up, y_down, x_up, x_down):
        pl.semaphore_signal(barrier, inc=1, device_id=(peer, col),
                            device_id_type=pl.DeviceIdType.MESH)
    pl.semaphore_wait(barrier, 4)

    lanes = []
    for a in range(nx):
        for p in range(splits):
            if a < nx // 2:
                lanes.append((y_up, 1, a, p * piece))
            else:
                lanes.append((y_down, -1, a, p * piece))
    copies1 = []
    for k in range(ny - 1):
        step_copies = []
        for d, (peer, sign, a, r0) in enumerate(lanes):
            c = (y - sign * (k + 1) + 2 * ny) % ny
            if k == 0:
                src = part_ref.at[a, c, r0:r0 + piece]
            else:
                copies1[k - 1][d].wait_recv()
                send1[d, k] = (recv1[d, k - 1].astype(jnp.float32)
                               + part_ref[a, c, r0:r0 + piece].astype(jnp.float32)).astype(send1.dtype)
                src = send1.at[d, k]
            cp = pltpu.make_async_remote_copy(
                src_ref=src, dst_ref=recv1.at[d, k],
                send_sem=s1_send.at[d, k], recv_sem=s1_recv.at[d, k],
                device_id=(peer, col), device_id_type=pl.DeviceIdType.MESH)
            cp.start()
            step_copies.append(cp)
        copies1.append(step_copies)
    for d, (peer, sign, a, r0) in enumerate(lanes):
        copies1[ny - 2][d].wait_recv()
        acc[a, r0:r0 + piece] = (recv1[d, ny - 2].astype(jnp.float32)
                                 + part_ref[a, y, r0:r0 + piece].astype(jnp.float32))

    lanes2 = [(x_up, 1, 0), (x_up, 1, quarter), (x_down, -1, 2 * quarter), (x_down, -1, 3 * quarter)]
    copies2 = []
    for k in range(nx - 1):
        step_copies = []
        for d, (peer, sign, r0) in enumerate(lanes2):
            c = (x - sign * (k + 1) + 2 * nx) % nx
            if k == 0:
                src = acc.at[c, r0:r0 + quarter]
            else:
                copies2[k - 1][d].wait_recv()
                send2[d, k] = recv2[d, k - 1] + acc[c, r0:r0 + quarter]
                src = send2.at[d, k]
            cp = pltpu.make_async_remote_copy(
                src_ref=src, dst_ref=recv2.at[d, k],
                send_sem=s2_send.at[d, k], recv_sem=s2_recv.at[d, k],
                device_id=(peer, col), device_id_type=pl.DeviceIdType.MESH)
            cp.start()
            step_copies.append(cp)
        copies2.append(step_copies)
    for d, (peer, sign, r0) in enumerate(lanes2):
        copies2[nx - 2][d].wait_recv()
        out_ref[r0:r0 + quarter] = (recv2[d, nx - 2] + acc[x, r0:r0 + quarter]).astype(out_ref.dtype)
    for step_copies in copies1 + copies2:
        for cp in step_copies:
            cp.wait_send()


def ring_reduce(part, nx, ny, splits=2):
    width = part.shape[-1]
    rows = part.shape[0] // (nx * ny)
    part = part.reshape(nx, ny, rows, width)
    n1 = nx * splits
    vmem = pltpu.MemorySpace.VMEM
    return pl.pallas_call(
        functools.partial(ring_reduce_kernel, nx, ny, splits),
        out_shape=jax.ShapeDtypeStruct((rows, width), jnp.bfloat16),
        in_specs=[pl.BlockSpec(memory_space=vmem)],
        out_specs=pl.BlockSpec(memory_space=vmem),
        scratch_shapes=[
            pltpu.VMEM((n1, ny - 1, rows // splits, width), jnp.bfloat16),
            pltpu.VMEM((n1, ny - 1, rows // splits, width), jnp.bfloat16),
            pltpu.VMEM((nx, rows, width), jnp.float32),
            pltpu.VMEM((4, nx - 1, rows // 4, width), jnp.float32),
            pltpu.VMEM((4, nx - 1, rows // 4, width), jnp.float32),
            pltpu.SemaphoreType.DMA((n1, ny - 1)),
            pltpu.SemaphoreType.DMA((n1, ny - 1)),
            pltpu.SemaphoreType.DMA((4, nx - 1)),
            pltpu.SemaphoreType.DMA((4, nx - 1)),
        ],
        compiler_params=pltpu.CompilerParams(
            collective_id=1, has_side_effects=True, vmem_limit_bytes=48 * 1024 * 1024
        ),
    )(part)


def ring_ffn_kernel(nx, ny, splits, tok_ref, wg_ref, wu_ref, wd_ref, out_ref, ret_ref, pbuf, recv1, send1,
                    acc, recv2, send2, s1_send, s1_recv, s2_send, s2_recv, r_send, r_recv):
    me = lax.axis_index("seq")
    col = lax.axis_index("exp")
    x = me // ny
    y = me % ny
    y_up = x * ny + (y + 1) % ny
    y_down = x * ny + (y + ny - 1) % ny
    x_up = ((x + 1) % nx) * ny + y
    x_down = ((x + nx - 1) % nx) * ny + y
    rows = tok_ref.shape[2]
    width = tok_ref.shape[3]
    piece = rows // splits
    quarter = rows // 4
    half_x = nx // 2

    def partials(c_up, c_down):
        tok = jnp.concatenate(
            [tok_ref[0:half_x, c_up].reshape(half_x * rows, width),
             tok_ref[half_x:nx, c_down].reshape((nx - half_x) * rows, width)], axis=0)
        gate = jnp.dot(tok, wg_ref[...], preferred_element_type=jnp.float32)
        upward = jnp.dot(tok, wu_ref[...], preferred_element_type=jnp.float32)
        act = (gate / (1.0 + jnp.exp(-gate)) * upward).astype(jnp.bfloat16)
        down = lax.dot_general(act, wd_ref[...], (((1,), (1,)), ((), ())),
                               preferred_element_type=jnp.float32)
        pbuf[...] = down.astype(jnp.bfloat16).reshape(nx, rows, width)

    n_exp = lax.axis_size("exp")
    group = rows // n_exp
    barrier = pltpu.get_barrier_semaphore()
    for peer in (y_up, y_down, x_up, x_down):
        pl.semaphore_signal(barrier, inc=1, device_id=(peer, col),
                            device_id_type=pl.DeviceIdType.MESH)
    for k in range(1, n_exp):
        pl.semaphore_signal(barrier, inc=1, device_id=(me, (col + k) % n_exp),
                            device_id_type=pl.DeviceIdType.MESH)
    pl.semaphore_wait(barrier, 4 + n_exp - 1)

    lanes = []
    for a in range(nx):
        for p in range(splits):
            if a < half_x:
                lanes.append((y_up, 1, a, p * piece))
            else:
                lanes.append((y_down, -1, a, p * piece))
    copies1 = []
    for k in range(ny - 1):
        partials((y - k - 1 + ny) % ny, (y + k + 1) % ny)
        step_copies = []
        for d, (peer, sign, a, r0) in enumerate(lanes):
            if k == 0:
                send1[d, k] = pbuf[a, r0:r0 + piece]
            else:
                copies1[k - 1][d].wait_recv()
                send1[d, k] = (recv1[d, k - 1].astype(jnp.float32)
                               + pbuf[a, r0:r0 + piece].astype(jnp.float32)).astype(send1.dtype)
            cp = pltpu.make_async_remote_copy(
                src_ref=send1.at[d, k], dst_ref=recv1.at[d, k],
                send_sem=s1_send.at[d, k], recv_sem=s1_recv.at[d, k],
                device_id=(peer, col), device_id_type=pl.DeviceIdType.MESH)
            cp.start()
            step_copies.append(cp)
        copies1.append(step_copies)
    partials(y, y)
    for d, (peer, sign, a, r0) in enumerate(lanes):
        copies1[ny - 2][d].wait_recv()
        acc[a, r0:r0 + piece] = (recv1[d, ny - 2].astype(jnp.float32)
                                 + pbuf[a, r0:r0 + piece].astype(jnp.float32))

    lanes2 = [(x_up, 1, 0), (x_up, 1, quarter), (x_down, -1, 2 * quarter), (x_down, -1, 3 * quarter)]
    copies2 = []
    for k in range(nx - 1):
        step_copies = []
        for d, (peer, sign, r0) in enumerate(lanes2):
            c = (x - sign * (k + 1) + 2 * nx) % nx
            if k == 0:
                src = acc.at[c, r0:r0 + quarter]
            else:
                copies2[k - 1][d].wait_recv()
                send2[d, k] = recv2[d, k - 1] + acc[c, r0:r0 + quarter]
                src = send2.at[d, k]
            cp = pltpu.make_async_remote_copy(
                src_ref=src, dst_ref=recv2.at[d, k],
                send_sem=s2_send.at[d, k], recv_sem=s2_recv.at[d, k],
                device_id=(peer, col), device_id_type=pl.DeviceIdType.MESH)
            cp.start()
            step_copies.append(cp)
        copies2.append(step_copies)
    for d, (peer, sign, r0) in enumerate(lanes2):
        copies2[nx - 2][d].wait_recv()
        out_ref[r0:r0 + quarter] = (recv2[d, nx - 2] + acc[x, r0:r0 + quarter]).astype(out_ref.dtype)
    back = []
    for k in range(1, n_exp):
        peer = (col + k) % n_exp
        cp = pltpu.make_async_remote_copy(
            src_ref=out_ref.at[pl.ds(peer * group, group)], dst_ref=ret_ref.at[col],
            send_sem=r_send.at[k - 1], recv_sem=r_recv.at[k - 1],
            device_id=(me, peer), device_id_type=pl.DeviceIdType.MESH)
        cp.start()
        back.append(cp)
    own = pltpu.make_async_copy(out_ref.at[pl.ds(col * group, group)], ret_ref.at[col], r_send.at[n_exp - 1])
    own.start()
    own.wait()
    for step_copies in copies1 + copies2:
        for cp in step_copies:
            cp.wait_send()
    for cp in back:
        cp.wait()


def ring_ffn(tokens, w_gate, w_up, w_down, nx, ny, n_exp, splits=2):
    width = tokens.shape[-1]
    rows = tokens.shape[0] // (nx * ny)
    tokens = tokens.reshape(nx, ny, rows, width)
    n1 = nx * splits
    vmem = pltpu.MemorySpace.VMEM
    return pl.pallas_call(
        functools.partial(ring_ffn_kernel, nx, ny, splits),
        out_shape=(jax.ShapeDtypeStruct((rows, width), jnp.bfloat16),
                   jax.ShapeDtypeStruct((n_exp, rows // n_exp, width), jnp.bfloat16)),
        in_specs=[pl.BlockSpec(memory_space=vmem)] * 4,
        out_specs=(pl.BlockSpec(memory_space=vmem), pl.BlockSpec(memory_space=vmem)),
        scratch_shapes=[
            pltpu.VMEM((nx, rows, width), jnp.bfloat16),
            pltpu.VMEM((n1, ny - 1, rows // splits, width), jnp.bfloat16),
            pltpu.VMEM((n1, ny - 1, rows // splits, width), jnp.bfloat16),
            pltpu.VMEM((nx, rows, width), jnp.float32),
            pltpu.VMEM((4, nx - 1, rows // 4, width), jnp.float32),
            pltpu.VMEM((4, nx - 1, rows // 4, width), jnp.float32),
            pltpu.SemaphoreType.DMA((n1, ny - 1)),
            pltpu.SemaphoreType.DMA((n1, ny - 1)),
            pltpu.SemaphoreType.DMA((4, nx - 1)),
            pltpu.SemaphoreType.DMA((4, nx - 1)),
            pltpu.SemaphoreType.DMA((n_exp,)),
            pltpu.SemaphoreType.DMA((n_exp - 1,)),
        ],
        compiler_params=pltpu.CompilerParams(
            collective_id=5, has_side_effects=True, vmem_limit_bytes=56 * 1024 * 1024
        ),
    )(tokens, w_gate, w_up, w_down)


def shift_exchange_kernel(offsets, axis, other, block_ref, out_ref, send_sems, recv_sems):
    n = lax.axis_size(axis)
    me = lax.axis_index(axis)
    col = lax.axis_index(other)

    def dev(peer):
        return (peer, col) if axis == "seq" else (col, peer)

    targets = [(me + o + n * len(offsets)) % n for o in offsets]
    barrier = pltpu.get_barrier_semaphore()
    for peer in targets:
        pl.semaphore_signal(barrier, inc=1, device_id=dev(peer),
                            device_id_type=pl.DeviceIdType.MESH)
    pl.semaphore_wait(barrier, len(offsets))
    copies = []
    for j, peer in enumerate(targets):
        cp = pltpu.make_async_remote_copy(
            src_ref=block_ref, dst_ref=out_ref.at[j],
            send_sem=send_sems.at[j], recv_sem=recv_sems.at[j],
            device_id=dev(peer), device_id_type=pl.DeviceIdType.MESH)
        cp.start()
        copies.append(cp)
    for cp in copies:
        cp.wait()


def shift_exchange(block, offsets, axis, other, cid):
    vmem = pltpu.MemorySpace.VMEM
    k = len(offsets)
    return pl.pallas_call(
        functools.partial(shift_exchange_kernel, tuple(offsets), axis, other),
        out_shape=jax.ShapeDtypeStruct((k,) + block.shape, block.dtype),
        in_specs=[pl.BlockSpec(memory_space=vmem)],
        out_specs=pl.BlockSpec(memory_space=vmem),
        scratch_shapes=[pltpu.SemaphoreType.DMA((k,)), pltpu.SemaphoreType.DMA((k,))],
        compiler_params=pltpu.CompilerParams(collective_id=cid, has_side_effects=True),
    )(block)


def exp_all_to_all_kernel(x_ref, y_ref, send_sems, recv_sems):
    n = lax.axis_size("exp")
    me = lax.axis_index("exp")
    row = lax.axis_index("seq")
    barrier = pltpu.get_barrier_semaphore()
    for k in range(1, n):
        pl.semaphore_signal(barrier, inc=1, device_id=(row, (me + k) % n),
                            device_id_type=pl.DeviceIdType.MESH)
    pl.semaphore_wait(barrier, n - 1)
    copies = []
    for k in range(1, n):
        peer = (me + k) % n
        cp = pltpu.make_async_remote_copy(
            src_ref=x_ref.at[peer], dst_ref=y_ref.at[me],
            send_sem=send_sems.at[k - 1], recv_sem=recv_sems.at[k - 1],
            device_id=(row, peer), device_id_type=pl.DeviceIdType.MESH)
        cp.start()
        copies.append(cp)
    y_ref[me] = x_ref[me]
    for cp in copies:
        cp.wait()


def exp_all_to_all(x, cid):
    n = x.shape[0]
    vmem = pltpu.MemorySpace.VMEM
    return pl.pallas_call(
        exp_all_to_all_kernel,
        out_shape=jax.ShapeDtypeStruct(x.shape, x.dtype),
        in_specs=[pl.BlockSpec(memory_space=vmem)],
        out_specs=pl.BlockSpec(memory_space=vmem),
        scratch_shapes=[pltpu.SemaphoreType.DMA((n - 1,)), pltpu.SemaphoreType.DMA((n - 1,))],
        compiler_params=pltpu.CompilerParams(collective_id=cid, has_side_effects=True),
    )(x)


def ring_gather_kernel(nx, ny, axis, other, pieces, block_ref, out_ref, local_sem, send_sems, recv_sems):
    me = lax.axis_index(axis)
    col = lax.axis_index(other)
    x = me // ny
    y = me % ny
    rows = block_ref.shape[0]
    hr = rows // 2

    def dev(a, b):
        idx = (a + nx) % nx * ny + (b + ny) % ny
        return (idx, col) if axis == "seq" else (col, idx)

    peers = [dev(x, y + 1), dev(x, y - 1), dev(x + 1, y), dev(x - 1, y)]
    barrier = pltpu.get_barrier_semaphore()
    for peer in peers:
        pl.semaphore_signal(barrier, inc=1, device_id=peer, device_id_type=pl.DeviceIdType.MESH)
    pl.semaphore_wait(barrier, 4)

    own = pltpu.make_async_copy(block_ref, out_ref.at[x, y], local_sem.at[0])
    own.start()
    sem_count = [0]

    def unit(axis, stage, u, lo, hi):
        if axis == "y":
            return out_ref.at[x, u, lo:hi] if stage == 1 else out_ref.at[:, u, lo:hi]
        return out_ref.at[u, y, lo:hi] if stage == 1 else out_ref.at[u, :, lo:hi]

    def ring(axis, stage, lo, hi):
        n = ny if axis == "y" else nx
        c = y if axis == "y" else x
        half = n // 2
        mid = (lo + hi) // 2
        steps = []
        for sign in (1, -1):
            prev = None
            lane = []
            for k in range(half):
                u = (c - sign * k + 2 * n) % n
                a_lo, a_hi = lo, hi
                if k == half - 1 and n % 2 == 0:
                    a_lo, a_hi = (lo, mid) if sign == 1 else (mid, hi)
                if stage == 1 and k == 0:
                    src = block_ref.at[a_lo:a_hi]
                else:
                    src = unit(axis, stage, u, a_lo, a_hi)
                dst = unit(axis, stage, u, a_lo, a_hi)
                target = dev(x, y + sign) if axis == "y" else dev(x + sign, y)
                j = sem_count[0]
                sem_count[0] += 1
                cp = pltpu.make_async_remote_copy(
                    src_ref=src, dst_ref=dst, send_sem=send_sems.at[j], recv_sem=recv_sems.at[j],
                    device_id=target, device_id_type=pl.DeviceIdType.MESH)
                lane.append((prev, cp))
                prev = cp
            steps.append(lane)
        return steps

    plans = []
    step = hr // pieces
    for p in range(pieces):
        for base, first, second in ((0, "y", "x"), (hr, "x", "y")):
            lo = base + p * step
            s1 = ring(first, 1, lo, lo + step)
            s2 = ring(second, 2, lo, lo + step)
            plans.append((s1, s2))

    started = []

    def run(lane_list):
        depth = max(len(l) for l in lane_list)
        for k in range(depth):
            for lane in lane_list:
                if k < len(lane):
                    prev, cp = lane[k]
                    if prev is not None:
                        prev.wait_recv()
                    cp.start()
                    started.append(cp)

    run([lane for s1, _ in plans for lane in s1])
    for s1, _ in plans:
        for lane in s1:
            lane[-1][1].wait_recv()
    own.wait()
    run([lane for _, s2 in plans for lane in s2])
    for _, s2 in plans:
        for lane in s2:
            lane[-1][1].wait_recv()
    for cp in started:
        cp.wait_send()


def ring_gather(block, nx, ny, axis="seq", other="exp", cid=3, pieces=1):
    vmem = pltpu.MemorySpace.VMEM
    n_sems = 4 * pieces * (nx // 2 + ny // 2) + 4
    return pl.pallas_call(
        functools.partial(ring_gather_kernel, nx, ny, axis, other, pieces),
        out_shape=jax.ShapeDtypeStruct((nx, ny) + block.shape, block.dtype),
        in_specs=[pl.BlockSpec(memory_space=vmem)],
        out_specs=pl.BlockSpec(memory_space=vmem),
        scratch_shapes=[
            pltpu.SemaphoreType.DMA((1,)),
            pltpu.SemaphoreType.DMA((n_sems,)),
            pltpu.SemaphoreType.DMA((n_sems,)),
        ],
        compiler_params=pltpu.CompilerParams(
            collective_id=cid, has_side_effects=True, vmem_limit_bytes=48 * 1024 * 1024
        ),
    )(block)


def rms_scale(matrix, gain):
    mean_square = jnp.mean(matrix * matrix, axis=-1, keepdims=True)
    return matrix * lax.rsqrt(mean_square + EPSILON) * gain


def expert_terms(block, gate_slice, up_slice, down_slice):
    gate = jnp.einsum("nek,ekf->nef", block, gate_slice, preferred_element_type=jnp.float32)
    upward = jnp.einsum("nek,ekf->nef", block, up_slice, preferred_element_type=jnp.float32)
    act = (jax.nn.silu(gate) * upward).astype(jnp.bfloat16)
    return jnp.einsum("nef,ekf->nek", act, down_slice, preferred_element_type=jnp.float32)


def local(
    tokens,
    array_type,
    block_pattern,
    gain_attn,
    w_query,
    w_key,
    w_value,
    logit_scale,
    w_out,
    gain_ffn,
    w_gate,
    w_up,
    w_down,
):
    n_exp = lax.axis_size("exp")
    row_count = tokens.shape[0]
    width = tokens.shape[1]
    head_cols = w_query.shape[1]
    heads_dev = logit_scale.shape[0]
    head_size = head_cols // heads_dev
    n_blocks = block_pattern.shape[0]
    inputs = tokens.astype(jnp.float32)
    normed_attn = rms_scale(inputs, gain_attn).astype(jnp.bfloat16)
    projector = jnp.concatenate([w_query, w_key, w_value], axis=1)
    joined_qkv = jnp.dot(
        ring_gather(normed_attn, n_exp // CORES, CORES, "exp", "seq", 4, pieces=2).reshape(n_exp * row_count, width),
        projector,
        preferred_element_type=jnp.float32,
    ).astype(jnp.bfloat16)
    block_len = joined_qkv.shape[0]
    query_heads = joined_qkv[:, :head_cols].reshape(block_len, heads_dev, head_size)
    key_value = joined_qkv[:, head_cols:]
    position = lax.axis_index("seq")
    head_scale = logit_scale[:, None, None]

    offsets = [d for d in range(1, REACH + 1)] + [-d for d in range(1, REACH + 1)]
    neighbours = shift_exchange(key_value, offsets, "seq", "exp", 2)
    band = jnp.concatenate([key_value[None], neighbours], axis=0)
    n_band = band.shape[0]
    sources = jnp.stack([position] + [(position - o) % n_blocks for o in offsets])
    allowed = jnp.repeat(block_pattern[position, sources] > 0, block_len)
    key_band = band[:, :, :head_cols].reshape(n_band * block_len, heads_dev, head_size)
    value_band = band[:, :, head_cols:].reshape(n_band * block_len, heads_dev, head_size)
    scores = (
        jnp.einsum("qhd,khd->hqk", query_heads, key_band, preferred_element_type=jnp.float32)
        * head_scale
    )
    scores = jnp.where(allowed[None, None, :], scores, -jnp.inf)
    row_top = jnp.max(scores, axis=2, keepdims=True)
    weights = jnp.exp(scores - row_top)
    weight_sum = jnp.sum(weights, axis=2)
    weighted = jnp.einsum(
        "hqk,khd->qhd",
        weights.astype(jnp.bfloat16),
        value_band,
        preferred_element_type=jnp.float32,
    )
    heads_out = (
        (weighted / jnp.transpose(weight_sum)[:, :, None])
        .astype(jnp.bfloat16)
        .reshape(block_len, head_cols)
    )
    all_heads = lax.all_to_all(heads_out, "exp", split_axis=0, concat_axis=1, tiled=True)
    attn_out = jnp.dot(
        all_heads,
        lax.all_gather(w_out, "exp", axis=0, tiled=True),
        preferred_element_type=jnp.float32,
    )
    hidden_state = inputs + attn_out
    normed_ffn = rms_scale(hidden_state, gain_ffn).astype(jnp.bfloat16)
    experts_dev = w_gate.shape[0]
    n_total = experts_dev * n_exp
    capacity = 2 * row_count // n_total
    one_hot = (array_type[:, None] == jnp.arange(n_total, dtype=jnp.int32)[None, :]).astype(
        jnp.int32
    )
    slot_rank = jnp.sum(jnp.cumsum(one_hot, axis=0) * one_hot, axis=1) - 1
    owner = array_type // experts_dev
    local_expert = array_type % experts_dev
    slot_id = (owner * capacity + slot_rank) * experts_dev + local_expert
    n_slots = n_exp * capacity * experts_dev
    selector = (slot_id[None, :] == jnp.arange(n_slots, dtype=jnp.int32)[:, None]).astype(
        jnp.bfloat16
    )
    outgoing = jnp.dot(selector, normed_ffn, preferred_element_type=jnp.float32).astype(
        jnp.bfloat16
    )
    outgoing = outgoing.reshape(n_exp * capacity, experts_dev, width)
    arrived = lax.all_to_all(outgoing, "exp", split_axis=0, concat_axis=0, tiled=True)
    n_seq = lax.axis_size("seq")
    y_size = Y_RING if n_seq % Y_RING == 0 else n_seq
    gathered = ring_gather(
        arrived.reshape(arrived.shape[0], width), n_seq // y_size, y_size, pieces=2
    ).reshape((n_seq * arrived.shape[0],) + arrived.shape[1:])
    n_seq = lax.axis_size("seq")
    y_size = Y_RING if n_seq % Y_RING == 0 else n_seq
    returned = ring_ffn(
        gathered.reshape(gathered.shape[0], width),
        w_gate[0], w_up[0], w_down[0], n_seq // y_size, y_size, n_exp,
    )[1].reshape((-1,) + gathered.shape[1:])
    expert_out = jnp.dot(
        jnp.transpose(selector),
        returned.reshape(n_slots, width),
        preferred_element_type=jnp.float32,
    )
    return (hidden_state + expert_out).astype(jnp.bfloat16)


def solution(mesh):
    return jax.shard_map(
        local,
        mesh=mesh,
        in_specs=(
            P(("seq", "exp"), None),
            P(("seq", "exp")),
            P(),
            P(),
            P(None, "exp"),
            P(None, "exp"),
            P(None, "exp"),
            P("exp"),
            P("exp", None),
            P(),
            P("exp", None, "seq"),
            P("exp", None, "seq"),
            P("exp", None, "seq"),
        ),
        out_specs=P(("seq", "exp"), None),
        check_vma=False,
    )
```

```python
import jax
import jax.numpy as jnp
from jax import lax
from jax.sharding import PartitionSpec as P
from jax.experimental import pallas as pl
from jax.experimental.pallas import tpu as pltpu
import functools

REACH = 3
Y_RING = 8
CORES = 2


EPSILON = 1e-05


def passed_along(block, axis, distance):
    devices = range(lax.axis_size(axis))
    route = [((i - distance) % len(devices), i) for i in devices]
    return lax.ppermute(block, axis, route)


def ring_reduce_kernel(nx, ny, splits, part_ref, out_ref, recv1, send1, acc, recv2, send2,
                       s1_send, s1_recv, s2_send, s2_recv):
    me = lax.axis_index("seq")
    col = lax.axis_index("exp")
    x = me // ny
    y = me % ny
    y_up = x * ny + (y + 1) % ny
    y_down = x * ny + (y + ny - 1) % ny
    x_up = ((x + 1) % nx) * ny + y
    x_down = ((x + nx - 1) % nx) * ny + y
    rows = part_ref.shape[2]
    piece = rows // splits
    quarter = rows // 4

    barrier = pltpu.get_barrier_semaphore()
    for peer in (y_up, y_down, x_up, x_down):
        pl.semaphore_signal(barrier, inc=1, device_id=(peer, col),
                            device_id_type=pl.DeviceIdType.MESH)
    pl.semaphore_wait(barrier, 4)

    lanes = []
    for a in range(nx):
        for p in range(splits):
            if a < nx // 2:
                lanes.append((y_up, 1, a, p * piece))
            else:
                lanes.append((y_down, -1, a, p * piece))
    copies1 = []
    for k in range(ny - 1):
        step_copies = []
        for d, (peer, sign, a, r0) in enumerate(lanes):
            c = (y - sign * (k + 1) + 2 * ny) % ny
            if k == 0:
                src = part_ref.at[a, c, r0:r0 + piece]
            else:
                copies1[k - 1][d].wait_recv()
                send1[d, k] = (recv1[d, k - 1].astype(jnp.float32)
                               + part_ref[a, c, r0:r0 + piece].astype(jnp.float32)).astype(send1.dtype)
                src = send1.at[d, k]
            cp = pltpu.make_async_remote_copy(
                src_ref=src, dst_ref=recv1.at[d, k],
                send_sem=s1_send.at[d, k], recv_sem=s1_recv.at[d, k],
                device_id=(peer, col), device_id_type=pl.DeviceIdType.MESH)
            cp.start()
            step_copies.append(cp)
        copies1.append(step_copies)
    for d, (peer, sign, a, r0) in enumerate(lanes):
        copies1[ny - 2][d].wait_recv()
        acc[a, r0:r0 + piece] = (recv1[d, ny - 2].astype(jnp.float32)
                                 + part_ref[a, y, r0:r0 + piece].astype(jnp.float32))

    lanes2 = [(x_up, 1, 0), (x_up, 1, quarter), (x_down, -1, 2 * quarter), (x_down, -1, 3 * quarter)]
    copies2 = []
    for k in range(nx - 1):
        step_copies = []
        for d, (peer, sign, r0) in enumerate(lanes2):
            c = (x - sign * (k + 1) + 2 * nx) % nx
            if k == 0:
                src = acc.at[c, r0:r0 + quarter]
            else:
                copies2[k - 1][d].wait_recv()
                send2[d, k] = recv2[d, k - 1] + acc[c, r0:r0 + quarter]
                src = send2.at[d, k]
            cp = pltpu.make_async_remote_copy(
                src_ref=src, dst_ref=recv2.at[d, k],
                send_sem=s2_send.at[d, k], recv_sem=s2_recv.at[d, k],
                device_id=(peer, col), device_id_type=pl.DeviceIdType.MESH)
            cp.start()
            step_copies.append(cp)
        copies2.append(step_copies)
    for d, (peer, sign, r0) in enumerate(lanes2):
        copies2[nx - 2][d].wait_recv()
        out_ref[r0:r0 + quarter] = (recv2[d, nx - 2] + acc[x, r0:r0 + quarter]).astype(out_ref.dtype)
    for step_copies in copies1 + copies2:
        for cp in step_copies:
            cp.wait_send()


def ring_reduce(part, nx, ny, splits=2):
    width = part.shape[-1]
    rows = part.shape[0] // (nx * ny)
    part = part.reshape(nx, ny, rows, width)
    n1 = nx * splits
    vmem = pltpu.MemorySpace.VMEM
    return pl.pallas_call(
        functools.partial(ring_reduce_kernel, nx, ny, splits),
        out_shape=jax.ShapeDtypeStruct((rows, width), jnp.bfloat16),
        in_specs=[pl.BlockSpec(memory_space=vmem)],
        out_specs=pl.BlockSpec(memory_space=vmem),
        scratch_shapes=[
            pltpu.VMEM((n1, ny - 1, rows // splits, width), jnp.bfloat16),
            pltpu.VMEM((n1, ny - 1, rows // splits, width), jnp.bfloat16),
            pltpu.VMEM((nx, rows, width), jnp.float32),
            pltpu.VMEM((4, nx - 1, rows // 4, width), jnp.float32),
            pltpu.VMEM((4, nx - 1, rows // 4, width), jnp.float32),
            pltpu.SemaphoreType.DMA((n1, ny - 1)),
            pltpu.SemaphoreType.DMA((n1, ny - 1)),
            pltpu.SemaphoreType.DMA((4, nx - 1)),
            pltpu.SemaphoreType.DMA((4, nx - 1)),
        ],
        compiler_params=pltpu.CompilerParams(
            collective_id=1, has_side_effects=True, vmem_limit_bytes=48 * 1024 * 1024
        ),
    )(part)


def ring_ffn_kernel(nx, ny, splits, tok_ref, wg_ref, wu_ref, wd_ref, out_ref, ret_ref, pbuf, recv1, send1,
                    acc, recv2, send2, s1_send, s1_recv, s2_send, s2_recv, r_send, r_recv):
    me = lax.axis_index("seq")
    col = lax.axis_index("exp")
    x = me // ny
    y = me % ny
    y_up = x * ny + (y + 1) % ny
    y_down = x * ny + (y + ny - 1) % ny
    x_up = ((x + 1) % nx) * ny + y
    x_down = ((x + nx - 1) % nx) * ny + y
    rows = tok_ref.shape[2]
    width = tok_ref.shape[3]
    piece = rows // splits
    quarter = rows // 4
    half_x = nx // 2

    def partials(c_up, c_down):
        tok = jnp.concatenate(
            [tok_ref[0:half_x, c_up].reshape(half_x * rows, width),
             tok_ref[half_x:nx, c_down].reshape((nx - half_x) * rows, width)], axis=0)
        gate = jnp.dot(tok, wg_ref[...], preferred_element_type=jnp.float32)
        upward = jnp.dot(tok, wu_ref[...], preferred_element_type=jnp.float32)
        act = (gate / (1.0 + jnp.exp(-gate)) * upward).astype(jnp.bfloat16)
        down = lax.dot_general(act, wd_ref[...], (((1,), (1,)), ((), ())),
                               preferred_element_type=jnp.float32)
        pbuf[...] = down.astype(jnp.bfloat16).reshape(nx, rows, width)

    n_exp = lax.axis_size("exp")
    group = rows // n_exp
    barrier = pltpu.get_barrier_semaphore()
    for peer in (y_up, y_down, x_up, x_down):
        pl.semaphore_signal(barrier, inc=1, device_id=(peer, col),
                            device_id_type=pl.DeviceIdType.MESH)
    for k in range(1, n_exp):
        pl.semaphore_signal(barrier, inc=1, device_id=(me, (col + k) % n_exp),
                            device_id_type=pl.DeviceIdType.MESH)
    pl.semaphore_wait(barrier, 4 + n_exp - 1)

    lanes = []
    for a in range(nx):
        for p in range(splits):
            if a < half_x:
                lanes.append((y_up, 1, a, p * piece))
            else:
                lanes.append((y_down, -1, a, p * piece))
    copies1 = []
    for k in range(ny - 1):
        partials((y - k - 1 + ny) % ny, (y + k + 1) % ny)
        step_copies = []
        for d, (peer, sign, a, r0) in enumerate(lanes):
            if k == 0:
                send1[d, k] = pbuf[a, r0:r0 + piece]
            else:
                copies1[k - 1][d].wait_recv()
                send1[d, k] = (recv1[d, k - 1].astype(jnp.float32)
                               + pbuf[a, r0:r0 + piece].astype(jnp.float32)).astype(send1.dtype)
            cp = pltpu.make_async_remote_copy(
                src_ref=send1.at[d, k], dst_ref=recv1.at[d, k],
                send_sem=s1_send.at[d, k], recv_sem=s1_recv.at[d, k],
                device_id=(peer, col), device_id_type=pl.DeviceIdType.MESH)
            cp.start()
            step_copies.append(cp)
        copies1.append(step_copies)
    partials(y, y)
    for d, (peer, sign, a, r0) in enumerate(lanes):
        copies1[ny - 2][d].wait_recv()
        acc[a, r0:r0 + piece] = (recv1[d, ny - 2].astype(jnp.float32)
                                 + pbuf[a, r0:r0 + piece].astype(jnp.float32))

    lanes2 = [(x_up, 1, 0), (x_up, 1, quarter), (x_down, -1, 2 * quarter), (x_down, -1, 3 * quarter)]
    copies2 = []
    for k in range(nx - 1):
        step_copies = []
        for d, (peer, sign, r0) in enumerate(lanes2):
            c = (x - sign * (k + 1) + 2 * nx) % nx
            if k == 0:
                src = acc.at[c, r0:r0 + quarter]
            else:
                copies2[k - 1][d].wait_recv()
                send2[d, k] = recv2[d, k - 1] + acc[c, r0:r0 + quarter]
                src = send2.at[d, k]
            cp = pltpu.make_async_remote_copy(
                src_ref=src, dst_ref=recv2.at[d, k],
                send_sem=s2_send.at[d, k], recv_sem=s2_recv.at[d, k],
                device_id=(peer, col), device_id_type=pl.DeviceIdType.MESH)
            cp.start()
            step_copies.append(cp)
        copies2.append(step_copies)
    for d, (peer, sign, r0) in enumerate(lanes2):
        copies2[nx - 2][d].wait_recv()
        out_ref[r0:r0 + quarter] = (recv2[d, nx - 2] + acc[x, r0:r0 + quarter]).astype(out_ref.dtype)
    back = []
    for k in range(1, n_exp):
        peer = (col + k) % n_exp
        cp = pltpu.make_async_remote_copy(
            src_ref=out_ref.at[pl.ds(peer * group, group)], dst_ref=ret_ref.at[col],
            send_sem=r_send.at[k - 1], recv_sem=r_recv.at[k - 1],
            device_id=(me, peer), device_id_type=pl.DeviceIdType.MESH)
        cp.start()
        back.append(cp)
    own = pltpu.make_async_copy(out_ref.at[pl.ds(col * group, group)], ret_ref.at[col], r_send.at[n_exp - 1])
    own.start()
    own.wait()
    for step_copies in copies1 + copies2:
        for cp in step_copies:
            cp.wait_send()
    for cp in back:
        cp.wait()


def ring_ffn(tokens, w_gate, w_up, w_down, nx, ny, n_exp, splits=2):
    width = tokens.shape[-1]
    rows = tokens.shape[0] // (nx * ny)
    tokens = tokens.reshape(nx, ny, rows, width)
    n1 = nx * splits
    vmem = pltpu.MemorySpace.VMEM
    return pl.pallas_call(
        functools.partial(ring_ffn_kernel, nx, ny, splits),
        out_shape=(jax.ShapeDtypeStruct((rows, width), jnp.bfloat16),
                   jax.ShapeDtypeStruct((n_exp, rows // n_exp, width), jnp.bfloat16)),
        in_specs=[pl.BlockSpec(memory_space=vmem)] * 4,
        out_specs=(pl.BlockSpec(memory_space=vmem), pl.BlockSpec(memory_space=vmem)),
        scratch_shapes=[
            pltpu.VMEM((nx, rows, width), jnp.bfloat16),
            pltpu.VMEM((n1, ny - 1, rows // splits, width), jnp.bfloat16),
            pltpu.VMEM((n1, ny - 1, rows // splits, width), jnp.bfloat16),
            pltpu.VMEM((nx, rows, width), jnp.float32),
            pltpu.VMEM((4, nx - 1, rows // 4, width), jnp.float32),
            pltpu.VMEM((4, nx - 1, rows // 4, width), jnp.float32),
            pltpu.SemaphoreType.DMA((n1, ny - 1)),
            pltpu.SemaphoreType.DMA((n1, ny - 1)),
            pltpu.SemaphoreType.DMA((4, nx - 1)),
            pltpu.SemaphoreType.DMA((4, nx - 1)),
            pltpu.SemaphoreType.DMA((n_exp,)),
            pltpu.SemaphoreType.DMA((n_exp - 1,)),
        ],
        compiler_params=pltpu.CompilerParams(
            collective_id=5, has_side_effects=True, vmem_limit_bytes=56 * 1024 * 1024
        ),
    )(tokens, w_gate, w_up, w_down)


def shift_exchange_kernel(offsets, axis, other, block_ref, out_ref, send_sems, recv_sems):
    n = lax.axis_size(axis)
    me = lax.axis_index(axis)
    col = lax.axis_index(other)

    def dev(peer):
        return (peer, col) if axis == "seq" else (col, peer)

    targets = [(me + o + n * len(offsets)) % n for o in offsets]
    barrier = pltpu.get_barrier_semaphore()
    for peer in targets:
        pl.semaphore_signal(barrier, inc=1, device_id=dev(peer),
                            device_id_type=pl.DeviceIdType.MESH)
    pl.semaphore_wait(barrier, len(offsets))
    copies = []
    for j, peer in enumerate(targets):
        cp = pltpu.make_async_remote_copy(
            src_ref=block_ref, dst_ref=out_ref.at[j],
            send_sem=send_sems.at[j], recv_sem=recv_sems.at[j],
            device_id=dev(peer), device_id_type=pl.DeviceIdType.MESH)
        cp.start()
        copies.append(cp)
    for cp in copies:
        cp.wait()


def shift_exchange(block, offsets, axis, other, cid):
    vmem = pltpu.MemorySpace.VMEM
    k = len(offsets)
    return pl.pallas_call(
        functools.partial(shift_exchange_kernel, tuple(offsets), axis, other),
        out_shape=jax.ShapeDtypeStruct((k,) + block.shape, block.dtype),
        in_specs=[pl.BlockSpec(memory_space=vmem)],
        out_specs=pl.BlockSpec(memory_space=vmem),
        scratch_shapes=[pltpu.SemaphoreType.DMA((k,)), pltpu.SemaphoreType.DMA((k,))],
        compiler_params=pltpu.CompilerParams(collective_id=cid, has_side_effects=True),
    )(block)


def exp_all_to_all_kernel(x_ref, y_ref, send_sems, recv_sems):
    n = lax.axis_size("exp")
    me = lax.axis_index("exp")
    row = lax.axis_index("seq")
    barrier = pltpu.get_barrier_semaphore()
    for k in range(1, n):
        pl.semaphore_signal(barrier, inc=1, device_id=(row, (me + k) % n),
                            device_id_type=pl.DeviceIdType.MESH)
    pl.semaphore_wait(barrier, n - 1)
    copies = []
    for k in range(1, n):
        peer = (me + k) % n
        cp = pltpu.make_async_remote_copy(
            src_ref=x_ref.at[peer], dst_ref=y_ref.at[me],
            send_sem=send_sems.at[k - 1], recv_sem=recv_sems.at[k - 1],
            device_id=(row, peer), device_id_type=pl.DeviceIdType.MESH)
        cp.start()
        copies.append(cp)
    y_ref[me] = x_ref[me]
    for cp in copies:
        cp.wait()


def exp_all_to_all(x, cid):
    n = x.shape[0]
    vmem = pltpu.MemorySpace.VMEM
    return pl.pallas_call(
        exp_all_to_all_kernel,
        out_shape=jax.ShapeDtypeStruct(x.shape, x.dtype),
        in_specs=[pl.BlockSpec(memory_space=vmem)],
        out_specs=pl.BlockSpec(memory_space=vmem),
        scratch_shapes=[pltpu.SemaphoreType.DMA((n - 1,)), pltpu.SemaphoreType.DMA((n - 1,))],
        compiler_params=pltpu.CompilerParams(collective_id=cid, has_side_effects=True),
    )(x)


def ring_gather_kernel(nx, ny, axis, other, pieces, route, block_ref, out_ref, local_sem, send_sems, recv_sems,
                       r_send, r_recv):
    me = lax.axis_index(axis)
    col = lax.axis_index(other)
    x = me // ny
    y = me % ny
    rows = block_ref.shape[0]
    hr = rows // 2

    def dev(a, b):
        idx = (a + nx) % nx * ny + (b + ny) % ny
        return (idx, col) if axis == "seq" else (col, idx)

    peers = [dev(x, y + 1), dev(x, y - 1), dev(x + 1, y), dev(x - 1, y)]
    n_other = lax.axis_size(other)
    barrier = pltpu.get_barrier_semaphore()
    for peer in peers:
        pl.semaphore_signal(barrier, inc=1, device_id=peer, device_id_type=pl.DeviceIdType.MESH)
    if route:
        for k in range(1, n_other):
            pl.semaphore_signal(barrier, inc=1, device_id=(me, (col + k) % n_other),
                                device_id_type=pl.DeviceIdType.MESH)
    pl.semaphore_wait(barrier, 4 + (n_other - 1 if route else 0))

    if route:
        group = rows // n_other
        routed = []
        for k in range(1, n_other):
            peer = (col + k) % n_other
            cp = pltpu.make_async_remote_copy(
                src_ref=block_ref.at[pl.ds(peer * group, group)],
                dst_ref=out_ref.at[x, y, pl.ds(col * group, group)],
                send_sem=r_send.at[k - 1], recv_sem=r_recv.at[k - 1],
                device_id=(me, peer), device_id_type=pl.DeviceIdType.MESH)
            cp.start()
            routed.append(cp)
        own = pltpu.make_async_copy(block_ref.at[pl.ds(col * group, group)],
                                    out_ref.at[x, y, pl.ds(col * group, group)], local_sem.at[0])
        own.start()
        own.wait()
        for cp in routed:
            cp.wait()
        block_ref = out_ref.at[x, y]
    else:
        own = pltpu.make_async_copy(block_ref, out_ref.at[x, y], local_sem.at[0])
        own.start()
    sem_count = [0]

    def unit(axis, stage, u, lo, hi):
        if axis == "y":
            return out_ref.at[x, u, lo:hi] if stage == 1 else out_ref.at[:, u, lo:hi]
        return out_ref.at[u, y, lo:hi] if stage == 1 else out_ref.at[u, :, lo:hi]

    def ring(axis, stage, lo, hi):
        n = ny if axis == "y" else nx
        c = y if axis == "y" else x
        half = n // 2
        mid = (lo + hi) // 2
        steps = []
        for sign in (1, -1):
            prev = None
            lane = []
            for k in range(half):
                u = (c - sign * k + 2 * n) % n
                a_lo, a_hi = lo, hi
                if k == half - 1 and n % 2 == 0:
                    a_lo, a_hi = (lo, mid) if sign == 1 else (mid, hi)
                if stage == 1 and k == 0:
                    src = block_ref.at[a_lo:a_hi]
                else:
                    src = unit(axis, stage, u, a_lo, a_hi)
                dst = unit(axis, stage, u, a_lo, a_hi)
                target = dev(x, y + sign) if axis == "y" else dev(x + sign, y)
                j = sem_count[0]
                sem_count[0] += 1
                cp = pltpu.make_async_remote_copy(
                    src_ref=src, dst_ref=dst, send_sem=send_sems.at[j], recv_sem=recv_sems.at[j],
                    device_id=target, device_id_type=pl.DeviceIdType.MESH)
                lane.append((prev, cp))
                prev = cp
            steps.append(lane)
        return steps

    plans = []
    step = hr // pieces
    for p in range(pieces):
        for base, first, second in ((0, "y", "x"), (hr, "x", "y")):
            lo = base + p * step
            s1 = ring(first, 1, lo, lo + step)
            s2 = ring(second, 2, lo, lo + step)
            plans.append((s1, s2))

    started = []

    def run(lane_list):
        depth = max(len(l) for l in lane_list)
        for k in range(depth):
            for lane in lane_list:
                if k < len(lane):
                    prev, cp = lane[k]
                    if prev is not None:
                        prev.wait_recv()
                    cp.start()
                    started.append(cp)

    run([lane for s1, _ in plans for lane in s1])
    for s1, _ in plans:
        for lane in s1:
            lane[-1][1].wait_recv()
    if not route:
        own.wait()
    run([lane for _, s2 in plans for lane in s2])
    for _, s2 in plans:
        for lane in s2:
            lane[-1][1].wait_recv()
    for cp in started:
        cp.wait_send()


def ring_gather(block, nx, ny, axis="seq", other="exp", cid=3, pieces=1, route=False, n_other=2):
    vmem = pltpu.MemorySpace.VMEM
    n_sems = 4 * pieces * (nx // 2 + ny // 2) + 4
    return pl.pallas_call(
        functools.partial(ring_gather_kernel, nx, ny, axis, other, pieces, route),
        out_shape=jax.ShapeDtypeStruct((nx, ny) + block.shape, block.dtype),
        in_specs=[pl.BlockSpec(memory_space=vmem)],
        out_specs=pl.BlockSpec(memory_space=vmem),
        scratch_shapes=[
            pltpu.SemaphoreType.DMA((1,)),
            pltpu.SemaphoreType.DMA((n_sems,)),
            pltpu.SemaphoreType.DMA((n_sems,)),
            pltpu.SemaphoreType.DMA((n_other,)),
            pltpu.SemaphoreType.DMA((n_other,)),
        ],
        compiler_params=pltpu.CompilerParams(
            collective_id=cid, has_side_effects=True, vmem_limit_bytes=48 * 1024 * 1024
        ),
    )(block)


def rms_scale(matrix, gain):
    mean_square = jnp.mean(matrix * matrix, axis=-1, keepdims=True)
    return matrix * lax.rsqrt(mean_square + EPSILON) * gain


def expert_terms(block, gate_slice, up_slice, down_slice):
    gate = jnp.einsum("nek,ekf->nef", block, gate_slice, preferred_element_type=jnp.float32)
    upward = jnp.einsum("nek,ekf->nef", block, up_slice, preferred_element_type=jnp.float32)
    act = (jax.nn.silu(gate) * upward).astype(jnp.bfloat16)
    return jnp.einsum("nef,ekf->nek", act, down_slice, preferred_element_type=jnp.float32)


def local(
    tokens,
    array_type,
    block_pattern,
    gain_attn,
    w_query,
    w_key,
    w_value,
    logit_scale,
    w_out,
    gain_ffn,
    w_gate,
    w_up,
    w_down,
):
    n_exp = lax.axis_size("exp")
    row_count = tokens.shape[0]
    width = tokens.shape[1]
    head_cols = w_query.shape[1]
    heads_dev = logit_scale.shape[0]
    head_size = head_cols // heads_dev
    n_blocks = block_pattern.shape[0]
    inputs = tokens.astype(jnp.float32)
    normed_attn = rms_scale(inputs, gain_attn).astype(jnp.bfloat16)
    projector = jnp.concatenate([w_query, w_key, w_value], axis=1)
    joined_qkv = jnp.dot(
        ring_gather(normed_attn, n_exp // CORES, CORES, "exp", "seq", 4, pieces=2).reshape(n_exp * row_count, width),
        projector,
        preferred_element_type=jnp.float32,
    ).astype(jnp.bfloat16)
    block_len = joined_qkv.shape[0]
    query_heads = joined_qkv[:, :head_cols].reshape(block_len, heads_dev, head_size)
    key_value = joined_qkv[:, head_cols:]
    position = lax.axis_index("seq")
    head_scale = logit_scale[:, None, None]

    offsets = [d for d in range(1, REACH + 1)] + [-d for d in range(1, REACH + 1)]
    neighbours = shift_exchange(key_value, offsets, "seq", "exp", 2)
    band = jnp.concatenate([key_value[None], neighbours], axis=0)
    n_band = band.shape[0]
    sources = jnp.stack([position] + [(position - o) % n_blocks for o in offsets])
    allowed = jnp.repeat(block_pattern[position, sources] > 0, block_len)
    key_band = band[:, :, :head_cols].reshape(n_band * block_len, heads_dev, head_size)
    value_band = band[:, :, head_cols:].reshape(n_band * block_len, heads_dev, head_size)
    scores = (
        jnp.einsum("qhd,khd->hqk", query_heads, key_band, preferred_element_type=jnp.float32)
        * head_scale
    )
    scores = jnp.where(allowed[None, None, :], scores, -jnp.inf)
    row_top = jnp.max(scores, axis=2, keepdims=True)
    weights = jnp.exp(scores - row_top)
    weight_sum = jnp.sum(weights, axis=2)
    weighted = jnp.einsum(
        "hqk,khd->qhd",
        weights.astype(jnp.bfloat16),
        value_band,
        preferred_element_type=jnp.float32,
    )
    heads_out = (
        (weighted / jnp.transpose(weight_sum)[:, :, None])
        .astype(jnp.bfloat16)
        .reshape(block_len, head_cols)
    )
    all_heads = lax.all_to_all(heads_out, "exp", split_axis=0, concat_axis=1, tiled=True)
    attn_out = jnp.dot(
        all_heads,
        lax.all_gather(w_out, "exp", axis=0, tiled=True),
        preferred_element_type=jnp.float32,
    )
    hidden_state = inputs + attn_out
    normed_ffn = rms_scale(hidden_state, gain_ffn).astype(jnp.bfloat16)
    experts_dev = w_gate.shape[0]
    n_total = experts_dev * n_exp
    capacity = 2 * row_count // n_total
    one_hot = (array_type[:, None] == jnp.arange(n_total, dtype=jnp.int32)[None, :]).astype(
        jnp.int32
    )
    slot_rank = jnp.sum(jnp.cumsum(one_hot, axis=0) * one_hot, axis=1) - 1
    owner = array_type // experts_dev
    local_expert = array_type % experts_dev
    slot_id = (owner * capacity + slot_rank) * experts_dev + local_expert
    n_slots = n_exp * capacity * experts_dev
    selector = (slot_id[None, :] == jnp.arange(n_slots, dtype=jnp.int32)[:, None]).astype(
        jnp.bfloat16
    )
    outgoing = jnp.dot(selector, normed_ffn, preferred_element_type=jnp.float32).astype(
        jnp.bfloat16
    )
    outgoing = outgoing.reshape(n_exp * capacity, experts_dev, width)
    n_seq = lax.axis_size("seq")
    y_size = Y_RING if n_seq % Y_RING == 0 else n_seq
    gathered = ring_gather(
        outgoing.reshape(-1, width), n_seq // y_size, y_size, pieces=2, route=True, n_other=n_exp
    ).reshape((n_seq * outgoing.shape[0],) + outgoing.shape[1:])
    n_seq = lax.axis_size("seq")
    y_size = Y_RING if n_seq % Y_RING == 0 else n_seq
    returned = ring_ffn(
        gathered.reshape(gathered.shape[0], width),
        w_gate[0], w_up[0], w_down[0], n_seq // y_size, y_size, n_exp,
    )[1].reshape((-1,) + gathered.shape[1:])
    expert_out = jnp.dot(
        jnp.transpose(selector),
        returned.reshape(n_slots, width),
        preferred_element_type=jnp.float32,
    )
    return (hidden_state + expert_out).astype(jnp.bfloat16)


def solution(mesh):
    return jax.shard_map(
        local,
        mesh=mesh,
        in_specs=(
            P(("seq", "exp"), None),
            P(("seq", "exp")),
            P(),
            P(),
            P(None, "exp"),
            P(None, "exp"),
            P(None, "exp"),
            P("exp"),
            P("exp", None),
            P(),
            P("exp", None, "seq"),
            P("exp", None, "seq"),
            P("exp", None, "seq"),
        ),
        out_specs=P(("seq", "exp"), None),
        check_vma=False,
    )
```

```python
import jax
import jax.numpy as jnp
from jax import lax
from jax.sharding import PartitionSpec as P
from jax.experimental import pallas as pl
from jax.experimental.pallas import tpu as pltpu
import functools

REACH = 3
Y_RING = 8
CORES = 2


EPSILON = 1e-05


def passed_along(block, axis, distance):
    devices = range(lax.axis_size(axis))
    route = [((i - distance) % len(devices), i) for i in devices]
    return lax.ppermute(block, axis, route)


def ring_reduce_kernel(nx, ny, splits, part_ref, out_ref, recv1, send1, acc, recv2, send2,
                       s1_send, s1_recv, s2_send, s2_recv):
    me = lax.axis_index("seq")
    col = lax.axis_index("exp")
    x = me // ny
    y = me % ny
    y_up = x * ny + (y + 1) % ny
    y_down = x * ny + (y + ny - 1) % ny
    x_up = ((x + 1) % nx) * ny + y
    x_down = ((x + nx - 1) % nx) * ny + y
    rows = part_ref.shape[2]
    piece = rows // splits
    quarter = rows // 4

    barrier = pltpu.get_barrier_semaphore()
    for peer in (y_up, y_down, x_up, x_down):
        pl.semaphore_signal(barrier, inc=1, device_id=(peer, col),
                            device_id_type=pl.DeviceIdType.MESH)
    pl.semaphore_wait(barrier, 4)

    lanes = []
    for a in range(nx):
        for p in range(splits):
            if a < nx // 2:
                lanes.append((y_up, 1, a, p * piece))
            else:
                lanes.append((y_down, -1, a, p * piece))
    copies1 = []
    for k in range(ny - 1):
        step_copies = []
        for d, (peer, sign, a, r0) in enumerate(lanes):
            c = (y - sign * (k + 1) + 2 * ny) % ny
            if k == 0:
                src = part_ref.at[a, c, r0:r0 + piece]
            else:
                copies1[k - 1][d].wait_recv()
                send1[d, k] = (recv1[d, k - 1].astype(jnp.float32)
                               + part_ref[a, c, r0:r0 + piece].astype(jnp.float32)).astype(send1.dtype)
                src = send1.at[d, k]
            cp = pltpu.make_async_remote_copy(
                src_ref=src, dst_ref=recv1.at[d, k],
                send_sem=s1_send.at[d, k], recv_sem=s1_recv.at[d, k],
                device_id=(peer, col), device_id_type=pl.DeviceIdType.MESH)
            cp.start()
            step_copies.append(cp)
        copies1.append(step_copies)
    for d, (peer, sign, a, r0) in enumerate(lanes):
        copies1[ny - 2][d].wait_recv()
        acc[a, r0:r0 + piece] = (recv1[d, ny - 2].astype(jnp.float32)
                                 + part_ref[a, y, r0:r0 + piece].astype(jnp.float32))

    lanes2 = [(x_up, 1, 0), (x_up, 1, quarter), (x_down, -1, 2 * quarter), (x_down, -1, 3 * quarter)]
    copies2 = []
    for k in range(nx - 1):
        step_copies = []
        for d, (peer, sign, r0) in enumerate(lanes2):
            c = (x - sign * (k + 1) + 2 * nx) % nx
            if k == 0:
                src = acc.at[c, r0:r0 + quarter]
            else:
                copies2[k - 1][d].wait_recv()
                send2[d, k] = recv2[d, k - 1] + acc[c, r0:r0 + quarter]
                src = send2.at[d, k]
            cp = pltpu.make_async_remote_copy(
                src_ref=src, dst_ref=recv2.at[d, k],
                send_sem=s2_send.at[d, k], recv_sem=s2_recv.at[d, k],
                device_id=(peer, col), device_id_type=pl.DeviceIdType.MESH)
            cp.start()
            step_copies.append(cp)
        copies2.append(step_copies)
    for d, (peer, sign, r0) in enumerate(lanes2):
        copies2[nx - 2][d].wait_recv()
        out_ref[r0:r0 + quarter] = (recv2[d, nx - 2] + acc[x, r0:r0 + quarter]).astype(out_ref.dtype)
    for step_copies in copies1 + copies2:
        for cp in step_copies:
            cp.wait_send()


def ring_reduce(part, nx, ny, splits=2):
    width = part.shape[-1]
    rows = part.shape[0] // (nx * ny)
    part = part.reshape(nx, ny, rows, width)
    n1 = nx * splits
    vmem = pltpu.MemorySpace.VMEM
    return pl.pallas_call(
        functools.partial(ring_reduce_kernel, nx, ny, splits),
        out_shape=jax.ShapeDtypeStruct((rows, width), jnp.bfloat16),
        in_specs=[pl.BlockSpec(memory_space=vmem)],
        out_specs=pl.BlockSpec(memory_space=vmem),
        scratch_shapes=[
            pltpu.VMEM((n1, ny - 1, rows // splits, width), jnp.bfloat16),
            pltpu.VMEM((n1, ny - 1, rows // splits, width), jnp.bfloat16),
            pltpu.VMEM((nx, rows, width), jnp.float32),
            pltpu.VMEM((4, nx - 1, rows // 4, width), jnp.float32),
            pltpu.VMEM((4, nx - 1, rows // 4, width), jnp.float32),
            pltpu.SemaphoreType.DMA((n1, ny - 1)),
            pltpu.SemaphoreType.DMA((n1, ny - 1)),
            pltpu.SemaphoreType.DMA((4, nx - 1)),
            pltpu.SemaphoreType.DMA((4, nx - 1)),
        ],
        compiler_params=pltpu.CompilerParams(
            collective_id=1, has_side_effects=True, vmem_limit_bytes=48 * 1024 * 1024
        ),
    )(part)


def ring_ffn_kernel(nx, ny, splits, tok_ref, wg_ref, wu_ref, wd_ref, out_ref, ret_ref, pbuf, recv1, send1,
                    acc, recv2, send2, s1_send, s1_recv, s2_send, s2_recv, r_send, r_recv):
    me = lax.axis_index("seq")
    col = lax.axis_index("exp")
    x = me // ny
    y = me % ny
    y_up = x * ny + (y + 1) % ny
    y_down = x * ny + (y + ny - 1) % ny
    x_up = ((x + 1) % nx) * ny + y
    x_down = ((x + nx - 1) % nx) * ny + y
    rows = tok_ref.shape[2]
    width = tok_ref.shape[3]
    piece = rows // splits
    quarter = rows // 4
    half_x = nx // 2

    def partials(c_up, c_down):
        tok = jnp.concatenate(
            [tok_ref[0:half_x, c_up].reshape(half_x * rows, width),
             tok_ref[half_x:nx, c_down].reshape((nx - half_x) * rows, width)], axis=0)
        gate = jnp.dot(tok, wg_ref[...], preferred_element_type=jnp.float32)
        upward = jnp.dot(tok, wu_ref[...], preferred_element_type=jnp.float32)
        act = (gate / (1.0 + jnp.exp(-gate)) * upward).astype(jnp.bfloat16)
        down = lax.dot_general(act, wd_ref[...], (((1,), (1,)), ((), ())),
                               preferred_element_type=jnp.float32)
        pbuf[...] = down.astype(jnp.bfloat16).reshape(nx, rows, width)

    n_exp = lax.axis_size("exp")
    group = rows // n_exp
    barrier = pltpu.get_barrier_semaphore()
    for peer in (y_up, y_down, x_up, x_down):
        pl.semaphore_signal(barrier, inc=1, device_id=(peer, col),
                            device_id_type=pl.DeviceIdType.MESH)
    for k in range(1, n_exp):
        pl.semaphore_signal(barrier, inc=1, device_id=(me, (col + k) % n_exp),
                            device_id_type=pl.DeviceIdType.MESH)
    pl.semaphore_wait(barrier, 4 + n_exp - 1)

    lanes = []
    for a in range(nx):
        for p in range(splits):
            if a < half_x:
                lanes.append((y_up, 1, a, p * piece))
            else:
                lanes.append((y_down, -1, a, p * piece))
    copies1 = []
    for k in range(ny - 1):
        partials((y - k - 1 + ny) % ny, (y + k + 1) % ny)
        step_copies = []
        for d, (peer, sign, a, r0) in enumerate(lanes):
            if k == 0:
                send1[d, k] = pbuf[a, r0:r0 + piece]
            else:
                copies1[k - 1][d].wait_recv()
                send1[d, k] = (recv1[d, k - 1].astype(jnp.float32)
                               + pbuf[a, r0:r0 + piece].astype(jnp.float32)).astype(send1.dtype)
            cp = pltpu.make_async_remote_copy(
                src_ref=send1.at[d, k], dst_ref=recv1.at[d, k],
                send_sem=s1_send.at[d, k], recv_sem=s1_recv.at[d, k],
                device_id=(peer, col), device_id_type=pl.DeviceIdType.MESH)
            cp.start()
            step_copies.append(cp)
        copies1.append(step_copies)
    partials(y, y)
    for d, (peer, sign, a, r0) in enumerate(lanes):
        copies1[ny - 2][d].wait_recv()
        acc[a, r0:r0 + piece] = (recv1[d, ny - 2].astype(jnp.float32)
                                 + pbuf[a, r0:r0 + piece].astype(jnp.float32))

    lanes2 = [(x_up, 1, 0), (x_up, 1, quarter), (x_down, -1, 2 * quarter), (x_down, -1, 3 * quarter)]
    copies2 = []
    for k in range(nx - 1):
        step_copies = []
        for d, (peer, sign, r0) in enumerate(lanes2):
            c = (x - sign * (k + 1) + 2 * nx) % nx
            if k == 0:
                src = acc.at[c, r0:r0 + quarter]
            else:
                copies2[k - 1][d].wait_recv()
                send2[d, k] = recv2[d, k - 1] + acc[c, r0:r0 + quarter]
                src = send2.at[d, k]
            cp = pltpu.make_async_remote_copy(
                src_ref=src, dst_ref=recv2.at[d, k],
                send_sem=s2_send.at[d, k], recv_sem=s2_recv.at[d, k],
                device_id=(peer, col), device_id_type=pl.DeviceIdType.MESH)
            cp.start()
            step_copies.append(cp)
        copies2.append(step_copies)
    for d, (peer, sign, r0) in enumerate(lanes2):
        copies2[nx - 2][d].wait_recv()
        out_ref[r0:r0 + quarter] = (recv2[d, nx - 2] + acc[x, r0:r0 + quarter]).astype(out_ref.dtype)
    back = []
    for k in range(1, n_exp):
        peer = (col + k) % n_exp
        cp = pltpu.make_async_remote_copy(
            src_ref=out_ref.at[pl.ds(peer * group, group)], dst_ref=ret_ref.at[col],
            send_sem=r_send.at[k - 1], recv_sem=r_recv.at[k - 1],
            device_id=(me, peer), device_id_type=pl.DeviceIdType.MESH)
        cp.start()
        back.append(cp)
    own = pltpu.make_async_copy(out_ref.at[pl.ds(col * group, group)], ret_ref.at[col], r_send.at[n_exp - 1])
    own.start()
    own.wait()
    for step_copies in copies1 + copies2:
        for cp in step_copies:
            cp.wait_send()
    for cp in back:
        cp.wait()


def ring_ffn(tokens, w_gate, w_up, w_down, nx, ny, n_exp, splits=2):
    width = tokens.shape[-1]
    rows = tokens.shape[0] // (nx * ny)
    tokens = tokens.reshape(nx, ny, rows, width)
    n1 = nx * splits
    vmem = pltpu.MemorySpace.VMEM
    return pl.pallas_call(
        functools.partial(ring_ffn_kernel, nx, ny, splits),
        out_shape=(jax.ShapeDtypeStruct((rows, width), jnp.bfloat16),
                   jax.ShapeDtypeStruct((n_exp, rows // n_exp, width), jnp.bfloat16)),
        in_specs=[pl.BlockSpec(memory_space=vmem)] * 4,
        out_specs=(pl.BlockSpec(memory_space=vmem), pl.BlockSpec(memory_space=vmem)),
        scratch_shapes=[
            pltpu.VMEM((nx, rows, width), jnp.bfloat16),
            pltpu.VMEM((n1, ny - 1, rows // splits, width), jnp.bfloat16),
            pltpu.VMEM((n1, ny - 1, rows // splits, width), jnp.bfloat16),
            pltpu.VMEM((nx, rows, width), jnp.float32),
            pltpu.VMEM((4, nx - 1, rows // 4, width), jnp.float32),
            pltpu.VMEM((4, nx - 1, rows // 4, width), jnp.float32),
            pltpu.SemaphoreType.DMA((n1, ny - 1)),
            pltpu.SemaphoreType.DMA((n1, ny - 1)),
            pltpu.SemaphoreType.DMA((4, nx - 1)),
            pltpu.SemaphoreType.DMA((4, nx - 1)),
            pltpu.SemaphoreType.DMA((n_exp,)),
            pltpu.SemaphoreType.DMA((n_exp - 1,)),
        ],
        compiler_params=pltpu.CompilerParams(
            collective_id=5, has_side_effects=True, vmem_limit_bytes=56 * 1024 * 1024
        ),
    )(tokens, w_gate, w_up, w_down)


def shift_exchange_kernel(offsets, axis, other, block_ref, out_ref, send_sems, recv_sems):
    n = lax.axis_size(axis)
    me = lax.axis_index(axis)
    col = lax.axis_index(other)

    def dev(peer):
        return (peer, col) if axis == "seq" else (col, peer)

    targets = [(me + o + n * len(offsets)) % n for o in offsets]
    barrier = pltpu.get_barrier_semaphore()
    for peer in targets:
        pl.semaphore_signal(barrier, inc=1, device_id=dev(peer),
                            device_id_type=pl.DeviceIdType.MESH)
    pl.semaphore_wait(barrier, len(offsets))
    copies = []
    for j, peer in enumerate(targets):
        cp = pltpu.make_async_remote_copy(
            src_ref=block_ref, dst_ref=out_ref.at[j],
            send_sem=send_sems.at[j], recv_sem=recv_sems.at[j],
            device_id=dev(peer), device_id_type=pl.DeviceIdType.MESH)
        cp.start()
        copies.append(cp)
    for cp in copies:
        cp.wait()


def shift_exchange(block, offsets, axis, other, cid):
    vmem = pltpu.MemorySpace.VMEM
    k = len(offsets)
    return pl.pallas_call(
        functools.partial(shift_exchange_kernel, tuple(offsets), axis, other),
        out_shape=jax.ShapeDtypeStruct((k,) + block.shape, block.dtype),
        in_specs=[pl.BlockSpec(memory_space=vmem)],
        out_specs=pl.BlockSpec(memory_space=vmem),
        scratch_shapes=[pltpu.SemaphoreType.DMA((k,)), pltpu.SemaphoreType.DMA((k,))],
        compiler_params=pltpu.CompilerParams(collective_id=cid, has_side_effects=True),
    )(block)


def exp_all_to_all_kernel(x_ref, y_ref, send_sems, recv_sems):
    n = lax.axis_size("exp")
    me = lax.axis_index("exp")
    row = lax.axis_index("seq")
    barrier = pltpu.get_barrier_semaphore()
    for k in range(1, n):
        pl.semaphore_signal(barrier, inc=1, device_id=(row, (me + k) % n),
                            device_id_type=pl.DeviceIdType.MESH)
    pl.semaphore_wait(barrier, n - 1)
    copies = []
    for k in range(1, n):
        peer = (me + k) % n
        cp = pltpu.make_async_remote_copy(
            src_ref=x_ref.at[peer], dst_ref=y_ref.at[me],
            send_sem=send_sems.at[k - 1], recv_sem=recv_sems.at[k - 1],
            device_id=(row, peer), device_id_type=pl.DeviceIdType.MESH)
        cp.start()
        copies.append(cp)
    y_ref[me] = x_ref[me]
    for cp in copies:
        cp.wait()


def exp_all_to_all(x, cid):
    n = x.shape[0]
    vmem = pltpu.MemorySpace.VMEM
    return pl.pallas_call(
        exp_all_to_all_kernel,
        out_shape=jax.ShapeDtypeStruct(x.shape, x.dtype),
        in_specs=[pl.BlockSpec(memory_space=vmem)],
        out_specs=pl.BlockSpec(memory_space=vmem),
        scratch_shapes=[pltpu.SemaphoreType.DMA((n - 1,)), pltpu.SemaphoreType.DMA((n - 1,))],
        compiler_params=pltpu.CompilerParams(collective_id=cid, has_side_effects=True),
    )(x)


def ring_gather_kernel(nx, ny, axis, other, pieces, route, block_ref, out_ref, local_sem, send_sems, recv_sems,
                       r_send, r_recv):
    me = lax.axis_index(axis)
    col = lax.axis_index(other)
    x = me // ny
    y = me % ny
    rows = block_ref.shape[0]
    hr = rows // 2

    def dev(a, b):
        idx = (a + nx) % nx * ny + (b + ny) % ny
        return (idx, col) if axis == "seq" else (col, idx)

    peers = []
    for d in range(1, min(2, ny // 2) + 1):
        peers += [dev(x, y + d), dev(x, y - d)]
    for d in range(1, min(2, nx // 2) + 1):
        peers += [dev(x + d, y), dev(x - d, y)]
    n_other = lax.axis_size(other)
    barrier = pltpu.get_barrier_semaphore()
    for peer in peers:
        pl.semaphore_signal(barrier, inc=1, device_id=peer, device_id_type=pl.DeviceIdType.MESH)
    if route:
        for k in range(1, n_other):
            pl.semaphore_signal(barrier, inc=1, device_id=(me, (col + k) % n_other),
                                device_id_type=pl.DeviceIdType.MESH)
    pl.semaphore_wait(barrier, len(peers) + (n_other - 1 if route else 0))

    if route:
        group = rows // n_other
        routed = []
        for k in range(1, n_other):
            peer = (col + k) % n_other
            cp = pltpu.make_async_remote_copy(
                src_ref=block_ref.at[pl.ds(peer * group, group)],
                dst_ref=out_ref.at[x, y, pl.ds(col * group, group)],
                send_sem=r_send.at[k - 1], recv_sem=r_recv.at[k - 1],
                device_id=(me, peer), device_id_type=pl.DeviceIdType.MESH)
            cp.start()
            routed.append(cp)
        own = pltpu.make_async_copy(block_ref.at[pl.ds(col * group, group)],
                                    out_ref.at[x, y, pl.ds(col * group, group)], local_sem.at[0])
        own.start()
        own.wait()
        for cp in routed:
            cp.wait()
        block_ref = out_ref.at[x, y]
    else:
        own = pltpu.make_async_copy(block_ref, out_ref.at[x, y], local_sem.at[0])
        own.start()
    sem_count = [0]

    def unit(axis, stage, u, lo, hi):
        if axis == "y":
            return out_ref.at[x, u, lo:hi] if stage == 1 else out_ref.at[:, u, lo:hi]
        return out_ref.at[u, y, lo:hi] if stage == 1 else out_ref.at[u, :, lo:hi]

    def ring(axis, stage, lo, hi):
        n = ny if axis == "y" else nx
        c = y if axis == "y" else x
        half = n // 2
        mid = (lo + hi) // 2
        steps = []
        for sign in (1, -1):
            def rows_for(d):
                if d == half and n % 2 == 0:
                    return (lo, mid) if sign == 1 else (mid, hi)
                return (lo, hi)

            def target(d):
                return dev(x, y + sign * d) if axis == "y" else dev(x + sign * d, y)

            direct = {}
            for d in range(1, min(2, half) + 1):
                a_lo, a_hi = rows_for(d)
                src = block_ref.at[a_lo:a_hi] if stage == 1 else unit(axis, stage, c, a_lo, a_hi)
                j = sem_count[0]
                sem_count[0] += 1
                cp = pltpu.make_async_remote_copy(
                    src_ref=src, dst_ref=unit(axis, stage, c, a_lo, a_hi),
                    send_sem=send_sems.at[j], recv_sem=recv_sems.at[j],
                    device_id=target(d), device_id_type=pl.DeviceIdType.MESH)
                direct[d] = cp
                steps.append([(None, cp)])
            for d in range(3, half + 1):
                a_lo, a_hi = rows_for(d)
                u = (c - sign * (d - 2) + 2 * n) % n
                j = sem_count[0]
                sem_count[0] += 1
                cp = pltpu.make_async_remote_copy(
                    src_ref=unit(axis, stage, u, a_lo, a_hi), dst_ref=unit(axis, stage, u, a_lo, a_hi),
                    send_sem=send_sems.at[j], recv_sem=recv_sems.at[j],
                    device_id=target(2), device_id_type=pl.DeviceIdType.MESH)
                steps[len(steps) - min(2, half) + (d - 3)].append((direct[d - 2], cp))
        return steps

    plans = []
    step = hr // pieces
    for p in range(pieces):
        for base, first, second in ((0, "y", "x"), (hr, "x", "y")):
            lo = base + p * step
            s1 = ring(first, 1, lo, lo + step)
            s2 = ring(second, 2, lo, lo + step)
            plans.append((s1, s2))

    started = []

    def run(lane_list):
        depth = max(len(l) for l in lane_list)
        for k in range(depth):
            for lane in lane_list:
                if k < len(lane):
                    prev, cp = lane[k]
                    if prev is not None:
                        prev.wait_recv()
                    cp.start()
                    started.append(cp)

    run([lane for s1, _ in plans for lane in s1])
    for s1, _ in plans:
        for lane in s1:
            lane[-1][1].wait_recv()
    if not route:
        own.wait()
    run([lane for _, s2 in plans for lane in s2])
    for _, s2 in plans:
        for lane in s2:
            lane[-1][1].wait_recv()
    for cp in started:
        cp.wait_send()


def ring_gather(block, nx, ny, axis="seq", other="exp", cid=3, pieces=1, route=False, n_other=2):
    vmem = pltpu.MemorySpace.VMEM
    n_sems = 4 * pieces * (nx // 2 + ny // 2) + 4
    return pl.pallas_call(
        functools.partial(ring_gather_kernel, nx, ny, axis, other, pieces, route),
        out_shape=jax.ShapeDtypeStruct((nx, ny) + block.shape, block.dtype),
        in_specs=[pl.BlockSpec(memory_space=vmem)],
        out_specs=pl.BlockSpec(memory_space=vmem),
        scratch_shapes=[
            pltpu.SemaphoreType.DMA((1,)),
            pltpu.SemaphoreType.DMA((n_sems,)),
            pltpu.SemaphoreType.DMA((n_sems,)),
            pltpu.SemaphoreType.DMA((n_other,)),
            pltpu.SemaphoreType.DMA((n_other,)),
        ],
        compiler_params=pltpu.CompilerParams(
            collective_id=cid, has_side_effects=True, vmem_limit_bytes=48 * 1024 * 1024
        ),
    )(block)


def rms_scale(matrix, gain):
    mean_square = jnp.mean(matrix * matrix, axis=-1, keepdims=True)
    return matrix * lax.rsqrt(mean_square + EPSILON) * gain


def expert_terms(block, gate_slice, up_slice, down_slice):
    gate = jnp.einsum("nek,ekf->nef", block, gate_slice, preferred_element_type=jnp.float32)
    upward = jnp.einsum("nek,ekf->nef", block, up_slice, preferred_element_type=jnp.float32)
    act = (jax.nn.silu(gate) * upward).astype(jnp.bfloat16)
    return jnp.einsum("nef,ekf->nek", act, down_slice, preferred_element_type=jnp.float32)


def local(
    tokens,
    array_type,
    block_pattern,
    gain_attn,
    w_query,
    w_key,
    w_value,
    logit_scale,
    w_out,
    gain_ffn,
    w_gate,
    w_up,
    w_down,
):
    n_exp = lax.axis_size("exp")
    row_count = tokens.shape[0]
    width = tokens.shape[1]
    head_cols = w_query.shape[1]
    heads_dev = logit_scale.shape[0]
    head_size = head_cols // heads_dev
    n_blocks = block_pattern.shape[0]
    inputs = tokens.astype(jnp.float32)
    normed_attn = rms_scale(inputs, gain_attn).astype(jnp.bfloat16)
    projector = jnp.concatenate([w_query, w_key, w_value], axis=1)
    joined_qkv = jnp.dot(
        ring_gather(normed_attn, n_exp // CORES, CORES, "exp", "seq", 4, pieces=2).reshape(n_exp * row_count, width),
        projector,
        preferred_element_type=jnp.float32,
    ).astype(jnp.bfloat16)
    block_len = joined_qkv.shape[0]
    query_heads = joined_qkv[:, :head_cols].reshape(block_len, heads_dev, head_size)
    key_value = joined_qkv[:, head_cols:]
    position = lax.axis_index("seq")
    head_scale = logit_scale[:, None, None]

    offsets = [d for d in range(1, REACH + 1)] + [-d for d in range(1, REACH + 1)]
    neighbours = shift_exchange(key_value, offsets, "seq", "exp", 2)
    band = jnp.concatenate([key_value[None], neighbours], axis=0)
    n_band = band.shape[0]
    sources = jnp.stack([position] + [(position - o) % n_blocks for o in offsets])
    allowed = jnp.repeat(block_pattern[position, sources] > 0, block_len)
    key_band = band[:, :, :head_cols].reshape(n_band * block_len, heads_dev, head_size)
    value_band = band[:, :, head_cols:].reshape(n_band * block_len, heads_dev, head_size)
    scores = (
        jnp.einsum("qhd,khd->hqk", query_heads, key_band, preferred_element_type=jnp.float32)
        * head_scale
    )
    scores = jnp.where(allowed[None, None, :], scores, -jnp.inf)
    row_top = jnp.max(scores, axis=2, keepdims=True)
    weights = jnp.exp(scores - row_top)
    weight_sum = jnp.sum(weights, axis=2)
    weighted = jnp.einsum(
        "hqk,khd->qhd",
        weights.astype(jnp.bfloat16),
        value_band,
        preferred_element_type=jnp.float32,
    )
    heads_out = (
        (weighted / jnp.transpose(weight_sum)[:, :, None])
        .astype(jnp.bfloat16)
        .reshape(block_len, head_cols)
    )
    all_heads = lax.all_to_all(heads_out, "exp", split_axis=0, concat_axis=1, tiled=True)
    attn_out = jnp.dot(
        all_heads,
        lax.all_gather(w_out, "exp", axis=0, tiled=True),
        preferred_element_type=jnp.float32,
    )
    hidden_state = inputs + attn_out
    normed_ffn = rms_scale(hidden_state, gain_ffn).astype(jnp.bfloat16)
    experts_dev = w_gate.shape[0]
    n_total = experts_dev * n_exp
    capacity = 2 * row_count // n_total
    one_hot = (array_type[:, None] == jnp.arange(n_total, dtype=jnp.int32)[None, :]).astype(
        jnp.int32
    )
    slot_rank = jnp.sum(jnp.cumsum(one_hot, axis=0) * one_hot, axis=1) - 1
    owner = array_type // experts_dev
    local_expert = array_type % experts_dev
    slot_id = (owner * capacity + slot_rank) * experts_dev + local_expert
    n_slots = n_exp * capacity * experts_dev
    selector = (slot_id[None, :] == jnp.arange(n_slots, dtype=jnp.int32)[:, None]).astype(
        jnp.bfloat16
    )
    outgoing = jnp.dot(selector, normed_ffn, preferred_element_type=jnp.float32).astype(
        jnp.bfloat16
    )
    outgoing = outgoing.reshape(n_exp * capacity, experts_dev, width)
    n_seq = lax.axis_size("seq")
    y_size = Y_RING if n_seq % Y_RING == 0 else n_seq
    gathered = ring_gather(
        outgoing.reshape(-1, width), n_seq // y_size, y_size, pieces=2, route=True, n_other=n_exp
    ).reshape((n_seq * outgoing.shape[0],) + outgoing.shape[1:])
    n_seq = lax.axis_size("seq")
    y_size = Y_RING if n_seq % Y_RING == 0 else n_seq
    returned = ring_ffn(
        gathered.reshape(gathered.shape[0], width),
        w_gate[0], w_up[0], w_down[0], n_seq // y_size, y_size, n_exp,
    )[1].reshape((-1,) + gathered.shape[1:])
    expert_out = jnp.dot(
        jnp.transpose(selector),
        returned.reshape(n_slots, width),
        preferred_element_type=jnp.float32,
    )
    return (hidden_state + expert_out).astype(jnp.bfloat16)


def solution(mesh):
    return jax.shard_map(
        local,
        mesh=mesh,
        in_specs=(
            P(("seq", "exp"), None),
            P(("seq", "exp")),
            P(),
            P(),
            P(None, "exp"),
            P(None, "exp"),
            P(None, "exp"),
            P("exp"),
            P("exp", None),
            P(),
            P("exp", None, "seq"),
            P("exp", None, "seq"),
            P("exp", None, "seq"),
        ),
        out_specs=P(("seq", "exp"), None),
        check_vma=False,
    )
```

```python
import jax
import jax.numpy as jnp
from jax import lax
from jax.sharding import PartitionSpec as P
from jax.experimental import pallas as pl
from jax.experimental.pallas import tpu as pltpu
import functools

REACH = 3
Y_RING = 8
CORES = 2


EPSILON = 1e-05


def passed_along(block, axis, distance):
    devices = range(lax.axis_size(axis))
    route = [((i - distance) % len(devices), i) for i in devices]
    return lax.ppermute(block, axis, route)


def ring_reduce_kernel(nx, ny, splits, part_ref, out_ref, recv1, send1, acc, recv2, send2,
                       s1_send, s1_recv, s2_send, s2_recv):
    me = lax.axis_index("seq")
    col = lax.axis_index("exp")
    x = me // ny
    y = me % ny
    y_up = x * ny + (y + 1) % ny
    y_down = x * ny + (y + ny - 1) % ny
    x_up = ((x + 1) % nx) * ny + y
    x_down = ((x + nx - 1) % nx) * ny + y
    rows = part_ref.shape[2]
    piece = rows // splits
    quarter = rows // 4

    barrier = pltpu.get_barrier_semaphore()
    for peer in (y_up, y_down, x_up, x_down):
        pl.semaphore_signal(barrier, inc=1, device_id=(peer, col),
                            device_id_type=pl.DeviceIdType.MESH)
    pl.semaphore_wait(barrier, 4)

    lanes = []
    for a in range(nx):
        for p in range(splits):
            if a < nx // 2:
                lanes.append((y_up, 1, a, p * piece))
            else:
                lanes.append((y_down, -1, a, p * piece))
    copies1 = []
    for k in range(ny - 1):
        step_copies = []
        for d, (peer, sign, a, r0) in enumerate(lanes):
            c = (y - sign * (k + 1) + 2 * ny) % ny
            if k == 0:
                src = part_ref.at[a, c, r0:r0 + piece]
            else:
                copies1[k - 1][d].wait_recv()
                send1[d, k] = (recv1[d, k - 1].astype(jnp.float32)
                               + part_ref[a, c, r0:r0 + piece].astype(jnp.float32)).astype(send1.dtype)
                src = send1.at[d, k]
            cp = pltpu.make_async_remote_copy(
                src_ref=src, dst_ref=recv1.at[d, k],
                send_sem=s1_send.at[d, k], recv_sem=s1_recv.at[d, k],
                device_id=(peer, col), device_id_type=pl.DeviceIdType.MESH)
            cp.start()
            step_copies.append(cp)
        copies1.append(step_copies)
    for d, (peer, sign, a, r0) in enumerate(lanes):
        copies1[ny - 2][d].wait_recv()
        acc[a, r0:r0 + piece] = (recv1[d, ny - 2].astype(jnp.float32)
                                 + part_ref[a, y, r0:r0 + piece].astype(jnp.float32))

    lanes2 = [(x_up, 1, 0), (x_up, 1, quarter), (x_down, -1, 2 * quarter), (x_down, -1, 3 * quarter)]
    copies2 = []
    for k in range(nx - 1):
        step_copies = []
        for d, (peer, sign, r0) in enumerate(lanes2):
            c = (x - sign * (k + 1) + 2 * nx) % nx
            if k == 0:
                src = acc.at[c, r0:r0 + quarter]
            else:
                copies2[k - 1][d].wait_recv()
                send2[d, k] = recv2[d, k - 1] + acc[c, r0:r0 + quarter]
                src = send2.at[d, k]
            cp = pltpu.make_async_remote_copy(
                src_ref=src, dst_ref=recv2.at[d, k],
                send_sem=s2_send.at[d, k], recv_sem=s2_recv.at[d, k],
                device_id=(peer, col), device_id_type=pl.DeviceIdType.MESH)
            cp.start()
            step_copies.append(cp)
        copies2.append(step_copies)
    for d, (peer, sign, r0) in enumerate(lanes2):
        copies2[nx - 2][d].wait_recv()
        out_ref[r0:r0 + quarter] = (recv2[d, nx - 2] + acc[x, r0:r0 + quarter]).astype(out_ref.dtype)
    for step_copies in copies1 + copies2:
        for cp in step_copies:
            cp.wait_send()


def ring_reduce(part, nx, ny, splits=2):
    width = part.shape[-1]
    rows = part.shape[0] // (nx * ny)
    part = part.reshape(nx, ny, rows, width)
    n1 = nx * splits
    vmem = pltpu.MemorySpace.VMEM
    return pl.pallas_call(
        functools.partial(ring_reduce_kernel, nx, ny, splits),
        out_shape=jax.ShapeDtypeStruct((rows, width), jnp.bfloat16),
        in_specs=[pl.BlockSpec(memory_space=vmem)],
        out_specs=pl.BlockSpec(memory_space=vmem),
        scratch_shapes=[
            pltpu.VMEM((n1, ny - 1, rows // splits, width), jnp.bfloat16),
            pltpu.VMEM((n1, ny - 1, rows // splits, width), jnp.bfloat16),
            pltpu.VMEM((nx, rows, width), jnp.float32),
            pltpu.VMEM((4, nx - 1, rows // 4, width), jnp.float32),
            pltpu.VMEM((4, nx - 1, rows // 4, width), jnp.float32),
            pltpu.SemaphoreType.DMA((n1, ny - 1)),
            pltpu.SemaphoreType.DMA((n1, ny - 1)),
            pltpu.SemaphoreType.DMA((4, nx - 1)),
            pltpu.SemaphoreType.DMA((4, nx - 1)),
        ],
        compiler_params=pltpu.CompilerParams(
            collective_id=1, has_side_effects=True, vmem_limit_bytes=48 * 1024 * 1024
        ),
    )(part)


def ring_ffn_kernel(nx, ny, splits, tok_ref, wg_ref, wu_ref, wd_ref, out_ref, ret_ref, pbuf, recv1, send1,
                    acc, recv2, send2, s1_send, s1_recv, s2_send, s2_recv, r_send, r_recv):
    me = lax.axis_index("seq")
    col = lax.axis_index("exp")
    x = me // ny
    y = me % ny
    y_up = x * ny + (y + 1) % ny
    y_down = x * ny + (y + ny - 1) % ny
    x_up = ((x + 1) % nx) * ny + y
    x_down = ((x + nx - 1) % nx) * ny + y
    rows = tok_ref.shape[2]
    width = tok_ref.shape[3]
    piece = rows // splits
    quarter = rows // 4
    half_x = nx // 2

    def partials(c_up, c_down):
        tok = jnp.concatenate(
            [tok_ref[0:half_x, c_up].reshape(half_x * rows, width),
             tok_ref[half_x:nx, c_down].reshape((nx - half_x) * rows, width)], axis=0)
        gate = jnp.dot(tok, wg_ref[...], preferred_element_type=jnp.float32)
        upward = jnp.dot(tok, wu_ref[...], preferred_element_type=jnp.float32)
        act = (gate / (1.0 + jnp.exp(-gate)) * upward).astype(jnp.bfloat16)
        down = lax.dot_general(act, wd_ref[...], (((1,), (1,)), ((), ())),
                               preferred_element_type=jnp.float32)
        pbuf[...] = down.astype(jnp.bfloat16).reshape(nx, rows, width)

    n_exp = lax.axis_size("exp")
    group = rows // n_exp
    barrier = pltpu.get_barrier_semaphore()
    for peer in (y_up, y_down, x_up, x_down):
        pl.semaphore_signal(barrier, inc=1, device_id=(peer, col),
                            device_id_type=pl.DeviceIdType.MESH)
    for k in range(1, n_exp):
        pl.semaphore_signal(barrier, inc=1, device_id=(me, (col + k) % n_exp),
                            device_id_type=pl.DeviceIdType.MESH)
    pl.semaphore_wait(barrier, 4 + n_exp - 1)

    lanes = []
    for a in range(nx):
        for p in range(splits):
            if a < half_x:
                lanes.append((y_up, 1, a, p * piece))
            else:
                lanes.append((y_down, -1, a, p * piece))
    copies1 = []
    for k in range(ny - 1):
        partials((y - k - 1 + ny) % ny, (y + k + 1) % ny)
        step_copies = []
        for d, (peer, sign, a, r0) in enumerate(lanes):
            if k == 0:
                send1[d, k] = pbuf[a, r0:r0 + piece]
            else:
                copies1[k - 1][d].wait_recv()
                send1[d, k] = (recv1[d, k - 1].astype(jnp.float32)
                               + pbuf[a, r0:r0 + piece].astype(jnp.float32)).astype(send1.dtype)
            cp = pltpu.make_async_remote_copy(
                src_ref=send1.at[d, k], dst_ref=recv1.at[d, k],
                send_sem=s1_send.at[d, k], recv_sem=s1_recv.at[d, k],
                device_id=(peer, col), device_id_type=pl.DeviceIdType.MESH)
            cp.start()
            step_copies.append(cp)
        copies1.append(step_copies)
    partials(y, y)
    for d, (peer, sign, a, r0) in enumerate(lanes):
        copies1[ny - 2][d].wait_recv()
        acc[a, r0:r0 + piece] = (recv1[d, ny - 2].astype(jnp.float32)
                                 + pbuf[a, r0:r0 + piece].astype(jnp.float32))

    lanes2 = [(x_up, 1, 0), (x_up, 1, quarter), (x_down, -1, 2 * quarter), (x_down, -1, 3 * quarter)]
    copies2 = []
    for k in range(nx - 1):
        step_copies = []
        for d, (peer, sign, r0) in enumerate(lanes2):
            c = (x - sign * (k + 1) + 2 * nx) % nx
            if k == 0:
                src = acc.at[c, r0:r0 + quarter]
            else:
                copies2[k - 1][d].wait_recv()
                send2[d, k] = recv2[d, k - 1] + acc[c, r0:r0 + quarter]
                src = send2.at[d, k]
            cp = pltpu.make_async_remote_copy(
                src_ref=src, dst_ref=recv2.at[d, k],
                send_sem=s2_send.at[d, k], recv_sem=s2_recv.at[d, k],
                device_id=(peer, col), device_id_type=pl.DeviceIdType.MESH)
            cp.start()
            step_copies.append(cp)
        copies2.append(step_copies)
    for d, (peer, sign, r0) in enumerate(lanes2):
        copies2[nx - 2][d].wait_recv()
        out_ref[r0:r0 + quarter] = (recv2[d, nx - 2] + acc[x, r0:r0 + quarter]).astype(out_ref.dtype)
    back = []
    for k in range(1, n_exp):
        peer = (col + k) % n_exp
        cp = pltpu.make_async_remote_copy(
            src_ref=out_ref.at[pl.ds(peer * group, group)], dst_ref=ret_ref.at[col],
            send_sem=r_send.at[k - 1], recv_sem=r_recv.at[k - 1],
            device_id=(me, peer), device_id_type=pl.DeviceIdType.MESH)
        cp.start()
        back.append(cp)
    own = pltpu.make_async_copy(out_ref.at[pl.ds(col * group, group)], ret_ref.at[col], r_send.at[n_exp - 1])
    own.start()
    own.wait()
    for step_copies in copies1 + copies2:
        for cp in step_copies:
            cp.wait_send()
    for cp in back:
        cp.wait()


def ring_ffn(tokens, w_gate, w_up, w_down, nx, ny, n_exp, splits=2):
    width = tokens.shape[-1]
    rows = tokens.shape[0] // (nx * ny)
    tokens = tokens.reshape(nx, ny, rows, width)
    n1 = nx * splits
    vmem = pltpu.MemorySpace.VMEM
    return pl.pallas_call(
        functools.partial(ring_ffn_kernel, nx, ny, splits),
        out_shape=(jax.ShapeDtypeStruct((rows, width), jnp.bfloat16),
                   jax.ShapeDtypeStruct((n_exp, rows // n_exp, width), jnp.bfloat16)),
        in_specs=[pl.BlockSpec(memory_space=vmem)] * 4,
        out_specs=(pl.BlockSpec(memory_space=vmem), pl.BlockSpec(memory_space=vmem)),
        scratch_shapes=[
            pltpu.VMEM((nx, rows, width), jnp.bfloat16),
            pltpu.VMEM((n1, ny - 1, rows // splits, width), jnp.bfloat16),
            pltpu.VMEM((n1, ny - 1, rows // splits, width), jnp.bfloat16),
            pltpu.VMEM((nx, rows, width), jnp.float32),
            pltpu.VMEM((4, nx - 1, rows // 4, width), jnp.float32),
            pltpu.VMEM((4, nx - 1, rows // 4, width), jnp.float32),
            pltpu.SemaphoreType.DMA((n1, ny - 1)),
            pltpu.SemaphoreType.DMA((n1, ny - 1)),
            pltpu.SemaphoreType.DMA((4, nx - 1)),
            pltpu.SemaphoreType.DMA((4, nx - 1)),
            pltpu.SemaphoreType.DMA((n_exp,)),
            pltpu.SemaphoreType.DMA((n_exp - 1,)),
        ],
        compiler_params=pltpu.CompilerParams(
            collective_id=5, has_side_effects=True, vmem_limit_bytes=56 * 1024 * 1024
        ),
    )(tokens, w_gate, w_up, w_down)


def shift_exchange_kernel(offsets, axis, other, block_ref, out_ref, send_sems, recv_sems):
    n = lax.axis_size(axis)
    me = lax.axis_index(axis)
    col = lax.axis_index(other)

    def dev(peer):
        return (peer, col) if axis == "seq" else (col, peer)

    targets = [(me + o + n * len(offsets)) % n for o in offsets]
    barrier = pltpu.get_barrier_semaphore()
    for peer in targets:
        pl.semaphore_signal(barrier, inc=1, device_id=dev(peer),
                            device_id_type=pl.DeviceIdType.MESH)
    pl.semaphore_wait(barrier, len(offsets))
    copies = []
    for j, peer in enumerate(targets):
        cp = pltpu.make_async_remote_copy(
            src_ref=block_ref, dst_ref=out_ref.at[j],
            send_sem=send_sems.at[j], recv_sem=recv_sems.at[j],
            device_id=dev(peer), device_id_type=pl.DeviceIdType.MESH)
        cp.start()
        copies.append(cp)
    for cp in copies:
        cp.wait()


def shift_exchange(block, offsets, axis, other, cid):
    vmem = pltpu.MemorySpace.VMEM
    k = len(offsets)
    return pl.pallas_call(
        functools.partial(shift_exchange_kernel, tuple(offsets), axis, other),
        out_shape=jax.ShapeDtypeStruct((k,) + block.shape, block.dtype),
        in_specs=[pl.BlockSpec(memory_space=vmem)],
        out_specs=pl.BlockSpec(memory_space=vmem),
        scratch_shapes=[pltpu.SemaphoreType.DMA((k,)), pltpu.SemaphoreType.DMA((k,))],
        compiler_params=pltpu.CompilerParams(collective_id=cid, has_side_effects=True),
    )(block)


def exp_all_to_all_kernel(x_ref, y_ref, send_sems, recv_sems):
    n = lax.axis_size("exp")
    me = lax.axis_index("exp")
    row = lax.axis_index("seq")
    barrier = pltpu.get_barrier_semaphore()
    for k in range(1, n):
        pl.semaphore_signal(barrier, inc=1, device_id=(row, (me + k) % n),
                            device_id_type=pl.DeviceIdType.MESH)
    pl.semaphore_wait(barrier, n - 1)
    copies = []
    for k in range(1, n):
        peer = (me + k) % n
        cp = pltpu.make_async_remote_copy(
            src_ref=x_ref.at[peer], dst_ref=y_ref.at[me],
            send_sem=send_sems.at[k - 1], recv_sem=recv_sems.at[k - 1],
            device_id=(row, peer), device_id_type=pl.DeviceIdType.MESH)
        cp.start()
        copies.append(cp)
    y_ref[me] = x_ref[me]
    for cp in copies:
        cp.wait()


def exp_all_to_all(x, cid):
    n = x.shape[0]
    vmem = pltpu.MemorySpace.VMEM
    return pl.pallas_call(
        exp_all_to_all_kernel,
        out_shape=jax.ShapeDtypeStruct(x.shape, x.dtype),
        in_specs=[pl.BlockSpec(memory_space=vmem)],
        out_specs=pl.BlockSpec(memory_space=vmem),
        scratch_shapes=[pltpu.SemaphoreType.DMA((n - 1,)), pltpu.SemaphoreType.DMA((n - 1,))],
        compiler_params=pltpu.CompilerParams(collective_id=cid, has_side_effects=True),
    )(x)


def ring_gather_kernel(nx, ny, axis, other, pieces, route, skip, block_ref, out_ref, local_sem, send_sems, recv_sems,
                       r_send, r_recv):
    me = lax.axis_index(axis)
    col = lax.axis_index(other)
    x = me // ny
    y = me % ny
    rows = block_ref.shape[0]
    hr = rows // 2

    def dev(a, b):
        idx = (a + nx) % nx * ny + (b + ny) % ny
        return (idx, col) if axis == "seq" else (col, idx)

    peers = []
    reach = 2 if skip else 1
    for d in range(1, min(reach, ny // 2) + 1):
        peers += [dev(x, y + d), dev(x, y - d)]
    for d in range(1, min(reach, nx // 2) + 1):
        peers += [dev(x + d, y), dev(x - d, y)]
    n_other = lax.axis_size(other)
    barrier = pltpu.get_barrier_semaphore()
    for peer in peers:
        pl.semaphore_signal(barrier, inc=1, device_id=peer, device_id_type=pl.DeviceIdType.MESH)
    if route:
        for k in range(1, n_other):
            pl.semaphore_signal(barrier, inc=1, device_id=(me, (col + k) % n_other),
                                device_id_type=pl.DeviceIdType.MESH)
    pl.semaphore_wait(barrier, len(peers) + (n_other - 1 if route else 0))

    if route:
        group = rows // n_other
        routed = []
        for k in range(1, n_other):
            peer = (col + k) % n_other
            cp = pltpu.make_async_remote_copy(
                src_ref=block_ref.at[pl.ds(peer * group, group)],
                dst_ref=out_ref.at[x, y, pl.ds(col * group, group)],
                send_sem=r_send.at[k - 1], recv_sem=r_recv.at[k - 1],
                device_id=(me, peer), device_id_type=pl.DeviceIdType.MESH)
            cp.start()
            routed.append(cp)
        own = pltpu.make_async_copy(block_ref.at[pl.ds(col * group, group)],
                                    out_ref.at[x, y, pl.ds(col * group, group)], local_sem.at[0])
        own.start()
        own.wait()
        for cp in routed:
            cp.wait()
        block_ref = out_ref.at[x, y]
    else:
        own = pltpu.make_async_copy(block_ref, out_ref.at[x, y], local_sem.at[0])
        own.start()
    sem_count = [0]

    def unit(axis, stage, u, lo, hi):
        if axis == "y":
            return out_ref.at[x, u, lo:hi] if stage == 1 else out_ref.at[:, u, lo:hi]
        return out_ref.at[u, y, lo:hi] if stage == 1 else out_ref.at[u, :, lo:hi]

    def ring(axis, stage, lo, hi):
        n = ny if axis == "y" else nx
        c = y if axis == "y" else x
        half = n // 2
        mid = (lo + hi) // 2
        steps = []
        for sign in (1, -1):
            def rows_for(d):
                if d == half and n % 2 == 0:
                    return (lo, mid) if sign == 1 else (mid, hi)
                return (lo, hi)

            def target(d):
                return dev(x, y + sign * d) if axis == "y" else dev(x + sign * d, y)

            direct = {}
            for d in range(1, min(2, half) + 1):
                a_lo, a_hi = rows_for(d)
                src = block_ref.at[a_lo:a_hi] if stage == 1 else unit(axis, stage, c, a_lo, a_hi)
                j = sem_count[0]
                sem_count[0] += 1
                cp = pltpu.make_async_remote_copy(
                    src_ref=src, dst_ref=unit(axis, stage, c, a_lo, a_hi),
                    send_sem=send_sems.at[j], recv_sem=recv_sems.at[j],
                    device_id=target(d), device_id_type=pl.DeviceIdType.MESH)
                direct[d] = cp
                steps.append([(None, cp)])
            for d in range(3, half + 1):
                a_lo, a_hi = rows_for(d)
                u = (c - sign * (d - 2) + 2 * n) % n
                j = sem_count[0]
                sem_count[0] += 1
                cp = pltpu.make_async_remote_copy(
                    src_ref=unit(axis, stage, u, a_lo, a_hi), dst_ref=unit(axis, stage, u, a_lo, a_hi),
                    send_sem=send_sems.at[j], recv_sem=recv_sems.at[j],
                    device_id=target(2), device_id_type=pl.DeviceIdType.MESH)
                steps[len(steps) - min(2, half) + (d - 3)].append((direct[d - 2], cp))
        return steps

    def ring_chain(axis, stage, lo, hi):
        n = ny if axis == "y" else nx
        c = y if axis == "y" else x
        half = n // 2
        mid = (lo + hi) // 2
        steps = []
        for sign in (1, -1):
            prev = None
            lane = []
            for k in range(half):
                u = (c - sign * k + 2 * n) % n
                a_lo, a_hi = lo, hi
                if k == half - 1 and n % 2 == 0:
                    a_lo, a_hi = (lo, mid) if sign == 1 else (mid, hi)
                if stage == 1 and k == 0:
                    src = block_ref.at[a_lo:a_hi]
                else:
                    src = unit(axis, stage, u, a_lo, a_hi)
                dst = unit(axis, stage, u, a_lo, a_hi)
                target = dev(x, y + sign) if axis == "y" else dev(x + sign, y)
                j = sem_count[0]
                sem_count[0] += 1
                cp = pltpu.make_async_remote_copy(
                    src_ref=src, dst_ref=dst, send_sem=send_sems.at[j], recv_sem=recv_sems.at[j],
                    device_id=target, device_id_type=pl.DeviceIdType.MESH)
                lane.append((prev, cp))
                prev = cp
            steps.append(lane)
        return steps

    plans = []
    step = hr // pieces
    for p in range(pieces):
        for base, first, second in ((0, "y", "x"), (hr, "x", "y")):
            lo = base + p * step
            s1 = (ring if skip else ring_chain)(first, 1, lo, lo + step)
            s2 = (ring if skip else ring_chain)(second, 2, lo, lo + step)
            plans.append((s1, s2))

    started = []

    def run(lane_list):
        depth = max(len(l) for l in lane_list)
        for k in range(depth):
            for lane in lane_list:
                if k < len(lane):
                    prev, cp = lane[k]
                    if prev is not None:
                        prev.wait_recv()
                    cp.start()
                    started.append(cp)

    run([lane for s1, _ in plans for lane in s1])
    for s1, _ in plans:
        for lane in s1:
            lane[-1][1].wait_recv()
    if not route:
        own.wait()
    run([lane for _, s2 in plans for lane in s2])
    for _, s2 in plans:
        for lane in s2:
            lane[-1][1].wait_recv()
    for cp in started:
        cp.wait_send()


def ring_gather(block, nx, ny, axis="seq", other="exp", cid=3, pieces=1, route=False, n_other=2,
                skip=False):
    vmem = pltpu.MemorySpace.VMEM
    n_sems = 4 * pieces * (nx // 2 + ny // 2) + 4
    return pl.pallas_call(
        functools.partial(ring_gather_kernel, nx, ny, axis, other, pieces, route, skip),
        out_shape=jax.ShapeDtypeStruct((nx, ny) + block.shape, block.dtype),
        in_specs=[pl.BlockSpec(memory_space=vmem)],
        out_specs=pl.BlockSpec(memory_space=vmem),
        scratch_shapes=[
            pltpu.SemaphoreType.DMA((1,)),
            pltpu.SemaphoreType.DMA((n_sems,)),
            pltpu.SemaphoreType.DMA((n_sems,)),
            pltpu.SemaphoreType.DMA((n_other,)),
            pltpu.SemaphoreType.DMA((n_other,)),
        ],
        compiler_params=pltpu.CompilerParams(
            collective_id=cid, has_side_effects=True, vmem_limit_bytes=48 * 1024 * 1024
        ),
    )(block)


def rms_scale(matrix, gain):
    mean_square = jnp.mean(matrix * matrix, axis=-1, keepdims=True)
    return matrix * lax.rsqrt(mean_square + EPSILON) * gain


def expert_terms(block, gate_slice, up_slice, down_slice):
    gate = jnp.einsum("nek,ekf->nef", block, gate_slice, preferred_element_type=jnp.float32)
    upward = jnp.einsum("nek,ekf->nef", block, up_slice, preferred_element_type=jnp.float32)
    act = (jax.nn.silu(gate) * upward).astype(jnp.bfloat16)
    return jnp.einsum("nef,ekf->nek", act, down_slice, preferred_element_type=jnp.float32)


def local(
    tokens,
    array_type,
    block_pattern,
    gain_attn,
    w_query,
    w_key,
    w_value,
    logit_scale,
    w_out,
    gain_ffn,
    w_gate,
    w_up,
    w_down,
):
    n_exp = lax.axis_size("exp")
    row_count = tokens.shape[0]
    width = tokens.shape[1]
    head_cols = w_query.shape[1]
    heads_dev = logit_scale.shape[0]
    head_size = head_cols // heads_dev
    n_blocks = block_pattern.shape[0]
    inputs = tokens.astype(jnp.float32)
    normed_attn = rms_scale(inputs, gain_attn).astype(jnp.bfloat16)
    projector = jnp.concatenate([w_query, w_key, w_value], axis=1)
    joined_qkv = jnp.dot(
        ring_gather(normed_attn, n_exp // CORES, CORES, "exp", "seq", 4, pieces=2, skip=True).reshape(n_exp * row_count, width),
        projector,
        preferred_element_type=jnp.float32,
    ).astype(jnp.bfloat16)
    block_len = joined_qkv.shape[0]
    query_heads = joined_qkv[:, :head_cols].reshape(block_len, heads_dev, head_size)
    key_value = joined_qkv[:, head_cols:]
    position = lax.axis_index("seq")
    head_scale = logit_scale[:, None, None]

    offsets = [d for d in range(1, REACH + 1)] + [-d for d in range(1, REACH + 1)]
    neighbours = shift_exchange(key_value, offsets, "seq", "exp", 2)
    band = jnp.concatenate([key_value[None], neighbours], axis=0)
    n_band = band.shape[0]
    sources = jnp.stack([position] + [(position - o) % n_blocks for o in offsets])
    allowed = jnp.repeat(block_pattern[position, sources] > 0, block_len)
    key_band = band[:, :, :head_cols].reshape(n_band * block_len, heads_dev, head_size)
    value_band = band[:, :, head_cols:].reshape(n_band * block_len, heads_dev, head_size)
    scores = (
        jnp.einsum("qhd,khd->hqk", query_heads, key_band, preferred_element_type=jnp.float32)
        * head_scale
    )
    scores = jnp.where(allowed[None, None, :], scores, -jnp.inf)
    row_top = jnp.max(scores, axis=2, keepdims=True)
    weights = jnp.exp(scores - row_top)
    weight_sum = jnp.sum(weights, axis=2)
    weighted = jnp.einsum(
        "hqk,khd->qhd",
        weights.astype(jnp.bfloat16),
        value_band,
        preferred_element_type=jnp.float32,
    )
    heads_out = (
        (weighted / jnp.transpose(weight_sum)[:, :, None])
        .astype(jnp.bfloat16)
        .reshape(block_len, head_cols)
    )
    all_heads = lax.all_to_all(heads_out, "exp", split_axis=0, concat_axis=1, tiled=True)
    attn_out = jnp.dot(
        all_heads,
        lax.all_gather(w_out, "exp", axis=0, tiled=True),
        preferred_element_type=jnp.float32,
    )
    hidden_state = inputs + attn_out
    normed_ffn = rms_scale(hidden_state, gain_ffn).astype(jnp.bfloat16)
    experts_dev = w_gate.shape[0]
    n_total = experts_dev * n_exp
    capacity = 2 * row_count // n_total
    one_hot = (array_type[:, None] == jnp.arange(n_total, dtype=jnp.int32)[None, :]).astype(
        jnp.int32
    )
    slot_rank = jnp.sum(jnp.cumsum(one_hot, axis=0) * one_hot, axis=1) - 1
    owner = array_type // experts_dev
    local_expert = array_type % experts_dev
    slot_id = (owner * capacity + slot_rank) * experts_dev + local_expert
    n_slots = n_exp * capacity * experts_dev
    selector = (slot_id[None, :] == jnp.arange(n_slots, dtype=jnp.int32)[:, None]).astype(
        jnp.bfloat16
    )
    outgoing = jnp.dot(selector, normed_ffn, preferred_element_type=jnp.float32).astype(
        jnp.bfloat16
    )
    outgoing = outgoing.reshape(n_exp * capacity, experts_dev, width)
    n_seq = lax.axis_size("seq")
    y_size = Y_RING if n_seq % Y_RING == 0 else n_seq
    gathered = ring_gather(
        outgoing.reshape(-1, width), n_seq // y_size, y_size, pieces=2, route=True, n_other=n_exp
    ).reshape((n_seq * outgoing.shape[0],) + outgoing.shape[1:])
    n_seq = lax.axis_size("seq")
    y_size = Y_RING if n_seq % Y_RING == 0 else n_seq
    returned = ring_ffn(
        gathered.reshape(gathered.shape[0], width),
        w_gate[0], w_up[0], w_down[0], n_seq // y_size, y_size, n_exp,
    )[1].reshape((-1,) + gathered.shape[1:])
    expert_out = jnp.dot(
        jnp.transpose(selector),
        returned.reshape(n_slots, width),
        preferred_element_type=jnp.float32,
    )
    return (hidden_state + expert_out).astype(jnp.bfloat16)


def solution(mesh):
    return jax.shard_map(
        local,
        mesh=mesh,
        in_specs=(
            P(("seq", "exp"), None),
            P(("seq", "exp")),
            P(),
            P(),
            P(None, "exp"),
            P(None, "exp"),
            P(None, "exp"),
            P("exp"),
            P("exp", None),
            P(),
            P("exp", None, "seq"),
            P("exp", None, "seq"),
            P("exp", None, "seq"),
        ),
        out_specs=P(("seq", "exp"), None),
        check_vma=False,
    )
```

```python
import jax
import jax.numpy as jnp
from jax import lax
from jax.sharding import PartitionSpec as P
from jax.experimental import pallas as pl
from jax.experimental.pallas import tpu as pltpu
import functools

REACH = 3
Y_RING = 8
CORES = 2


EPSILON = 1e-05


def passed_along(block, axis, distance):
    devices = range(lax.axis_size(axis))
    route = [((i - distance) % len(devices), i) for i in devices]
    return lax.ppermute(block, axis, route)


def ring_reduce_kernel(nx, ny, splits, part_ref, out_ref, recv1, send1, acc, recv2, send2,
                       s1_send, s1_recv, s2_send, s2_recv):
    me = lax.axis_index("seq")
    col = lax.axis_index("exp")
    x = me // ny
    y = me % ny
    y_up = x * ny + (y + 1) % ny
    y_down = x * ny + (y + ny - 1) % ny
    x_up = ((x + 1) % nx) * ny + y
    x_down = ((x + nx - 1) % nx) * ny + y
    rows = part_ref.shape[2]
    piece = rows // splits
    quarter = rows // 4

    barrier = pltpu.get_barrier_semaphore()
    for peer in (y_up, y_down, x_up, x_down):
        pl.semaphore_signal(barrier, inc=1, device_id=(peer, col),
                            device_id_type=pl.DeviceIdType.MESH)
    pl.semaphore_wait(barrier, 4)

    lanes = []
    for a in range(nx):
        for p in range(splits):
            if a < nx // 2:
                lanes.append((y_up, 1, a, p * piece))
            else:
                lanes.append((y_down, -1, a, p * piece))
    copies1 = []
    for k in range(ny - 1):
        step_copies = []
        for d, (peer, sign, a, r0) in enumerate(lanes):
            c = (y - sign * (k + 1) + 2 * ny) % ny
            if k == 0:
                src = part_ref.at[a, c, r0:r0 + piece]
            else:
                copies1[k - 1][d].wait_recv()
                send1[d, k] = (recv1[d, k - 1].astype(jnp.float32)
                               + part_ref[a, c, r0:r0 + piece].astype(jnp.float32)).astype(send1.dtype)
                src = send1.at[d, k]
            cp = pltpu.make_async_remote_copy(
                src_ref=src, dst_ref=recv1.at[d, k],
                send_sem=s1_send.at[d, k], recv_sem=s1_recv.at[d, k],
                device_id=(peer, col), device_id_type=pl.DeviceIdType.MESH)
            cp.start()
            step_copies.append(cp)
        copies1.append(step_copies)
    for d, (peer, sign, a, r0) in enumerate(lanes):
        copies1[ny - 2][d].wait_recv()
        acc[a, r0:r0 + piece] = (recv1[d, ny - 2].astype(jnp.float32)
                                 + part_ref[a, y, r0:r0 + piece].astype(jnp.float32))

    lanes2 = [(x_up, 1, 0), (x_up, 1, quarter), (x_down, -1, 2 * quarter), (x_down, -1, 3 * quarter)]
    copies2 = []
    for k in range(nx - 1):
        step_copies = []
        for d, (peer, sign, r0) in enumerate(lanes2):
            c = (x - sign * (k + 1) + 2 * nx) % nx
            if k == 0:
                src = acc.at[c, r0:r0 + quarter]
            else:
                copies2[k - 1][d].wait_recv()
                send2[d, k] = recv2[d, k - 1] + acc[c, r0:r0 + quarter]
                src = send2.at[d, k]
            cp = pltpu.make_async_remote_copy(
                src_ref=src, dst_ref=recv2.at[d, k],
                send_sem=s2_send.at[d, k], recv_sem=s2_recv.at[d, k],
                device_id=(peer, col), device_id_type=pl.DeviceIdType.MESH)
            cp.start()
            step_copies.append(cp)
        copies2.append(step_copies)
    for d, (peer, sign, r0) in enumerate(lanes2):
        copies2[nx - 2][d].wait_recv()
        out_ref[r0:r0 + quarter] = (recv2[d, nx - 2] + acc[x, r0:r0 + quarter]).astype(out_ref.dtype)
    for step_copies in copies1 + copies2:
        for cp in step_copies:
            cp.wait_send()


def ring_reduce(part, nx, ny, splits=2):
    width = part.shape[-1]
    rows = part.shape[0] // (nx * ny)
    part = part.reshape(nx, ny, rows, width)
    n1 = nx * splits
    vmem = pltpu.MemorySpace.VMEM
    return pl.pallas_call(
        functools.partial(ring_reduce_kernel, nx, ny, splits),
        out_shape=jax.ShapeDtypeStruct((rows, width), jnp.bfloat16),
        in_specs=[pl.BlockSpec(memory_space=vmem)],
        out_specs=pl.BlockSpec(memory_space=vmem),
        scratch_shapes=[
            pltpu.VMEM((n1, ny - 1, rows // splits, width), jnp.bfloat16),
            pltpu.VMEM((n1, ny - 1, rows // splits, width), jnp.bfloat16),
            pltpu.VMEM((nx, rows, width), jnp.float32),
            pltpu.VMEM((4, nx - 1, rows // 4, width), jnp.float32),
            pltpu.VMEM((4, nx - 1, rows // 4, width), jnp.float32),
            pltpu.SemaphoreType.DMA((n1, ny - 1)),
            pltpu.SemaphoreType.DMA((n1, ny - 1)),
            pltpu.SemaphoreType.DMA((4, nx - 1)),
            pltpu.SemaphoreType.DMA((4, nx - 1)),
        ],
        compiler_params=pltpu.CompilerParams(
            collective_id=1, has_side_effects=True, vmem_limit_bytes=48 * 1024 * 1024
        ),
    )(part)


def ring_ffn_kernel(nx, ny, splits, tok_ref, wg_ref, wu_ref, wd_ref, out_ref, ret_ref, pbuf, recv1, send1,
                    acc, recv2, send2, s1_send, s1_recv, s2_send, s2_recv, r_send, r_recv):
    me = lax.axis_index("seq")
    col = lax.axis_index("exp")
    x = me // ny
    y = me % ny
    y_up = x * ny + (y + 1) % ny
    y_down = x * ny + (y + ny - 1) % ny
    x_up = ((x + 1) % nx) * ny + y
    x_down = ((x + nx - 1) % nx) * ny + y
    rows = tok_ref.shape[2]
    width = tok_ref.shape[3]
    piece = rows // splits
    quarter = rows // 4
    half_x = nx // 2

    def partials(c_up, c_down):
        tok = jnp.concatenate(
            [tok_ref[0:half_x, c_up].reshape(half_x * rows, width),
             tok_ref[half_x:nx, c_down].reshape((nx - half_x) * rows, width)], axis=0)
        gate = jnp.dot(tok, wg_ref[...], preferred_element_type=jnp.float32)
        upward = jnp.dot(tok, wu_ref[...], preferred_element_type=jnp.float32)
        act = (gate / (1.0 + jnp.exp(-gate)) * upward).astype(jnp.bfloat16)
        down = lax.dot_general(act, wd_ref[...], (((1,), (1,)), ((), ())),
                               preferred_element_type=jnp.float32)
        pbuf[...] = down.astype(jnp.bfloat16).reshape(nx, rows, width)

    n_exp = lax.axis_size("exp")
    group = rows // n_exp
    barrier = pltpu.get_barrier_semaphore()
    for peer in (y_up, y_down, x_up, x_down):
        pl.semaphore_signal(barrier, inc=1, device_id=(peer, col),
                            device_id_type=pl.DeviceIdType.MESH)
    for k in range(1, n_exp):
        pl.semaphore_signal(barrier, inc=1, device_id=(me, (col + k) % n_exp),
                            device_id_type=pl.DeviceIdType.MESH)
    pl.semaphore_wait(barrier, 4 + n_exp - 1)

    lanes = []
    for a in range(nx):
        for p in range(splits):
            if a < half_x:
                lanes.append((y_up, 1, a, p * piece))
            else:
                lanes.append((y_down, -1, a, p * piece))
    copies1 = []
    for k in range(ny - 1):
        partials((y - k - 1 + ny) % ny, (y + k + 1) % ny)
        step_copies = []
        for d, (peer, sign, a, r0) in enumerate(lanes):
            if k == 0:
                send1[d, k] = pbuf[a, r0:r0 + piece]
            else:
                copies1[k - 1][d].wait_recv()
                send1[d, k] = (recv1[d, k - 1].astype(jnp.float32)
                               + pbuf[a, r0:r0 + piece].astype(jnp.float32)).astype(send1.dtype)
            cp = pltpu.make_async_remote_copy(
                src_ref=send1.at[d, k], dst_ref=recv1.at[d, k],
                send_sem=s1_send.at[d, k], recv_sem=s1_recv.at[d, k],
                device_id=(peer, col), device_id_type=pl.DeviceIdType.MESH)
            cp.start()
            step_copies.append(cp)
        copies1.append(step_copies)
    partials(y, y)
    for d, (peer, sign, a, r0) in enumerate(lanes):
        copies1[ny - 2][d].wait_recv()
        acc[a, r0:r0 + piece] = (recv1[d, ny - 2].astype(jnp.float32)
                                 + pbuf[a, r0:r0 + piece].astype(jnp.float32))

    lanes2 = [(x_up, 1, 0), (x_up, 1, quarter), (x_down, -1, 2 * quarter), (x_down, -1, 3 * quarter)]
    copies2 = []
    for k in range(nx - 1):
        step_copies = []
        for d, (peer, sign, r0) in enumerate(lanes2):
            c = (x - sign * (k + 1) + 2 * nx) % nx
            if k == 0:
                src = acc.at[c, r0:r0 + quarter]
            else:
                copies2[k - 1][d].wait_recv()
                send2[d, k] = recv2[d, k - 1] + acc[c, r0:r0 + quarter]
                src = send2.at[d, k]
            cp = pltpu.make_async_remote_copy(
                src_ref=src, dst_ref=recv2.at[d, k],
                send_sem=s2_send.at[d, k], recv_sem=s2_recv.at[d, k],
                device_id=(peer, col), device_id_type=pl.DeviceIdType.MESH)
            cp.start()
            step_copies.append(cp)
        copies2.append(step_copies)
    for d, (peer, sign, r0) in enumerate(lanes2):
        copies2[nx - 2][d].wait_recv()
        out_ref[r0:r0 + quarter] = (recv2[d, nx - 2] + acc[x, r0:r0 + quarter]).astype(out_ref.dtype)
    back = []
    for k in range(1, n_exp):
        peer = (col + k) % n_exp
        cp = pltpu.make_async_remote_copy(
            src_ref=out_ref.at[pl.ds(peer * group, group)], dst_ref=ret_ref.at[col],
            send_sem=r_send.at[k - 1], recv_sem=r_recv.at[k - 1],
            device_id=(me, peer), device_id_type=pl.DeviceIdType.MESH)
        cp.start()
        back.append(cp)
    own = pltpu.make_async_copy(out_ref.at[pl.ds(col * group, group)], ret_ref.at[col], r_send.at[n_exp - 1])
    own.start()
    own.wait()
    for step_copies in copies1 + copies2:
        for cp in step_copies:
            cp.wait_send()
    for cp in back:
        cp.wait()


def ring_ffn(tokens, w_gate, w_up, w_down, nx, ny, n_exp, splits=2):
    width = tokens.shape[-1]
    rows = tokens.shape[0] // (nx * ny)
    tokens = tokens.reshape(nx, ny, rows, width)
    n1 = nx * splits
    vmem = pltpu.MemorySpace.VMEM
    return pl.pallas_call(
        functools.partial(ring_ffn_kernel, nx, ny, splits),
        out_shape=(jax.ShapeDtypeStruct((rows, width), jnp.bfloat16),
                   jax.ShapeDtypeStruct((n_exp, rows // n_exp, width), jnp.bfloat16)),
        in_specs=[pl.BlockSpec(memory_space=vmem)] * 4,
        out_specs=(pl.BlockSpec(memory_space=vmem), pl.BlockSpec(memory_space=vmem)),
        scratch_shapes=[
            pltpu.VMEM((nx, rows, width), jnp.bfloat16),
            pltpu.VMEM((n1, ny - 1, rows // splits, width), jnp.bfloat16),
            pltpu.VMEM((n1, ny - 1, rows // splits, width), jnp.bfloat16),
            pltpu.VMEM((nx, rows, width), jnp.float32),
            pltpu.VMEM((4, nx - 1, rows // 4, width), jnp.float32),
            pltpu.VMEM((4, nx - 1, rows // 4, width), jnp.float32),
            pltpu.SemaphoreType.DMA((n1, ny - 1)),
            pltpu.SemaphoreType.DMA((n1, ny - 1)),
            pltpu.SemaphoreType.DMA((4, nx - 1)),
            pltpu.SemaphoreType.DMA((4, nx - 1)),
            pltpu.SemaphoreType.DMA((n_exp,)),
            pltpu.SemaphoreType.DMA((n_exp - 1,)),
        ],
        compiler_params=pltpu.CompilerParams(
            collective_id=5, has_side_effects=True, vmem_limit_bytes=56 * 1024 * 1024
        ),
    )(tokens, w_gate, w_up, w_down)


def shift_exchange_kernel(offsets, axis, other, block_ref, out_ref, send_sems, recv_sems):
    n = lax.axis_size(axis)
    me = lax.axis_index(axis)
    col = lax.axis_index(other)

    def dev(peer):
        return (peer, col) if axis == "seq" else (col, peer)

    targets = [(me + o + n * len(offsets)) % n for o in offsets]
    barrier = pltpu.get_barrier_semaphore()
    for peer in targets:
        pl.semaphore_signal(barrier, inc=1, device_id=dev(peer),
                            device_id_type=pl.DeviceIdType.MESH)
    pl.semaphore_wait(barrier, len(offsets))
    copies = []
    for j, peer in enumerate(targets):
        cp = pltpu.make_async_remote_copy(
            src_ref=block_ref, dst_ref=out_ref.at[j],
            send_sem=send_sems.at[j], recv_sem=recv_sems.at[j],
            device_id=dev(peer), device_id_type=pl.DeviceIdType.MESH)
        cp.start()
        copies.append(cp)
    for cp in copies:
        cp.wait()


def shift_exchange(block, offsets, axis, other, cid):
    vmem = pltpu.MemorySpace.VMEM
    k = len(offsets)
    return pl.pallas_call(
        functools.partial(shift_exchange_kernel, tuple(offsets), axis, other),
        out_shape=jax.ShapeDtypeStruct((k,) + block.shape, block.dtype),
        in_specs=[pl.BlockSpec(memory_space=vmem)],
        out_specs=pl.BlockSpec(memory_space=vmem),
        scratch_shapes=[pltpu.SemaphoreType.DMA((k,)), pltpu.SemaphoreType.DMA((k,))],
        compiler_params=pltpu.CompilerParams(collective_id=cid, has_side_effects=True),
    )(block)


def exp_all_to_all_kernel(x_ref, y_ref, send_sems, recv_sems):
    n = lax.axis_size("exp")
    me = lax.axis_index("exp")
    row = lax.axis_index("seq")
    barrier = pltpu.get_barrier_semaphore()
    for k in range(1, n):
        pl.semaphore_signal(barrier, inc=1, device_id=(row, (me + k) % n),
                            device_id_type=pl.DeviceIdType.MESH)
    pl.semaphore_wait(barrier, n - 1)
    copies = []
    for k in range(1, n):
        peer = (me + k) % n
        cp = pltpu.make_async_remote_copy(
            src_ref=x_ref.at[peer], dst_ref=y_ref.at[me],
            send_sem=send_sems.at[k - 1], recv_sem=recv_sems.at[k - 1],
            device_id=(row, peer), device_id_type=pl.DeviceIdType.MESH)
        cp.start()
        copies.append(cp)
    y_ref[me] = x_ref[me]
    for cp in copies:
        cp.wait()


def exp_all_to_all(x, cid):
    n = x.shape[0]
    vmem = pltpu.MemorySpace.VMEM
    return pl.pallas_call(
        exp_all_to_all_kernel,
        out_shape=jax.ShapeDtypeStruct(x.shape, x.dtype),
        in_specs=[pl.BlockSpec(memory_space=vmem)],
        out_specs=pl.BlockSpec(memory_space=vmem),
        scratch_shapes=[pltpu.SemaphoreType.DMA((n - 1,)), pltpu.SemaphoreType.DMA((n - 1,))],
        compiler_params=pltpu.CompilerParams(collective_id=cid, has_side_effects=True),
    )(x)


def ring_gather_kernel(nx, ny, axis, other, pieces, route, skip, block_ref, out_ref, local_sem, send_sems, recv_sems,
                       r_send, r_recv):
    me = lax.axis_index(axis)
    col = lax.axis_index(other)
    x = me // ny
    y = me % ny
    rows = block_ref.shape[0]
    hr = rows // 2

    def dev(a, b):
        idx = (a + nx) % nx * ny + (b + ny) % ny
        return (idx, col) if axis == "seq" else (col, idx)

    peers = []
    reach = 2 if skip else 1
    for d in range(1, min(reach, ny // 2) + 1):
        peers += [dev(x, y + d), dev(x, y - d)]
    for d in range(1, min(reach, nx // 2) + 1):
        peers += [dev(x + d, y), dev(x - d, y)]
    n_other = lax.axis_size(other)
    barrier = pltpu.get_barrier_semaphore()
    for peer in peers:
        pl.semaphore_signal(barrier, inc=1, device_id=peer, device_id_type=pl.DeviceIdType.MESH)
    if route:
        for k in range(1, n_other):
            pl.semaphore_signal(barrier, inc=1, device_id=(me, (col + k) % n_other),
                                device_id_type=pl.DeviceIdType.MESH)
    pl.semaphore_wait(barrier, len(peers) + (n_other - 1 if route else 0))

    if route:
        group = rows // n_other
        routed = []
        for k in range(1, n_other):
            peer = (col + k) % n_other
            cp = pltpu.make_async_remote_copy(
                src_ref=block_ref.at[pl.ds(peer * group, group)],
                dst_ref=out_ref.at[x, y, pl.ds(col * group, group)],
                send_sem=r_send.at[k - 1], recv_sem=r_recv.at[k - 1],
                device_id=(me, peer), device_id_type=pl.DeviceIdType.MESH)
            cp.start()
            routed.append(cp)
        own = pltpu.make_async_copy(block_ref.at[pl.ds(col * group, group)],
                                    out_ref.at[x, y, pl.ds(col * group, group)], local_sem.at[0])
        own.start()
        own.wait()
        for cp in routed:
            cp.wait()
        block_ref = out_ref.at[x, y]
    else:
        own = pltpu.make_async_copy(block_ref, out_ref.at[x, y], local_sem.at[0])
        own.start()
    sem_count = [0]

    def unit(axis, stage, u, lo, hi):
        if axis == "y":
            return out_ref.at[x, u, lo:hi] if stage == 1 else out_ref.at[:, u, lo:hi]
        return out_ref.at[u, y, lo:hi] if stage == 1 else out_ref.at[u, :, lo:hi]

    def ring(axis, stage, lo, hi):
        n = ny if axis == "y" else nx
        c = y if axis == "y" else x
        half = n // 2
        mid = (lo + hi) // 2
        steps = []
        for sign in (1, -1):
            def rows_for(d):
                if d == half and n % 2 == 0:
                    return (lo, mid) if sign == 1 else (mid, hi)
                return (lo, hi)

            def target(d):
                return dev(x, y + sign * d) if axis == "y" else dev(x + sign * d, y)

            direct = {}
            for d in range(1, min(2, half) + 1):
                a_lo, a_hi = rows_for(d)
                src = block_ref.at[a_lo:a_hi] if stage == 1 else unit(axis, stage, c, a_lo, a_hi)
                j = sem_count[0]
                sem_count[0] += 1
                cp = pltpu.make_async_remote_copy(
                    src_ref=src, dst_ref=unit(axis, stage, c, a_lo, a_hi),
                    send_sem=send_sems.at[j], recv_sem=recv_sems.at[j],
                    device_id=target(d), device_id_type=pl.DeviceIdType.MESH)
                direct[d] = cp
                steps.append([(None, cp)])
            for d in range(3, half + 1):
                a_lo, a_hi = rows_for(d)
                u = (c - sign * (d - 2) + 2 * n) % n
                j = sem_count[0]
                sem_count[0] += 1
                cp = pltpu.make_async_remote_copy(
                    src_ref=unit(axis, stage, u, a_lo, a_hi), dst_ref=unit(axis, stage, u, a_lo, a_hi),
                    send_sem=send_sems.at[j], recv_sem=recv_sems.at[j],
                    device_id=target(2), device_id_type=pl.DeviceIdType.MESH)
                steps[len(steps) - min(2, half) + (d - 3)].append((direct[d - 2], cp))
        return steps

    def ring_chain(axis, stage, lo, hi):
        n = ny if axis == "y" else nx
        c = y if axis == "y" else x
        half = n // 2
        mid = (lo + hi) // 2
        steps = []
        for sign in (1, -1):
            prev = None
            lane = []
            for k in range(half):
                u = (c - sign * k + 2 * n) % n
                a_lo, a_hi = lo, hi
                if k == half - 1 and n % 2 == 0:
                    a_lo, a_hi = (lo, mid) if sign == 1 else (mid, hi)
                if stage == 1 and k == 0:
                    src = block_ref.at[a_lo:a_hi]
                else:
                    src = unit(axis, stage, u, a_lo, a_hi)
                dst = unit(axis, stage, u, a_lo, a_hi)
                target = dev(x, y + sign) if axis == "y" else dev(x + sign, y)
                j = sem_count[0]
                sem_count[0] += 1
                cp = pltpu.make_async_remote_copy(
                    src_ref=src, dst_ref=dst, send_sem=send_sems.at[j], recv_sem=recv_sems.at[j],
                    device_id=target, device_id_type=pl.DeviceIdType.MESH)
                lane.append((prev, cp))
                prev = cp
            steps.append(lane)
        return steps

    plans = []
    step = hr // pieces
    for p in range(pieces):
        for base, first, second in ((0, "y", "x"), (hr, "x", "y")):
            lo = base + p * step
            s1 = (ring if skip else ring_chain)(first, 1, lo, lo + step)
            s2 = (ring if skip else ring_chain)(second, 2, lo, lo + step)
            plans.append((s1, s2))

    started = []

    def run(lane_list):
        depth = max(len(l) for l in lane_list)
        for k in range(depth):
            for lane in lane_list:
                if k < len(lane):
                    prev, cp = lane[k]
                    if prev is not None:
                        prev.wait_recv()
                    cp.start()
                    started.append(cp)

    run([lane for s1, _ in plans for lane in s1])
    for s1, _ in plans:
        for lane in s1:
            lane[-1][1].wait_recv()
    if not route:
        own.wait()
    run([lane for _, s2 in plans for lane in s2])
    for _, s2 in plans:
        for lane in s2:
            lane[-1][1].wait_recv()
    for cp in started:
        cp.wait_send()


def ring_gather(block, nx, ny, axis="seq", other="exp", cid=3, pieces=1, route=False, n_other=2,
                skip=False):
    vmem = pltpu.MemorySpace.VMEM
    n_sems = 4 * pieces * (nx // 2 + ny // 2) + 4
    return pl.pallas_call(
        functools.partial(ring_gather_kernel, nx, ny, axis, other, pieces, route, skip),
        out_shape=jax.ShapeDtypeStruct((nx, ny) + block.shape, block.dtype),
        in_specs=[pl.BlockSpec(memory_space=vmem)],
        out_specs=pl.BlockSpec(memory_space=vmem),
        scratch_shapes=[
            pltpu.SemaphoreType.DMA((1,)),
            pltpu.SemaphoreType.DMA((n_sems,)),
            pltpu.SemaphoreType.DMA((n_sems,)),
            pltpu.SemaphoreType.DMA((n_other,)),
            pltpu.SemaphoreType.DMA((n_other,)),
        ],
        compiler_params=pltpu.CompilerParams(
            collective_id=cid, has_side_effects=True, vmem_limit_bytes=48 * 1024 * 1024
        ),
    )(block)


def rms_scale(matrix, gain):
    mean_square = jnp.mean(matrix * matrix, axis=-1, keepdims=True)
    return matrix * lax.rsqrt(mean_square + EPSILON) * gain


def expert_terms(block, gate_slice, up_slice, down_slice):
    gate = jnp.einsum("nek,ekf->nef", block, gate_slice, preferred_element_type=jnp.float32)
    upward = jnp.einsum("nek,ekf->nef", block, up_slice, preferred_element_type=jnp.float32)
    act = (jax.nn.silu(gate) * upward).astype(jnp.bfloat16)
    return jnp.einsum("nef,ekf->nek", act, down_slice, preferred_element_type=jnp.float32)


def local(
    tokens,
    array_type,
    block_pattern,
    gain_attn,
    w_query,
    w_key,
    w_value,
    logit_scale,
    w_out,
    gain_ffn,
    w_gate,
    w_up,
    w_down,
):
    n_exp = lax.axis_size("exp")
    row_count = tokens.shape[0]
    width = tokens.shape[1]
    head_cols = w_query.shape[1]
    heads_dev = logit_scale.shape[0]
    head_size = head_cols // heads_dev
    n_blocks = block_pattern.shape[0]
    inputs = tokens.astype(jnp.float32)
    normed_attn = rms_scale(inputs, gain_attn).astype(jnp.bfloat16)
    projector = jnp.concatenate([w_query, w_key, w_value], axis=1)
    joined_qkv = jnp.dot(
        ring_gather(normed_attn, n_exp // CORES, CORES, "exp", "seq", 4, skip=True).reshape(n_exp * row_count, width),
        projector,
        preferred_element_type=jnp.float32,
    ).astype(jnp.bfloat16)
    block_len = joined_qkv.shape[0]
    query_heads = joined_qkv[:, :head_cols].reshape(block_len, heads_dev, head_size)
    key_value = joined_qkv[:, head_cols:]
    position = lax.axis_index("seq")
    head_scale = logit_scale[:, None, None]

    offsets = [d for d in range(1, REACH + 1)] + [-d for d in range(1, REACH + 1)]
    neighbours = shift_exchange(key_value, offsets, "seq", "exp", 2)
    band = jnp.concatenate([key_value[None], neighbours], axis=0)
    n_band = band.shape[0]
    sources = jnp.stack([position] + [(position - o) % n_blocks for o in offsets])
    allowed = jnp.repeat(block_pattern[position, sources] > 0, block_len)
    key_band = band[:, :, :head_cols].reshape(n_band * block_len, heads_dev, head_size)
    value_band = band[:, :, head_cols:].reshape(n_band * block_len, heads_dev, head_size)
    scores = (
        jnp.einsum("qhd,khd->hqk", query_heads, key_band, preferred_element_type=jnp.float32)
        * head_scale
    )
    scores = jnp.where(allowed[None, None, :], scores, -jnp.inf)
    row_top = jnp.max(scores, axis=2, keepdims=True)
    weights = jnp.exp(scores - row_top)
    weight_sum = jnp.sum(weights, axis=2)
    weighted = jnp.einsum(
        "hqk,khd->qhd",
        weights.astype(jnp.bfloat16),
        value_band,
        preferred_element_type=jnp.float32,
    )
    heads_out = (
        (weighted / jnp.transpose(weight_sum)[:, :, None])
        .astype(jnp.bfloat16)
        .reshape(block_len, head_cols)
    )
    all_heads = lax.all_to_all(heads_out, "exp", split_axis=0, concat_axis=1, tiled=True)
    attn_out = jnp.dot(
        all_heads,
        lax.all_gather(w_out, "exp", axis=0, tiled=True),
        preferred_element_type=jnp.float32,
    )
    hidden_state = inputs + attn_out
    normed_ffn = rms_scale(hidden_state, gain_ffn).astype(jnp.bfloat16)
    experts_dev = w_gate.shape[0]
    n_total = experts_dev * n_exp
    capacity = 2 * row_count // n_total
    one_hot = (array_type[:, None] == jnp.arange(n_total, dtype=jnp.int32)[None, :]).astype(
        jnp.int32
    )
    slot_rank = jnp.sum(jnp.cumsum(one_hot, axis=0) * one_hot, axis=1) - 1
    owner = array_type // experts_dev
    local_expert = array_type % experts_dev
    slot_id = (owner * capacity + slot_rank) * experts_dev + local_expert
    n_slots = n_exp * capacity * experts_dev
    selector = (slot_id[None, :] == jnp.arange(n_slots, dtype=jnp.int32)[:, None]).astype(
        jnp.bfloat16
    )
    outgoing = jnp.dot(selector, normed_ffn, preferred_element_type=jnp.float32).astype(
        jnp.bfloat16
    )
    outgoing = outgoing.reshape(n_exp * capacity, experts_dev, width)
    n_seq = lax.axis_size("seq")
    y_size = Y_RING if n_seq % Y_RING == 0 else n_seq
    gathered = ring_gather(
        outgoing.reshape(-1, width), n_seq // y_size, y_size, pieces=2, route=True, n_other=n_exp
    ).reshape((n_seq * outgoing.shape[0],) + outgoing.shape[1:])
    n_seq = lax.axis_size("seq")
    y_size = Y_RING if n_seq % Y_RING == 0 else n_seq
    returned = ring_ffn(
        gathered.reshape(gathered.shape[0], width),
        w_gate[0], w_up[0], w_down[0], n_seq // y_size, y_size, n_exp,
    )[1].reshape((-1,) + gathered.shape[1:])
    expert_out = jnp.dot(
        jnp.transpose(selector),
        returned.reshape(n_slots, width),
        preferred_element_type=jnp.float32,
    )
    return (hidden_state + expert_out).astype(jnp.bfloat16)


def solution(mesh):
    return jax.shard_map(
        local,
        mesh=mesh,
        in_specs=(
            P(("seq", "exp"), None),
            P(("seq", "exp")),
            P(),
            P(),
            P(None, "exp"),
            P(None, "exp"),
            P(None, "exp"),
            P("exp"),
            P("exp", None),
            P(),
            P("exp", None, "seq"),
            P("exp", None, "seq"),
            P("exp", None, "seq"),
        ),
        out_specs=P(("seq", "exp"), None),
        check_vma=False,
    )
```
